128 devices in a mesh: ray: 16 (over x, z), tile: 8 (over y, core).
Axes of the slice: x: 4, y: 4, z: 4, core: 2. Of those that a mesh axis runs over, the one named last changes fastest.
Arguments:
- data: float32 [64, 262144], P(None, ('ray', 'tile')), may hold values from -6 to 6
- sensitivity: bfloat16 [4096, 256, 512], P(('ray', 'tile')), may hold values from -0.25 to 0.25
- block_tiles: int32 [128, 8, 4], P(('ray', 'tile')), may hold values from 0 to 47
- block_bundles: int32 [128, 8, 4], P(('ray', 'tile')), may hold values from 0 to 7
Outputs:
- solution: float32 [64, 196608], P(None, 'tile')
- residual: float32 [64, 262144], P(None, ('ray', 'tile'))
The draws below stay inside these ranges and needn't reach their ends.
Inputs may be any that keep to these rules, and one draw needn't show every extreme that they name: `block_tiles`: position of the block's tile among the 48 tiles of the owner given by the second index. `block_bundles`: the block's ray bundle among the device's 8 bundles.
All inputs are finite; a program needn't handle non-finite values.
Results may differ from the reference program's by a relative error of at most 0.004.
The reference program's roundings to bfloat16 on the way count: a program that leaves them out, or rounds other values in their place, can miss the bound.
Values may be sent and summed in bfloat16 or wider, within the bound.
A program may use at most 128 MiB of HBM per device.

```python
import math
import jax
import jax.numpy as jnp
import numpy as np
from jax import lax

RB = 256
CB = 512
COLS = 64
ITERS = 2
BUND_DEV = 8
TILE_DEV = 48
SLOTS = 4
RAYS = 262144
CELLS = 196608
BLOCKS = 4096
N_RAY = 16
N_TILE = 8


def place_ends(array, key, smallest, top_value):
    extent = array.shape
    place = [jax.random.randint(jax.random.fold_in(key, axis), (), 0, extent[axis]) for axis in range(len(extent))]
    array = array.at[tuple(place)].set(smallest)
    longest = extent.index(max(extent))
    place[longest] = (place[longest] + 1) % extent[longest]
    return array.at[tuple(place)].set(top_value)


def steps_of(own_key, shape, split, low, largest):
    def one(axis_at, shards_of):
        draws = jax.random.uniform(jax.random.fold_in(jax.random.fold_in(own_key, 6), axis_at), (shards_of,), jnp.float32, low / len(split), largest / len(split))
        return jnp.repeat(jnp.exp(draws), shape[axis_at] // shards_of).reshape((-1,) + (1,) * (len(shape) - axis_at - 1))

    factor_of = one(*split[0])
    for cut in split[1:]:
        factor_of = factor_of * one(*cut)
    return factor_of


def cumulative_ranks(count, slope):
    weights = [(1 << 20) // math.isqrt(standing ** slope) + 1 for standing in range(1, count + 1)]
    spread = 1 + sum(weights) // (1 << 30)
    return np.cumsum(np.array([max(1, weight // spread) for weight in weights]))


def ranked(rng, shape, number_of, lean):
    table = cumulative_ranks(number_of, lean)
    pick = jax.random.randint(jax.random.fold_in(rng, 1), shape, 0, int(table[number_of - 1]))
    grade = jnp.searchsorted(jnp.asarray(table, jnp.int32), pick, side="right")
    return jax.random.permutation(jax.random.fold_in(rng, 2), number_of)[grade].astype(jnp.int32)


def centred(own_key, dims, deviation, reach, cuts=(), held_as=jnp.bfloat16):
    values = jax.random.normal(own_key, dims, jnp.float32) * deviation
    if len(cuts) > 0:
        values = steps_of(own_key, dims, cuts, -0.22, 0.18) * values
    return jnp.clip(values, min=-reach, max=reach).astype(held_as)


def setup_inputs(seed: int = 0) -> dict:
    key_of = jax.random.split(jax.random.key(seed), 5)
    data = centred(key_of[0], (COLS, RAYS), 1.0, 6.0, ((1, 128),), jnp.float32)
    sensitivity = centred(key_of[1], (BLOCKS, RB, CB), CB ** -0.5, 0.25, ((0, 128),))
    block_tiles = place_ends(jax.random.randint(key_of[2], (N_RAY * N_TILE, N_TILE, SLOTS), 0, TILE_DEV), jax.random.fold_in(key_of[2], 1), 0, TILE_DEV - 1).astype(jnp.int32)
    block_bundles = place_ends(ranked(key_of[3], (N_RAY * N_TILE, N_TILE, SLOTS), BUND_DEV, 2), jax.random.fold_in(key_of[3], 3), 0, BUND_DEV - 1).astype(jnp.int32)
    return {"data": data, "sensitivity": sensitivity, "block_tiles": block_tiles, "block_bundles": block_bundles}


eps_norm = 1e-06

def column_norm(field):
    return jnp.sqrt(lax.optimization_barrier(jnp.sum(field * field, axis=1)) + eps_norm)

def owner_base():
    return jnp.arange(N_TILE, dtype=jnp.int32)[:, None] * TILE_DEV

def forward(field_bf, sensitivity, block_tiles, block_bundles):
    columns = field_bf.shape[0]
    tiles_all = field_bf.reshape(columns, N_TILE * TILE_DEV, CB)
    blocks_dev = sensitivity.reshape(N_RAY * N_TILE, N_TILE * SLOTS, RB, CB)
    base = owner_base()

    def one_device(packed):
        blocks, local_tiles, bundles = packed
        global_tiles = (local_tiles.astype(jnp.int32) + base).reshape(-1).astype(jnp.int32)
        tiles = jnp.take(tiles_all, global_tiles, axis=1).astype(jnp.float32)
        partial_value = jnp.einsum('cnk,nrk->ncr', tiles, blocks.astype(jnp.float32), precision=lax.Precision.HIGHEST)
        onehot = (bundles.reshape(-1)[:, None] == jnp.arange(BUND_DEV, dtype=jnp.int32)[None, :]).astype(jnp.float32)
        summed = jnp.einsum('ncr,nb->cbr', partial_value, onehot, precision=lax.Precision.HIGHEST)
        return summed.reshape(columns, BUND_DEV * RB)
    rays = lax.map(one_device, (blocks_dev, block_tiles, block_bundles))
    return jnp.transpose(rays, (1, 0, 2)).reshape(columns, RAYS)

def adjoint(rays_bf, sensitivity, block_tiles, block_bundles):
    columns = rays_bf.shape[0]
    rays_dev = jnp.transpose(rays_bf.reshape(columns, N_RAY * N_TILE, BUND_DEV, RB), (1, 0, 2, 3))
    blocks_dev = sensitivity.reshape(N_RAY * N_TILE, N_TILE * SLOTS, RB, CB)
    base = owner_base()

    def add_device(total, packed):
        blocks, local_tiles, bundles, rays = packed
        global_tiles = (local_tiles.astype(jnp.int32) + base).reshape(-1).astype(jnp.int32)
        picked = jnp.take(rays, bundles.reshape(-1).astype(jnp.int32), axis=1).astype(jnp.float32)
        terms = jnp.einsum('cnr,nrk->cnk', picked, blocks.astype(jnp.float32), precision=lax.Precision.HIGHEST)
        terms = lax.optimization_barrier(terms.astype(jnp.bfloat16)).astype(jnp.float32)
        return (total.at[:, global_tiles, :].add(terms), None)
    start = jnp.zeros((columns, N_TILE * TILE_DEV, CB), jnp.float32)
    total, unused = lax.scan(add_device, start, (blocks_dev, block_tiles, block_bundles, rays_dev))
    return total.reshape(columns, CELLS)

def reference(data, sensitivity, block_tiles, block_bundles):
    beta_now = column_norm(data)
    rays_dir = data / beta_now[:, None]
    model_dir = adjoint(rays_dir.astype(jnp.bfloat16), sensitivity, block_tiles, block_bundles)
    alpha_now = column_norm(model_dir)
    model_dir = model_dir / alpha_now[:, None]
    search = model_dir
    solution = jnp.zeros_like(model_dir)
    phi_bar = beta_now
    rho_bar = alpha_now
    for step in range(ITERS):
        rays_dir = forward(model_dir.astype(jnp.bfloat16), sensitivity, block_tiles, block_bundles) - alpha_now[:, None] * rays_dir
        beta_now = column_norm(rays_dir)
        rays_dir = rays_dir / beta_now[:, None]
        rho_now = jnp.sqrt(rho_bar * rho_bar + beta_now * beta_now)
        cosine = rho_bar / rho_now
        sine_part = beta_now / rho_now
        phi_now = cosine * phi_bar
        phi_bar = sine_part * phi_bar
        solution = solution + (phi_now / rho_now)[:, None] * search
        if step + 1 < ITERS:
            model_dir = adjoint(rays_dir.astype(jnp.bfloat16), sensitivity, block_tiles, block_bundles) - beta_now[:, None] * model_dir
            alpha_now = column_norm(model_dir)
            model_dir = model_dir / alpha_now[:, None]
            theta_now = sine_part * alpha_now
            rho_bar = -cosine * alpha_now
            search = model_dir - (theta_now / rho_now)[:, None] * search
    residual = data - forward(solution.astype(jnp.bfloat16), sensitivity, block_tiles, block_bundles)
    return (solution, residual)
```

```python
import jax
import jax.numpy as jnp
from jax import lax
from jax.sharding import PartitionSpec as P

RB = 256
CB = 512
ITERS = 2
BUND_DEV = 8
TILE_DEV = 48


import functools
from jax.experimental import pallas as pl
from jax.experimental.pallas import tpu as pltpu

MESH = pl.DeviceIdType.MESH


def stage_plan(mesh, axes):
    plan = []
    if "tile" in axes:
        tiles = mesh.shape["tile"]
        plan += [("tile", 2, 1), ("tile", tiles // 2, 2)]
    if "ray" in axes:
        rays = mesh.shape["ray"]
        inner = 4 if rays % 4 == 0 else 1
        plan += [("ray", inner, 1), ("ray", rays // inner, inner)]
    return tuple(stage for stage in plan if stage[1] > 1)


def reduce_kernel(plan, x_ref, o_ref, vals, send_sems, recv_sems):
    here = {"ray": lax.axis_index("ray"), "tile": lax.axis_index("tile")}

    def peer(axis, size, stride, k):
        idx = here[axis]
        pos = (idx // stride) % size
        other = idx + (((pos + k) % size) - pos) * stride
        coords = dict(here)
        coords[axis] = other
        return (coords["ray"], coords["tile"])

    barrier = pltpu.get_barrier_semaphore()
    count = 0
    for axis, size, stride in plan:
        for k in range(1, size):
            pl.semaphore_signal(barrier, inc=1, device_id=peer(axis, size, stride, k), device_id_type=MESH)
            count += 1
    pl.semaphore_wait(barrier, count)

    vals[0, 0] = x_ref[...]
    copies = []
    for s, (axis, size, stride) in enumerate(plan):
        src = x_ref if s == 0 else vals.at[s, 0]
        stage_copies = []
        for k in range(1, size):
            copy = pltpu.make_async_remote_copy(
                src_ref=src,
                dst_ref=vals.at[s, k],
                send_sem=send_sems.at[s, k],
                recv_sem=recv_sems.at[s, k],
                device_id=peer(axis, size, stride, (size - k) % size),
                device_id_type=MESH,
            )
            copy.start()
            stage_copies.append(copy)
        for copy in stage_copies:
            copy.wait_recv()
        copies += stage_copies
        pos = (here[axis] // stride) % size
        total = vals[s, (size - pos) % size]
        for q in range(1, size):
            total = total + vals[s, (q - pos + size) % size]
        if s + 1 < len(plan):
            vals[s + 1, 0] = total
        else:
            o_ref[...] = total
    for copy in copies:
        copy.wait_send()


def group_sum(mesh, axes, collective_id, partial):
    plan = stage_plan(mesh, axes)
    width = partial.shape[0]
    block = jnp.zeros((8, 128), jnp.float32).at[0, :width].set(partial)
    depth = max(size for _, size, _ in plan)
    out = pl.pallas_call(
        functools.partial(reduce_kernel, plan),
        out_shape=jax.ShapeDtypeStruct((8, 128), jnp.float32),
        in_specs=[pl.BlockSpec(memory_space=pltpu.VMEM)],
        out_specs=pl.BlockSpec(memory_space=pltpu.VMEM),
        scratch_shapes=[
            pltpu.VMEM((len(plan), depth, 8, 128), jnp.float32),
            pltpu.SemaphoreType.DMA((len(plan), depth)),
            pltpu.SemaphoreType.DMA((len(plan), depth)),
        ],
        compiler_params=pltpu.CompilerParams(collective_id=collective_id, has_side_effects=True),
    )(block)
    return out[0, :width]


eps_norm = 1e-06


def per_device(mesh, data, sensitivity, block_tiles, block_bundles):
    columns = data.shape[0]
    bundles = block_bundles.reshape(-1)
    requests = lax.all_to_all(block_tiles, "tile", split_axis=1, concat_axis=1, tiled=True).reshape(
        -1
    )
    bundle_onehot = (bundles[:, None] == jnp.arange(BUND_DEV, dtype=jnp.int32)[None, :]).astype(
        jnp.float32
    )
    owner_onehot = (requests[:, None] == jnp.arange(TILE_DEV, dtype=jnp.int32)[None, :]).astype(
        jnp.bfloat16
    )

    def fetch(field_bf):
        owned = field_bf.reshape(columns, TILE_DEV, CB)
        outgoing = jnp.take(owned, requests, axis=1)
        tiles = lax.all_to_all(outgoing, "tile", split_axis=1, concat_axis=1, tiled=True)
        return tiles

    def forward(field_bf):
        tiles = fetch(field_bf)
        partial_value = jnp.einsum(
            "cnk,nrk->ncr", tiles, sensitivity, preferred_element_type=jnp.float32
        )
        summed = jnp.einsum(
            "ncr,nb->cbr", partial_value, bundle_onehot, precision=lax.Precision.HIGHEST
        )
        return summed.reshape(columns, BUND_DEV * RB)

    def adjoint(rays_bf):
        picked = jnp.take(rays_bf.reshape(columns, BUND_DEV, RB), bundles, axis=1)
        terms = jnp.einsum(
            "cnr,nrk->cnk", picked, sensitivity, preferred_element_type=jnp.float32
        ).astype(jnp.bfloat16)
        arrived = lax.all_to_all(terms, "tile", split_axis=1, concat_axis=1, tiled=True)
        owned = jnp.einsum(
            "cnk,nt->ctk", arrived, owner_onehot, preferred_element_type=jnp.float32
        ).reshape(columns, TILE_DEV * CB)
        total = lax.psum(owned, "ray")
        return total

    def cell_norm(field):
        local = jnp.sum(field * field, axis=1)
        total = group_sum(mesh, ("tile",), 1, local)
        return jnp.sqrt(total + eps_norm)

    def ray_norm(rays):
        total = group_sum(mesh, ("ray", "tile"), 0, jnp.sum(rays * rays, axis=1))
        return jnp.sqrt(total + eps_norm)

    beta_now = ray_norm(data)
    rays_dir = data / beta_now[:, None]
    model_dir = adjoint(rays_dir.astype(jnp.bfloat16))
    alpha_now = cell_norm(model_dir)
    model_dir = model_dir / alpha_now[:, None]
    search = model_dir
    solution = jnp.zeros_like(model_dir)
    phi_bar = beta_now
    rho_bar = alpha_now
    for step in range(ITERS):
        rounded = model_dir.astype(jnp.bfloat16)
        rays_dir = forward(rounded) - alpha_now[:, None] * rays_dir
        beta_now = ray_norm(rays_dir)
        rays_dir = rays_dir / beta_now[:, None]
        rho_now = jnp.sqrt(rho_bar * rho_bar + beta_now * beta_now)
        cosine = rho_bar / rho_now
        sine_part = beta_now / rho_now
        phi_now = cosine * phi_bar
        phi_bar = sine_part * phi_bar
        solution = solution + (phi_now / rho_now)[:, None] * search
        if step + 1 < ITERS:
            model_dir = adjoint(rays_dir.astype(jnp.bfloat16)) - beta_now[:, None] * model_dir
            alpha_now = cell_norm(model_dir)
            model_dir = model_dir / alpha_now[:, None]
            theta_now = sine_part * alpha_now
            rho_bar = -cosine * alpha_now
            search = model_dir - (theta_now / rho_now)[:, None] * search
    residual = data - forward(solution.astype(jnp.bfloat16))
    return (solution, residual)


def solution(mesh):
    return jax.shard_map(
        functools.partial(per_device, mesh),
        mesh=mesh,
        in_specs=(
            P(None, ("ray", "tile")),
            P(("ray", "tile"), None, None),
            P(("ray", "tile"), None, None),
            P(("ray", "tile"), None, None),
        ),
        out_specs=(P(None, "tile"), P(None, ("ray", "tile"))),
        check_vma=False,
    )
```

```python
import jax
import jax.numpy as jnp
from jax import lax
from jax.sharding import PartitionSpec as P

RB = 256
CB = 512
ITERS = 2
BUND_DEV = 8
TILE_DEV = 48


import functools
from jax.experimental import pallas as pl
from jax.experimental.pallas import tpu as pltpu

MESH = pl.DeviceIdType.MESH


def stage_plan(mesh, axes):
    plan = []
    if "tile" in axes:
        tiles = mesh.shape["tile"]
        plan += [("tile", 2, 1), ("tile", tiles // 2, 2)]
    if "ray" in axes:
        rays = mesh.shape["ray"]
        inner = 4 if rays % 4 == 0 else 1
        plan += [("ray", inner, 1), ("ray", rays // inner, inner)]
    return tuple(stage for stage in plan if stage[1] > 1)


def reduce_kernel(plan, x_ref, o_ref, vals, send_sems, recv_sems):
    here = {"ray": lax.axis_index("ray"), "tile": lax.axis_index("tile")}

    def peer(axis, size, stride, k):
        idx = here[axis]
        pos = (idx // stride) % size
        other = idx + (((pos + k) % size) - pos) * stride
        coords = dict(here)
        coords[axis] = other
        return (coords["ray"], coords["tile"])

    barrier = pltpu.get_barrier_semaphore()
    count = 0
    for axis, size, stride in plan:
        for k in range(1, size):
            pl.semaphore_signal(barrier, inc=1, device_id=peer(axis, size, stride, k), device_id_type=MESH)
            count += 1
    pl.semaphore_wait(barrier, count)

    vals[0, 0] = x_ref[...]
    copies = []
    for s, (axis, size, stride) in enumerate(plan):
        src = x_ref if s == 0 else vals.at[s, 0]
        stage_copies = []
        for k in range(1, size):
            copy = pltpu.make_async_remote_copy(
                src_ref=src,
                dst_ref=vals.at[s, k],
                send_sem=send_sems.at[s, k],
                recv_sem=recv_sems.at[s, k],
                device_id=peer(axis, size, stride, (size - k) % size),
                device_id_type=MESH,
            )
            copy.start()
            stage_copies.append(copy)
        for copy in stage_copies:
            copy.wait_recv()
        copies += stage_copies
        pos = (here[axis] // stride) % size
        total = vals[s, (size - pos) % size]
        for q in range(1, size):
            total = total + vals[s, (q - pos + size) % size]
        if s + 1 < len(plan):
            vals[s + 1, 0] = total
        else:
            o_ref[...] = total
    for copy in copies:
        copy.wait_send()


def group_sum(mesh, axes, collective_id, partial):
    plan = stage_plan(mesh, axes)
    width = partial.shape[0]
    block = jnp.zeros((8, 128), jnp.float32).at[0, :width].set(partial)
    depth = max(size for _, size, _ in plan)
    out = pl.pallas_call(
        functools.partial(reduce_kernel, plan),
        out_shape=jax.ShapeDtypeStruct((8, 128), jnp.float32),
        in_specs=[pl.BlockSpec(memory_space=pltpu.VMEM)],
        out_specs=pl.BlockSpec(memory_space=pltpu.VMEM),
        scratch_shapes=[
            pltpu.VMEM((len(plan), depth, 8, 128), jnp.float32),
            pltpu.SemaphoreType.DMA((len(plan), depth)),
            pltpu.SemaphoreType.DMA((len(plan), depth)),
        ],
        compiler_params=pltpu.CompilerParams(collective_id=collective_id, has_side_effects=True),
    )(block)
    return out[0, :width]


eps_norm = 1e-06


def per_device(mesh, data, sensitivity, block_tiles, block_bundles):
    columns = data.shape[0]
    bundles = block_bundles.reshape(-1)
    requests = lax.all_to_all(block_tiles, "tile", split_axis=1, concat_axis=1, tiled=True).reshape(
        -1
    )
    bundle_onehot = (bundles[:, None] == jnp.arange(BUND_DEV, dtype=jnp.int32)[None, :]).astype(
        jnp.float32
    )
    owner_onehot = (requests[:, None] == jnp.arange(TILE_DEV, dtype=jnp.int32)[None, :]).astype(
        jnp.bfloat16
    )

    def fetch(field_bf):
        owned = field_bf.reshape(columns, TILE_DEV, CB)
        outgoing = jnp.take(owned, requests, axis=1)
        tiles = lax.all_to_all(outgoing, "tile", split_axis=1, concat_axis=1, tiled=True)
        return tiles

    def forward(field_bf):
        tiles = fetch(field_bf)
        partial_value = jnp.einsum(
            "cnk,nrk->ncr", tiles, sensitivity, preferred_element_type=jnp.float32
        )
        summed = jnp.einsum(
            "ncr,nb->cbr", partial_value, bundle_onehot, precision=lax.Precision.HIGHEST
        )
        return summed.reshape(columns, BUND_DEV * RB)

    def adjoint(rays_bf):
        picked = jnp.take(rays_bf.reshape(columns, BUND_DEV, RB), bundles, axis=1)
        terms = jnp.einsum(
            "cnr,nrk->cnk", picked, sensitivity, preferred_element_type=jnp.float32
        ).astype(jnp.bfloat16)
        arrived = lax.all_to_all(terms, "tile", split_axis=1, concat_axis=1, tiled=True)
        owned = jnp.einsum(
            "cnk,nt->ctk", arrived, owner_onehot, preferred_element_type=jnp.float32
        ).reshape(columns, TILE_DEV * CB)
        return lax.psum_scatter(owned, "ray", scatter_dimension=1, tiled=True)

    def gather_bf(field):
        return lax.all_gather(field.astype(jnp.bfloat16), "ray", axis=1, tiled=True)

    def cell_norm(field):
        local = jnp.sum(field * field, axis=1)
        total = group_sum(mesh, ("ray", "tile"), 0, local)
        return jnp.sqrt(total + eps_norm)

    def ray_norm(rays):
        total = group_sum(mesh, ("ray", "tile"), 0, jnp.sum(rays * rays, axis=1))
        return jnp.sqrt(total + eps_norm)

    beta_now = ray_norm(data)
    rays_dir = data / beta_now[:, None]
    model_dir = adjoint(rays_dir.astype(jnp.bfloat16))
    alpha_now = cell_norm(model_dir)
    model_dir = model_dir / alpha_now[:, None]
    search = model_dir
    solution = jnp.zeros_like(model_dir)
    phi_bar = beta_now
    rho_bar = alpha_now
    for step in range(ITERS):
        rays_dir = forward(gather_bf(model_dir)) - alpha_now[:, None] * rays_dir
        beta_now = ray_norm(rays_dir)
        rays_dir = rays_dir / beta_now[:, None]
        rho_now = jnp.sqrt(rho_bar * rho_bar + beta_now * beta_now)
        cosine = rho_bar / rho_now
        sine_part = beta_now / rho_now
        phi_now = cosine * phi_bar
        phi_bar = sine_part * phi_bar
        solution = solution + (phi_now / rho_now)[:, None] * search
        if step + 1 < ITERS:
            model_dir = adjoint(rays_dir.astype(jnp.bfloat16)) - beta_now[:, None] * model_dir
            alpha_now = cell_norm(model_dir)
            model_dir = model_dir / alpha_now[:, None]
            theta_now = sine_part * alpha_now
            rho_bar = -cosine * alpha_now
            search = model_dir - (theta_now / rho_now)[:, None] * search
    solution = lax.all_gather(solution, "ray", axis=1, tiled=True)
    residual = data - forward(solution.astype(jnp.bfloat16))
    return (solution, residual)


def solution(mesh):
    return jax.shard_map(
        functools.partial(per_device, mesh),
        mesh=mesh,
        in_specs=(
            P(None, ("ray", "tile")),
            P(("ray", "tile"), None, None),
            P(("ray", "tile"), None, None),
            P(("ray", "tile"), None, None),
        ),
        out_specs=(P(None, "tile"), P(None, ("ray", "tile"))),
        check_vma=False,
    )
```

```python
import jax
import jax.numpy as jnp
from jax import lax
from jax.sharding import PartitionSpec as P

RB = 256
CB = 512
ITERS = 2
BUND_DEV = 8
TILE_DEV = 48


import functools
from jax.experimental import pallas as pl
from jax.experimental.pallas import tpu as pltpu

MESH = pl.DeviceIdType.MESH


def stage_plan(mesh, axes):
    plan = [(axis, mesh.shape[axis], 1) for axis in ("tile", "ray") if axis in axes]
    return tuple(stage for stage in plan if stage[1] > 1)


def reduce_kernel(plan, x_ref, o_ref, vals, send_sems, recv_sems):
    here = {"ray": lax.axis_index("ray"), "tile": lax.axis_index("tile")}

    def peer(axis, size, stride, k):
        idx = here[axis]
        pos = (idx // stride) % size
        other = idx + (((pos + k) % size) - pos) * stride
        coords = dict(here)
        coords[axis] = other
        return (coords["ray"], coords["tile"])

    barrier = pltpu.get_barrier_semaphore()
    count = 0
    for axis, size, stride in plan:
        for k in range(1, size):
            pl.semaphore_signal(barrier, inc=1, device_id=peer(axis, size, stride, k), device_id_type=MESH)
            count += 1
    pl.semaphore_wait(barrier, count)

    vals[0, 0] = x_ref[...]
    copies = []
    for s, (axis, size, stride) in enumerate(plan):
        src = x_ref if s == 0 else vals.at[s, 0]
        stage_copies = []
        for k in range(1, size):
            copy = pltpu.make_async_remote_copy(
                src_ref=src,
                dst_ref=vals.at[s, k],
                send_sem=send_sems.at[s, k],
                recv_sem=recv_sems.at[s, k],
                device_id=peer(axis, size, stride, (size - k) % size),
                device_id_type=MESH,
            )
            copy.start()
            stage_copies.append(copy)
        for copy in stage_copies:
            copy.wait_recv()
        copies += stage_copies
        pos = (here[axis] // stride) % size
        total = vals[s, (size - pos) % size]
        for q in range(1, size):
            total = total + vals[s, (q - pos + size) % size]
        if s + 1 < len(plan):
            vals[s + 1, 0] = total
        else:
            o_ref[...] = total
    for copy in copies:
        copy.wait_send()


def group_sum(mesh, axes, collective_id, partial):
    plan = stage_plan(mesh, axes)
    width = partial.shape[0]
    block = jnp.zeros((8, 128), jnp.float32).at[0, :width].set(partial)
    depth = max(size for _, size, _ in plan)
    out = pl.pallas_call(
        functools.partial(reduce_kernel, plan),
        out_shape=jax.ShapeDtypeStruct((8, 128), jnp.float32),
        in_specs=[pl.BlockSpec(memory_space=pltpu.VMEM)],
        out_specs=pl.BlockSpec(memory_space=pltpu.VMEM),
        scratch_shapes=[
            pltpu.VMEM((len(plan), depth, 8, 128), jnp.float32),
            pltpu.SemaphoreType.DMA((len(plan), depth)),
            pltpu.SemaphoreType.DMA((len(plan), depth)),
        ],
        compiler_params=pltpu.CompilerParams(collective_id=collective_id, has_side_effects=True),
    )(block)
    return out[0, :width]


eps_norm = 1e-06


def per_device(mesh, data, sensitivity, block_tiles, block_bundles):
    columns = data.shape[0]
    bundles = block_bundles.reshape(-1)
    requests = lax.all_to_all(block_tiles, "tile", split_axis=1, concat_axis=1, tiled=True).reshape(
        -1
    )
    bundle_onehot = (bundles[:, None] == jnp.arange(BUND_DEV, dtype=jnp.int32)[None, :]).astype(
        jnp.float32
    )
    owner_onehot = (requests[:, None] == jnp.arange(TILE_DEV, dtype=jnp.int32)[None, :]).astype(
        jnp.bfloat16
    )

    def fetch(field_bf):
        owned = field_bf.reshape(columns, TILE_DEV, CB)
        outgoing = jnp.take(owned, requests, axis=1)
        tiles = lax.all_to_all(outgoing, "tile", split_axis=1, concat_axis=1, tiled=True)
        return tiles

    def forward(field_bf):
        tiles = fetch(field_bf)
        partial_value = jnp.einsum(
            "cnk,nrk->ncr", tiles, sensitivity, preferred_element_type=jnp.float32
        )
        summed = jnp.einsum(
            "ncr,nb->cbr", partial_value, bundle_onehot, precision=lax.Precision.HIGHEST
        )
        return summed.reshape(columns, BUND_DEV * RB)

    def adjoint(rays_bf):
        picked = jnp.take(rays_bf.reshape(columns, BUND_DEV, RB), bundles, axis=1)
        terms = jnp.einsum(
            "cnr,nrk->cnk", picked, sensitivity, preferred_element_type=jnp.float32
        ).astype(jnp.bfloat16)
        arrived = lax.all_to_all(terms, "tile", split_axis=1, concat_axis=1, tiled=True)
        owned = jnp.einsum(
            "cnk,nt->ctk", arrived, owner_onehot, preferred_element_type=jnp.float32
        ).reshape(columns, TILE_DEV * CB)
        total = lax.psum(owned, "ray")
        return total

    def cell_norm(field):
        local = jnp.sum(field * field, axis=1)
        total = group_sum(mesh, ("tile",), 1, local)
        return jnp.sqrt(total + eps_norm)

    def ray_norm(rays):
        total = group_sum(mesh, ("ray", "tile"), 0, jnp.sum(rays * rays, axis=1))
        return jnp.sqrt(total + eps_norm)

    beta_now = ray_norm(data)
    rays_dir = data / beta_now[:, None]
    model_dir = adjoint(rays_dir.astype(jnp.bfloat16))
    alpha_now = cell_norm(model_dir)
    model_dir = model_dir / alpha_now[:, None]
    search = model_dir
    solution = jnp.zeros_like(model_dir)
    phi_bar = beta_now
    rho_bar = alpha_now
    for step in range(ITERS):
        rounded = model_dir.astype(jnp.bfloat16)
        rays_dir = forward(rounded) - alpha_now[:, None] * rays_dir
        beta_now = ray_norm(rays_dir)
        rays_dir = rays_dir / beta_now[:, None]
        rho_now = jnp.sqrt(rho_bar * rho_bar + beta_now * beta_now)
        cosine = rho_bar / rho_now
        sine_part = beta_now / rho_now
        phi_now = cosine * phi_bar
        phi_bar = sine_part * phi_bar
        solution = solution + (phi_now / rho_now)[:, None] * search
        if step + 1 < ITERS:
            model_dir = adjoint(rays_dir.astype(jnp.bfloat16)) - beta_now[:, None] * model_dir
            alpha_now = cell_norm(model_dir)
            model_dir = model_dir / alpha_now[:, None]
            theta_now = sine_part * alpha_now
            rho_bar = -cosine * alpha_now
            search = model_dir - (theta_now / rho_now)[:, None] * search
    residual = data - forward(solution.astype(jnp.bfloat16))
    return (solution, residual)


def solution(mesh):
    return jax.shard_map(
        functools.partial(per_device, mesh),
        mesh=mesh,
        in_specs=(
            P(None, ("ray", "tile")),
            P(("ray", "tile"), None, None),
            P(("ray", "tile"), None, None),
            P(("ray", "tile"), None, None),
        ),
        out_specs=(P(None, "tile"), P(None, ("ray", "tile"))),
        check_vma=False,
    )
```

```python
import jax
import jax.numpy as jnp
from jax import lax
from jax.sharding import PartitionSpec as P

RB = 256
CB = 512
ITERS = 2
BUND_DEV = 8
TILE_DEV = 48


import functools
from jax.experimental import pallas as pl
from jax.experimental.pallas import tpu as pltpu

MESH = pl.DeviceIdType.MESH


def stage_plan(mesh, axes):
    plan = [(axis, mesh.shape[axis], 1) for axis in ("tile", "ray") if axis in axes]
    return tuple(stage for stage in plan if stage[1] > 1)


def reduce_kernel(plan, x_ref, o_ref, vals, send_sems, recv_sems):
    here = {"ray": lax.axis_index("ray"), "tile": lax.axis_index("tile")}

    def peer(axis, size, stride, k):
        idx = here[axis]
        pos = (idx // stride) % size
        other = idx + (((pos + k) % size) - pos) * stride
        coords = dict(here)
        coords[axis] = other
        return (coords["ray"], coords["tile"])

    barrier = pltpu.get_barrier_semaphore()
    count = 0
    for axis, size, stride in plan:
        for k in range(1, size):
            pl.semaphore_signal(barrier, inc=1, device_id=peer(axis, size, stride, k), device_id_type=MESH)
            count += 1
    pl.semaphore_wait(barrier, count)

    vals[0, 0] = x_ref[...]
    copies = []
    for s, (axis, size, stride) in enumerate(plan):
        src = x_ref if s == 0 else vals.at[s, 0]
        stage_copies = []
        for k in range(1, size):
            copy = pltpu.make_async_remote_copy(
                src_ref=src,
                dst_ref=vals.at[s, k],
                send_sem=send_sems.at[s, k],
                recv_sem=recv_sems.at[s, k],
                device_id=peer(axis, size, stride, (size - k) % size),
                device_id_type=MESH,
            )
            copy.start()
            stage_copies.append(copy)
        for copy in stage_copies:
            copy.wait_recv()
        copies += stage_copies
        pos = (here[axis] // stride) % size
        total = vals[s, (size - pos) % size]
        for q in range(1, size):
            total = total + vals[s, (q - pos + size) % size]
        if s + 1 < len(plan):
            vals[s + 1, 0] = total
        else:
            o_ref[...] = total
    for copy in copies:
        copy.wait_send()


def group_sum(mesh, axes, collective_id, partial):
    plan = stage_plan(mesh, axes)
    width = partial.shape[0]
    block = jnp.zeros((8, 128), jnp.float32).at[0, :width].set(partial)
    depth = max(size for _, size, _ in plan)
    out = pl.pallas_call(
        functools.partial(reduce_kernel, plan),
        out_shape=jax.ShapeDtypeStruct((8, 128), jnp.float32),
        in_specs=[pl.BlockSpec(memory_space=pltpu.VMEM)],
        out_specs=pl.BlockSpec(memory_space=pltpu.VMEM),
        scratch_shapes=[
            pltpu.VMEM((len(plan), depth, 8, 128), jnp.float32),
            pltpu.SemaphoreType.DMA((len(plan), depth)),
            pltpu.SemaphoreType.DMA((len(plan), depth)),
        ],
        compiler_params=pltpu.CompilerParams(collective_id=collective_id, has_side_effects=True),
    )(block)
    return out[0, :width]


def ray_axes(mesh):
    rays = mesh.shape["ray"]
    inner = 4 if rays % 4 == 0 else rays
    return ((inner, 1), (rays // inner, inner))


def allreduce_kernel(axes, x_ref, o_ref, recv1, recv2, part, send_sems, recv_sems):
    me = lax.axis_index("ray")
    tile = lax.axis_index("tile")
    rows = x_ref.shape[0]
    half = x_ref.shape[1] // 2
    w1 = half // axes[0][0]
    w2 = w1 // axes[1][0]

    def pos(axis):
        size, stride = axis
        return (me // stride) % size

    def peer(axis, k):
        size, stride = axis
        p = pos(axis)
        return (me + (((p - k + size) % size) - p) * stride, tile)

    def cols(start, width):
        return pl.ds(pl.multiple_of(start, 128), width)

    def add_rows(dst, srcs):
        def body(r, carry):
            block = pl.ds(pl.multiple_of(r * 8, 8), 8)
            total = srcs[0][block, :]
            for ref in srcs[1:]:
                total = total + ref[block, :]
            dst[block, :] = total
            return carry
        lax.fori_loop(0, rows // 8, body, 0)

    barrier = pltpu.get_barrier_semaphore()
    greeted = 0
    for axis in axes:
        for k in range(1, axis[0]):
            pl.semaphore_signal(barrier, inc=1, device_id=peer(axis, k), device_id_type=MESH)
            greeted += 1
    pl.semaphore_wait(barrier, greeted)

    plans = [(axes[0], axes[1]), (axes[1], axes[0])]
    sends = []

    def exchange(stage, h, axis, src_of, dst_of, landing_of):
        out = []
        for k in range(1, axis[0]):
            copy = pltpu.make_async_remote_copy(
                src_ref=src_of(k), dst_ref=dst_of(k),
                send_sem=send_sems.at[stage, h, k], recv_sem=recv_sems.at[stage, h, k],
                device_id=peer(axis, k), device_id_type=MESH)
            copy.start()
            sends.append(copy)
            out.append(pltpu.make_async_remote_copy(
                src_ref=src_of(k), dst_ref=landing_of(k),
                send_sem=send_sems.at[stage, h, k], recv_sem=recv_sems.at[stage, h, k],
                device_id=peer(axis, k), device_id_type=MESH))
        return out

    waits = []
    for h, (a1, a2) in enumerate(plans):
        n1, p1 = a1[0], pos(a1)
        recv1[h, 0] = x_ref[:, cols(h * half + p1 * w1, w1)]
        waits += exchange(
            0, h, a1,
            lambda k, h=h, n1=n1, p1=p1: x_ref.at[:, cols(h * half + ((p1 - k + n1) % n1) * w1, w1)],
            lambda k, h=h: recv1.at[h, k],
            lambda k, h=h: recv1.at[h, k])
    for copy in waits:
        copy.wait_recv()
    waits = []
    for h, (a1, a2) in enumerate(plans):
        n1, p1 = a1[0], pos(a1)
        n2, p2 = a2[0], pos(a2)
        add_rows(part.at[h], [recv1.at[h, (q - p1 + n1) % n1] for q in range(n1)])
        recv2[h, 0] = part[h, :, cols(p2 * w2, w2)]
        waits += exchange(
            1, h, a2,
            lambda k, h=h, n2=n2, p2=p2: part.at[h, :, cols(((p2 - k + n2) % n2) * w2, w2)],
            lambda k, h=h: recv2.at[h, k],
            lambda k, h=h: recv2.at[h, k])
    for copy in waits:
        copy.wait_recv()
    waits = []
    for h, (a1, a2) in enumerate(plans):
        n1, p1 = a1[0], pos(a1)
        n2, p2 = a2[0], pos(a2)
        base = h * half + p1 * w1
        add_rows(o_ref.at[:, cols(base + p2 * w2, w2)], [recv2.at[h, (q - p2 + n2) % n2] for q in range(n2)])
        waits += exchange(
            2, h, a2,
            lambda k, base=base, p2=p2: o_ref.at[:, cols(base + p2 * w2, w2)],
            lambda k, base=base, p2=p2: o_ref.at[:, cols(base + p2 * w2, w2)],
            lambda k, base=base, n2=n2, p2=p2: o_ref.at[:, cols(base + ((p2 + k) % n2) * w2, w2)])
    for copy in waits:
        copy.wait_recv()
    waits = []
    for h, (a1, a2) in enumerate(plans):
        n1, p1 = a1[0], pos(a1)
        waits += exchange(
            3, h, a1,
            lambda k, h=h, p1=p1: o_ref.at[:, cols(h * half + p1 * w1, w1)],
            lambda k, h=h, p1=p1: o_ref.at[:, cols(h * half + p1 * w1, w1)],
            lambda k, h=h, n1=n1, p1=p1: o_ref.at[:, cols(h * half + ((p1 + k) % n1) * w1, w1)])
    for copy in waits:
        copy.wait_recv()
    for copy in sends:
        copy.wait_send()


def ray_allreduce(mesh, owned):
    axes = ray_axes(mesh)
    rows, width = owned.shape
    half = width // 2
    w1 = half // axes[0][0]
    w2 = w1 // axes[1][0]
    depth = max(axes[0][0], axes[1][0])
    return pl.pallas_call(
        functools.partial(allreduce_kernel, axes),
        out_shape=jax.ShapeDtypeStruct((rows, width), jnp.float32),
        in_specs=[pl.BlockSpec(memory_space=pltpu.VMEM)],
        out_specs=pl.BlockSpec(memory_space=pltpu.VMEM),
        scratch_shapes=[
            pltpu.VMEM((2, depth, rows, w1), jnp.float32),
            pltpu.VMEM((2, depth, rows, w2), jnp.float32),
            pltpu.VMEM((2, rows, w1), jnp.float32),
            pltpu.SemaphoreType.DMA((4, 2, depth)),
            pltpu.SemaphoreType.DMA((4, 2, depth)),
        ],
        compiler_params=pltpu.CompilerParams(
            collective_id=2, has_side_effects=True, vmem_limit_bytes=60 * 1024 * 1024),
    )(owned)


eps_norm = 1e-06


def per_device(mesh, data, sensitivity, block_tiles, block_bundles):
    columns = data.shape[0]
    bundles = block_bundles.reshape(-1)
    requests = lax.all_to_all(block_tiles, "tile", split_axis=1, concat_axis=1, tiled=True).reshape(
        -1
    )
    bundle_onehot = (bundles[:, None] == jnp.arange(BUND_DEV, dtype=jnp.int32)[None, :]).astype(
        jnp.float32
    )
    owner_onehot = (requests[:, None] == jnp.arange(TILE_DEV, dtype=jnp.int32)[None, :]).astype(
        jnp.bfloat16
    )

    def fetch(field_bf):
        owned = field_bf.reshape(columns, TILE_DEV, CB)
        outgoing = jnp.take(owned, requests, axis=1)
        tiles = lax.all_to_all(outgoing, "tile", split_axis=1, concat_axis=1, tiled=True)
        return tiles

    def forward(field_bf):
        tiles = fetch(field_bf)
        partial_value = jnp.einsum(
            "cnk,nrk->ncr", tiles, sensitivity, preferred_element_type=jnp.float32
        )
        summed = jnp.einsum(
            "ncr,nb->cbr", partial_value, bundle_onehot, precision=lax.Precision.HIGHEST
        )
        return summed.reshape(columns, BUND_DEV * RB)

    def adjoint(rays_bf):
        picked = jnp.take(rays_bf.reshape(columns, BUND_DEV, RB), bundles, axis=1)
        terms = jnp.einsum(
            "cnr,nrk->cnk", picked, sensitivity, preferred_element_type=jnp.float32
        ).astype(jnp.bfloat16)
        arrived = lax.all_to_all(terms, "tile", split_axis=1, concat_axis=1, tiled=True)
        owned = jnp.einsum(
            "cnk,nt->ctk", arrived, owner_onehot, preferred_element_type=jnp.float32
        ).reshape(columns, TILE_DEV * CB)
        total = ray_allreduce(mesh, owned)
        return total

    def cell_norm(field):
        local = jnp.sum(field * field, axis=1)
        total = group_sum(mesh, ("tile",), 1, local)
        return jnp.sqrt(total + eps_norm)

    def ray_norm(rays):
        total = group_sum(mesh, ("ray", "tile"), 0, jnp.sum(rays * rays, axis=1))
        return jnp.sqrt(total + eps_norm)

    beta_now = ray_norm(data)
    rays_dir = data / beta_now[:, None]
    model_dir = adjoint(rays_dir.astype(jnp.bfloat16))
    alpha_now = cell_norm(model_dir)
    model_dir = model_dir / alpha_now[:, None]
    search = model_dir
    solution = jnp.zeros_like(model_dir)
    phi_bar = beta_now
    rho_bar = alpha_now
    for step in range(ITERS):
        rounded = model_dir.astype(jnp.bfloat16)
        rays_dir = forward(rounded) - alpha_now[:, None] * rays_dir
        beta_now = ray_norm(rays_dir)
        rays_dir = rays_dir / beta_now[:, None]
        rho_now = jnp.sqrt(rho_bar * rho_bar + beta_now * beta_now)
        cosine = rho_bar / rho_now
        sine_part = beta_now / rho_now
        phi_now = cosine * phi_bar
        phi_bar = sine_part * phi_bar
        solution = solution + (phi_now / rho_now)[:, None] * search
        if step + 1 < ITERS:
            model_dir = adjoint(rays_dir.astype(jnp.bfloat16)) - beta_now[:, None] * model_dir
            alpha_now = cell_norm(model_dir)
            model_dir = model_dir / alpha_now[:, None]
            theta_now = sine_part * alpha_now
            rho_bar = -cosine * alpha_now
            search = model_dir - (theta_now / rho_now)[:, None] * search
    residual = data - forward(solution.astype(jnp.bfloat16))
    return (solution, residual)


def solution(mesh):
    return jax.shard_map(
        functools.partial(per_device, mesh),
        mesh=mesh,
        in_specs=(
            P(None, ("ray", "tile")),
            P(("ray", "tile"), None, None),
            P(("ray", "tile"), None, None),
            P(("ray", "tile"), None, None),
        ),
        out_specs=(P(None, "tile"), P(None, ("ray", "tile"))),
        check_vma=False,
    )
```

```python
import jax
import jax.numpy as jnp
from jax import lax
from jax.sharding import PartitionSpec as P

RB = 256
CB = 512
ITERS = 2
BUND_DEV = 8
TILE_DEV = 48


import functools
from jax.experimental import pallas as pl
from jax.experimental.pallas import tpu as pltpu

MESH = pl.DeviceIdType.MESH


def stage_plan(mesh, axes):
    plan = [(axis, mesh.shape[axis], 1) for axis in ("tile", "ray") if axis in axes]
    return tuple(stage for stage in plan if stage[1] > 1)


def reduce_kernel(plan, x_ref, o_ref, vals, send_sems, recv_sems):
    here = {"ray": lax.axis_index("ray"), "tile": lax.axis_index("tile")}

    def peer(axis, size, stride, k):
        idx = here[axis]
        pos = (idx // stride) % size
        other = idx + (((pos + k) % size) - pos) * stride
        coords = dict(here)
        coords[axis] = other
        return (coords["ray"], coords["tile"])

    barrier = pltpu.get_barrier_semaphore()
    count = 0
    for axis, size, stride in plan:
        for k in range(1, size):
            pl.semaphore_signal(barrier, inc=1, device_id=peer(axis, size, stride, k), device_id_type=MESH)
            count += 1
    pl.semaphore_wait(barrier, count)

    vals[0, 0] = x_ref[...]
    copies = []
    for s, (axis, size, stride) in enumerate(plan):
        src = x_ref if s == 0 else vals.at[s, 0]
        stage_copies = []
        for k in range(1, size):
            copy = pltpu.make_async_remote_copy(
                src_ref=src,
                dst_ref=vals.at[s, k],
                send_sem=send_sems.at[s, k],
                recv_sem=recv_sems.at[s, k],
                device_id=peer(axis, size, stride, (size - k) % size),
                device_id_type=MESH,
            )
            copy.start()
            stage_copies.append(copy)
        for copy in stage_copies:
            copy.wait_recv()
        copies += stage_copies
        pos = (here[axis] // stride) % size
        total = vals[s, (size - pos) % size]
        for q in range(1, size):
            total = total + vals[s, (q - pos + size) % size]
        if s + 1 < len(plan):
            vals[s + 1, 0] = total
        else:
            o_ref[...] = total
    for copy in copies:
        copy.wait_send()


def group_sum(mesh, axes, collective_id, partial):
    plan = stage_plan(mesh, axes)
    width = partial.shape[0]
    block = jnp.zeros((8, 128), jnp.float32).at[0, :width].set(partial)
    depth = max(size for _, size, _ in plan)
    out = pl.pallas_call(
        functools.partial(reduce_kernel, plan),
        out_shape=jax.ShapeDtypeStruct((8, 128), jnp.float32),
        in_specs=[pl.BlockSpec(memory_space=pltpu.VMEM)],
        out_specs=pl.BlockSpec(memory_space=pltpu.VMEM),
        scratch_shapes=[
            pltpu.VMEM((len(plan), depth, 8, 128), jnp.float32),
            pltpu.SemaphoreType.DMA((len(plan), depth)),
            pltpu.SemaphoreType.DMA((len(plan), depth)),
        ],
        compiler_params=pltpu.CompilerParams(collective_id=collective_id, has_side_effects=True),
    )(block)
    return out[0, :width]


def ray_axes(mesh):
    rays = mesh.shape["ray"]
    inner = 4 if rays % 4 == 0 else rays
    return ((inner, 1), (rays // inner, inner))


def allreduce_kernel(axes, x_ref, o_ref, part, rbuf1, acc1, rbuf2, acc2, send_sems, recv_sems):
    me = lax.axis_index("ray")
    tile = lax.axis_index("tile")
    rows = x_ref.shape[0]
    half = x_ref.shape[1] // 2
    w1 = half // axes[0][0]
    w2 = w1 // axes[1][0]

    def pos(axis):
        size, stride = axis
        return (me // stride) % size

    def peer(axis, k):
        size, stride = axis
        p = pos(axis)
        return (me + (((p - k + size) % size) - p) * stride, tile)

    def cols(start, width):
        return pl.ds(pl.multiple_of(start, 128), width)

    def add_rows(dst, a, b):
        def body(r, carry):
            block = pl.ds(pl.multiple_of(r * 8, 8), 8)
            dst[block, :] = a[block, :] + b[block, :]
            return carry
        lax.fori_loop(0, rows // 8, body, 0)

    barrier = pltpu.get_barrier_semaphore()
    greeted = 0
    for axis in axes:
        for k in (1, axis[0] - 1) if axis[0] > 2 else (1,):
            pl.semaphore_signal(barrier, inc=1, device_id=peer(axis, k), device_id_type=MESH)
            greeted += 1
    pl.semaphore_wait(barrier, greeted)

    plans = [(axes[0], axes[1]), (axes[1], axes[0])]
    sends = []

    def send(stage, h, d, s, axis, src, dst, landing):
        size = axis[0]
        k = size - 1 if d == 0 else 1
        sems = dict(send_sem=send_sems.at[stage, h, d, s], recv_sem=recv_sems.at[stage, h, d, s],
                    device_id=peer(axis, k), device_id_type=MESH)
        copy = pltpu.make_async_remote_copy(src_ref=src, dst_ref=dst, **sems)
        copy.start()
        sends.append(copy)
        return pltpu.make_async_remote_copy(src_ref=src, dst_ref=landing, **sems)

    def reduce_scatter(stage, segs, rbuf, acc):
        steps = segs[0][0][0] - 1
        for s in range(steps):
            waits = []
            for h, (axis, own, final) in enumerate(segs):
                size, p = axis[0], pos(axis)
                for d in range(2):
                    sign = 1 if d == 0 else -1
                    src = own((p - sign * (s + 1) + 2 * size) % size, d) if s == 0 else acc.at[h, d, s - 1]
                    waits.append((h, d, send(stage, h, d, s, axis, src, rbuf.at[h, d, s], rbuf.at[h, d, s])))
            for h, d, copy in waits:
                copy.wait_recv()
            for h, (axis, own, final) in enumerate(segs):
                size, p = axis[0], pos(axis)
                for d in range(2):
                    sign = 1 if d == 0 else -1
                    mine = own((p - sign * (s + 2) + 2 * size) % size, d)
                    dst = final(d) if s == steps - 1 else acc.at[h, d, s]
                    add_rows(dst, rbuf.at[h, d, s], mine)

    def all_gather(stage, segs):
        steps = segs[0][0][0] - 1
        for s in range(steps):
            waits = []
            for h, (axis, region) in enumerate(segs):
                size, p = axis[0], pos(axis)
                for d in range(2):
                    sign = 1 if d == 0 else -1
                    src = region((p - sign * s + 2 * size) % size, d)
                    landing = region((p - sign * (s + 1) + 2 * size) % size, d)
                    waits.append(send(stage, h, d, s, axis, src, src, landing))
            for copy in waits:
                copy.wait_recv()

    q1, q2 = w1 // 2, w2 // 2
    seg1, seg2, seg3, seg4 = [], [], [], []
    for h, (a1, a2) in enumerate(plans):
        p1, p2 = pos(a1), pos(a2)
        base = h * half + p1 * w1
        seg1.append((a1,
                     lambda j, d, h=h: x_ref.at[:, cols(h * half + j * w1 + d * q1, q1)],
                     lambda d, h=h: part.at[h, :, cols(d * q1, q1)]))
        seg2.append((a2,
                     lambda j, d, h=h: part.at[h, :, cols(j * w2 + d * q2, q2)],
                     lambda d, base=base, p2=p2: o_ref.at[:, cols(base + p2 * w2 + d * q2, q2)]))
        seg3.append((a2, lambda j, d, base=base: o_ref.at[:, cols(base + j * w2 + d * q2, q2)]))
        seg4.append((a1, lambda j, d, h=h: o_ref.at[:, cols(h * half + j * w1 + d * q1, q1)]))
    reduce_scatter(0, seg1, rbuf1, acc1)
    reduce_scatter(1, seg2, rbuf2, acc2)
    all_gather(2, seg3)
    all_gather(3, seg4)
    for copy in sends:
        copy.wait_send()


def ray_allreduce(mesh, owned):
    axes = ray_axes(mesh)
    rows, width = owned.shape
    half = width // 2
    w1 = half // axes[0][0]
    w2 = w1 // axes[1][0]
    steps = max(axes[0][0], axes[1][0]) - 1
    return pl.pallas_call(
        functools.partial(allreduce_kernel, axes),
        out_shape=jax.ShapeDtypeStruct((rows, width), jnp.float32),
        in_specs=[pl.BlockSpec(memory_space=pltpu.VMEM)],
        out_specs=pl.BlockSpec(memory_space=pltpu.VMEM),
        scratch_shapes=[
            pltpu.VMEM((2, rows, w1), jnp.float32),
            pltpu.VMEM((2, 2, steps, rows, w1 // 2), jnp.float32),
            pltpu.VMEM((2, 2, steps, rows, w1 // 2), jnp.float32),
            pltpu.VMEM((2, 2, steps, rows, w2 // 2), jnp.float32),
            pltpu.VMEM((2, 2, steps, rows, w2 // 2), jnp.float32),
            pltpu.SemaphoreType.DMA((4, 2, 2, steps)),
            pltpu.SemaphoreType.DMA((4, 2, 2, steps)),
        ],
        compiler_params=pltpu.CompilerParams(
            collective_id=2, has_side_effects=True, vmem_limit_bytes=60 * 1024 * 1024),
    )(owned)


eps_norm = 1e-06


def per_device(mesh, data, sensitivity, block_tiles, block_bundles):
    columns = data.shape[0]
    bundles = block_bundles.reshape(-1)
    requests = lax.all_to_all(block_tiles, "tile", split_axis=1, concat_axis=1, tiled=True).reshape(
        -1
    )
    bundle_onehot = (bundles[:, None] == jnp.arange(BUND_DEV, dtype=jnp.int32)[None, :]).astype(
        jnp.float32
    )
    owner_onehot = (requests[:, None] == jnp.arange(TILE_DEV, dtype=jnp.int32)[None, :]).astype(
        jnp.bfloat16
    )

    def fetch(field_bf):
        owned = field_bf.reshape(columns, TILE_DEV, CB)
        outgoing = jnp.take(owned, requests, axis=1)
        tiles = lax.all_to_all(outgoing, "tile", split_axis=1, concat_axis=1, tiled=True)
        return tiles

    def forward(field_bf):
        tiles = fetch(field_bf)
        partial_value = jnp.einsum(
            "cnk,nrk->ncr", tiles, sensitivity, preferred_element_type=jnp.float32
        )
        summed = jnp.einsum(
            "ncr,nb->cbr", partial_value, bundle_onehot, precision=lax.Precision.HIGHEST
        )
        return summed.reshape(columns, BUND_DEV * RB)

    def adjoint(rays_bf):
        picked = jnp.take(rays_bf.reshape(columns, BUND_DEV, RB), bundles, axis=1)
        terms = jnp.einsum(
            "cnr,nrk->cnk", picked, sensitivity, preferred_element_type=jnp.float32
        ).astype(jnp.bfloat16)
        arrived = lax.all_to_all(terms, "tile", split_axis=1, concat_axis=1, tiled=True)
        owned = jnp.einsum(
            "cnk,nt->ctk", arrived, owner_onehot, preferred_element_type=jnp.float32
        ).reshape(columns, TILE_DEV * CB)
        total = ray_allreduce(mesh, owned)
        return total

    def cell_norm(field):
        local = jnp.sum(field * field, axis=1)
        total = group_sum(mesh, ("tile",), 1, local)
        return jnp.sqrt(total + eps_norm)

    def ray_norm(rays):
        total = group_sum(mesh, ("ray", "tile"), 0, jnp.sum(rays * rays, axis=1))
        return jnp.sqrt(total + eps_norm)

    beta_now = ray_norm(data)
    rays_dir = data / beta_now[:, None]
    model_dir = adjoint(rays_dir.astype(jnp.bfloat16))
    alpha_now = cell_norm(model_dir)
    model_dir = model_dir / alpha_now[:, None]
    search = model_dir
    solution = jnp.zeros_like(model_dir)
    phi_bar = beta_now
    rho_bar = alpha_now
    for step in range(ITERS):
        rounded = model_dir.astype(jnp.bfloat16)
        rays_dir = forward(rounded) - alpha_now[:, None] * rays_dir
        beta_now = ray_norm(rays_dir)
        rays_dir = rays_dir / beta_now[:, None]
        rho_now = jnp.sqrt(rho_bar * rho_bar + beta_now * beta_now)
        cosine = rho_bar / rho_now
        sine_part = beta_now / rho_now
        phi_now = cosine * phi_bar
        phi_bar = sine_part * phi_bar
        solution = solution + (phi_now / rho_now)[:, None] * search
        if step + 1 < ITERS:
            model_dir = adjoint(rays_dir.astype(jnp.bfloat16)) - beta_now[:, None] * model_dir
            alpha_now = cell_norm(model_dir)
            model_dir = model_dir / alpha_now[:, None]
            theta_now = sine_part * alpha_now
            rho_bar = -cosine * alpha_now
            search = model_dir - (theta_now / rho_now)[:, None] * search
    residual = data - forward(solution.astype(jnp.bfloat16))
    return (solution, residual)


def solution(mesh):
    return jax.shard_map(
        functools.partial(per_device, mesh),
        mesh=mesh,
        in_specs=(
            P(None, ("ray", "tile")),
            P(("ray", "tile"), None, None),
            P(("ray", "tile"), None, None),
            P(("ray", "tile"), None, None),
        ),
        out_specs=(P(None, "tile"), P(None, ("ray", "tile"))),
        check_vma=False,
    )
```

```python
import jax
import jax.numpy as jnp
from jax import lax
from jax.sharding import PartitionSpec as P

RB = 256
CB = 512
ITERS = 2
BUND_DEV = 8
TILE_DEV = 48


import functools
from jax.experimental import pallas as pl
from jax.experimental.pallas import tpu as pltpu

MESH = pl.DeviceIdType.MESH


def stage_plan(mesh, axes):
    plan = [(axis, mesh.shape[axis], 1) for axis in ("tile", "ray") if axis in axes]
    return tuple(stage for stage in plan if stage[1] > 1)


def reduce_kernel(plan, x_ref, o_ref, vals, send_sems, recv_sems):
    here = {"ray": lax.axis_index("ray"), "tile": lax.axis_index("tile")}

    def peer(axis, size, stride, k):
        idx = here[axis]
        pos = (idx // stride) % size
        other = idx + (((pos + k) % size) - pos) * stride
        coords = dict(here)
        coords[axis] = other
        return (coords["ray"], coords["tile"])

    barrier = pltpu.get_barrier_semaphore()
    count = 0
    for axis, size, stride in plan:
        for k in range(1, size):
            pl.semaphore_signal(barrier, inc=1, device_id=peer(axis, size, stride, k), device_id_type=MESH)
            count += 1
    pl.semaphore_wait(barrier, count)

    vals[0, 0] = x_ref[...]
    copies = []
    for s, (axis, size, stride) in enumerate(plan):
        src = x_ref if s == 0 else vals.at[s, 0]
        stage_copies = []
        for k in range(1, size):
            copy = pltpu.make_async_remote_copy(
                src_ref=src,
                dst_ref=vals.at[s, k],
                send_sem=send_sems.at[s, k],
                recv_sem=recv_sems.at[s, k],
                device_id=peer(axis, size, stride, (size - k) % size),
                device_id_type=MESH,
            )
            copy.start()
            stage_copies.append(copy)
        for copy in stage_copies:
            copy.wait_recv()
        copies += stage_copies
        pos = (here[axis] // stride) % size
        total = vals[s, (size - pos) % size]
        for q in range(1, size):
            total = total + vals[s, (q - pos + size) % size]
        if s + 1 < len(plan):
            vals[s + 1, 0] = total
        else:
            o_ref[...] = total
    for copy in copies:
        copy.wait_send()


def group_sum(mesh, axes, collective_id, partial):
    plan = stage_plan(mesh, axes)
    width = partial.shape[0]
    block = jnp.zeros((8, 128), jnp.float32).at[0, :width].set(partial)
    depth = max(size for _, size, _ in plan)
    out = pl.pallas_call(
        functools.partial(reduce_kernel, plan),
        out_shape=jax.ShapeDtypeStruct((8, 128), jnp.float32),
        in_specs=[pl.BlockSpec(memory_space=pltpu.VMEM)],
        out_specs=pl.BlockSpec(memory_space=pltpu.VMEM),
        scratch_shapes=[
            pltpu.VMEM((len(plan), depth, 8, 128), jnp.float32),
            pltpu.SemaphoreType.DMA((len(plan), depth)),
            pltpu.SemaphoreType.DMA((len(plan), depth)),
        ],
        compiler_params=pltpu.CompilerParams(collective_id=collective_id, has_side_effects=True),
    )(block)
    return out[0, :width]


def ray_axes(mesh):
    rays = mesh.shape["ray"]
    inner = 4 if rays % 4 == 0 else rays
    return ((inner, 1), (rays // inner, inner))


def allreduce_kernel(axes, x_ref, o_ref, part, rbuf1, acc1, rbuf2, send_sems, recv_sems):
    me = lax.axis_index("ray")
    tile = lax.axis_index("tile")
    rows = x_ref.shape[0]
    half = x_ref.shape[1] // 2
    w1 = half // axes[0][0]
    w2 = w1 // axes[1][0]

    def pos(axis):
        size, stride = axis
        return (me // stride) % size

    def peer(axis, k):
        size, stride = axis
        p = pos(axis)
        return (me + (((p - k + size) % size) - p) * stride, tile)

    def cols(start, width):
        return pl.ds(pl.multiple_of(start, 128), width)

    def add_rows(dst, a, b):
        def body(r, carry):
            block = pl.ds(pl.multiple_of(r * 8, 8), 8)
            dst[block, :] = a[block, :] + b[block, :]
            return carry
        lax.fori_loop(0, rows // 8, body, 0)

    barrier = pltpu.get_barrier_semaphore()
    greeted = 0
    for axis in axes:
        for k in range(1, axis[0]):
            pl.semaphore_signal(barrier, inc=1, device_id=peer(axis, k), device_id_type=MESH)
            greeted += 1
    pl.semaphore_wait(barrier, greeted)

    plans = [(axes[0], axes[1]), (axes[1], axes[0])]
    sends = []

    def send(stage, h, d, s, axis, src, dst, landing):
        size = axis[0]
        k = size - 1 if d == 0 else 1
        sems = dict(send_sem=send_sems.at[stage, h, d, s], recv_sem=recv_sems.at[stage, h, d, s],
                    device_id=peer(axis, k), device_id_type=MESH)
        copy = pltpu.make_async_remote_copy(src_ref=src, dst_ref=dst, **sems)
        copy.start()
        sends.append(copy)
        return pltpu.make_async_remote_copy(src_ref=src, dst_ref=landing, **sems)

    def reduce_scatter(stage, segs, rbuf, acc):
        steps = segs[0][0][0] - 1
        for s in range(steps):
            waits = []
            for h, (axis, own, final) in enumerate(segs):
                size, p = axis[0], pos(axis)
                for d in range(2):
                    sign = 1 if d == 0 else -1
                    src = own((p - sign * (s + 1) + 2 * size) % size, d) if s == 0 else acc.at[h, d, s - 1]
                    waits.append((h, d, send(stage, h, d, s, axis, src, rbuf.at[h, d, s], rbuf.at[h, d, s])))
            for h, d, copy in waits:
                copy.wait_recv()
            for h, (axis, own, final) in enumerate(segs):
                size, p = axis[0], pos(axis)
                for d in range(2):
                    sign = 1 if d == 0 else -1
                    mine = own((p - sign * (s + 2) + 2 * size) % size, d)
                    dst = final(d) if s == steps - 1 else acc.at[h, d, s]
                    add_rows(dst, rbuf.at[h, d, s], mine)

    def all_gather(stage, segs):
        steps = segs[0][0][0] - 1
        for s in range(steps):
            waits = []
            for h, (axis, region) in enumerate(segs):
                size, p = axis[0], pos(axis)
                for d in range(2):
                    sign = 1 if d == 0 else -1
                    src = region((p - sign * s + 2 * size) % size, d)
                    landing = region((p - sign * (s + 1) + 2 * size) % size, d)
                    waits.append(send(stage, h, d, s, axis, src, src, landing))
            for copy in waits:
                copy.wait_recv()

    def direct_reduce_scatter(stage, segs, rbuf, width):
        waits = []
        for h, (axis, own, final) in enumerate(segs):
            size, p = axis[0], pos(axis)
            for k in range(1, size):
                slot = rbuf.at[h, k - 1]
                copy = pltpu.make_async_remote_copy(
                    src_ref=own((p - k + size) % size), dst_ref=slot,
                    send_sem=send_sems.at[stage, h, 0, k - 1], recv_sem=recv_sems.at[stage, h, 0, k - 1],
                    device_id=peer(axis, k), device_id_type=MESH)
                copy.start()
                sends.append(copy)
                waits.append(copy)
        for copy in waits:
            copy.wait_recv()
        for h, (axis, own, final) in enumerate(segs):
            size, p = axis[0], pos(axis)
            def body(r, carry, h=h, size=size, p=p, own=own, final=final):
                block = pl.ds(pl.multiple_of(r * 8, 8), 8)
                total = None
                for q in range(size):
                    k = (q - p + size) % size
                    mine = own(p)[block, :]
                    other = rbuf[h, jnp.maximum(k - 1, 0), block, :]
                    val = jnp.where(k == 0, mine, other)
                    total = val if total is None else total + val
                final[block, :] = total
                return carry
            lax.fori_loop(0, rows // 8, body, 0)

    def direct_all_gather(stage, segs):
        waits = []
        for h, (axis, region) in enumerate(segs):
            size, p = axis[0], pos(axis)
            for k in range(1, size):
                copy = pltpu.make_async_remote_copy(
                    src_ref=region(p), dst_ref=region(p),
                    send_sem=send_sems.at[stage, h, 0, k - 1], recv_sem=recv_sems.at[stage, h, 0, k - 1],
                    device_id=peer(axis, k), device_id_type=MESH)
                copy.start()
                sends.append(copy)
                waits.append(pltpu.make_async_remote_copy(
                    src_ref=region(p), dst_ref=region((p + k) % size),
                    send_sem=send_sems.at[stage, h, 0, k - 1], recv_sem=recv_sems.at[stage, h, 0, k - 1],
                    device_id=peer(axis, k), device_id_type=MESH))
        for copy in waits:
            copy.wait_recv()

    q1, q2 = w1 // 2, w2 // 2
    seg1, seg2, seg3, seg4 = [], [], [], []
    for h, (a1, a2) in enumerate(plans):
        p1, p2 = pos(a1), pos(a2)
        base = h * half + p1 * w1
        seg1.append((a1,
                     lambda j, d, h=h: x_ref.at[:, cols(h * half + j * w1 + d * q1, q1)],
                     lambda d, h=h: part.at[h, :, cols(d * q1, q1)]))
        seg2.append((a2,
                     lambda j, h=h: part.at[h, :, cols(j * w2, w2)],
                     o_ref.at[:, cols(base + p2 * w2, w2)]))
        seg3.append((a2, lambda j, base=base: o_ref.at[:, cols(base + j * w2, w2)]))
        seg4.append((a1, lambda j, d, h=h: o_ref.at[:, cols(h * half + j * w1 + d * q1, q1)]))
    reduce_scatter(0, seg1, rbuf1, acc1)
    direct_reduce_scatter(1, seg2, rbuf2, w2)
    direct_all_gather(2, seg3)
    all_gather(3, seg4)
    for copy in sends:
        copy.wait_send()


def ray_allreduce(mesh, owned):
    axes = ray_axes(mesh)
    rows, width = owned.shape
    half = width // 2
    w1 = half // axes[0][0]
    w2 = w1 // axes[1][0]
    steps = max(axes[0][0], axes[1][0]) - 1
    return pl.pallas_call(
        functools.partial(allreduce_kernel, axes),
        out_shape=jax.ShapeDtypeStruct((rows, width), jnp.float32),
        in_specs=[pl.BlockSpec(memory_space=pltpu.VMEM)],
        out_specs=pl.BlockSpec(memory_space=pltpu.VMEM),
        scratch_shapes=[
            pltpu.VMEM((2, rows, w1), jnp.float32),
            pltpu.VMEM((2, 2, steps, rows, w1 // 2), jnp.float32),
            pltpu.VMEM((2, 2, steps, rows, w1 // 2), jnp.float32),
            pltpu.VMEM((2, steps, rows, w2), jnp.float32),
            pltpu.SemaphoreType.DMA((4, 2, 2, steps)),
            pltpu.SemaphoreType.DMA((4, 2, 2, steps)),
        ],
        compiler_params=pltpu.CompilerParams(
            collective_id=2, has_side_effects=True, vmem_limit_bytes=60 * 1024 * 1024),
    )(owned)


eps_norm = 1e-06


def per_device(mesh, data, sensitivity, block_tiles, block_bundles):
    columns = data.shape[0]
    bundles = block_bundles.reshape(-1)
    requests = lax.all_to_all(block_tiles, "tile", split_axis=1, concat_axis=1, tiled=True).reshape(
        -1
    )
    bundle_onehot = (bundles[:, None] == jnp.arange(BUND_DEV, dtype=jnp.int32)[None, :]).astype(
        jnp.float32
    )
    owner_onehot = (requests[:, None] == jnp.arange(TILE_DEV, dtype=jnp.int32)[None, :]).astype(
        jnp.bfloat16
    )

    def fetch(field_bf):
        owned = field_bf.reshape(columns, TILE_DEV, CB)
        outgoing = jnp.take(owned, requests, axis=1)
        tiles = lax.all_to_all(outgoing, "tile", split_axis=1, concat_axis=1, tiled=True)
        return tiles

    def forward(field_bf):
        tiles = fetch(field_bf)
        partial_value = jnp.einsum(
            "cnk,nrk->ncr", tiles, sensitivity, preferred_element_type=jnp.float32
        )
        summed = jnp.einsum(
            "ncr,nb->cbr", partial_value, bundle_onehot, precision=lax.Precision.HIGHEST
        )
        return summed.reshape(columns, BUND_DEV * RB)

    def adjoint(rays_bf):
        picked = jnp.take(rays_bf.reshape(columns, BUND_DEV, RB), bundles, axis=1)
        terms = jnp.einsum(
            "cnr,nrk->cnk", picked, sensitivity, preferred_element_type=jnp.float32
        ).astype(jnp.bfloat16)
        arrived = lax.all_to_all(terms, "tile", split_axis=1, concat_axis=1, tiled=True)
        owned = jnp.einsum(
            "cnk,nt->ctk", arrived, owner_onehot, preferred_element_type=jnp.float32
        ).reshape(columns, TILE_DEV * CB)
        total = ray_allreduce(mesh, owned)
        return total

    def cell_norm(field):
        local = jnp.sum(field * field, axis=1)
        total = group_sum(mesh, ("tile",), 1, local)
        return jnp.sqrt(total + eps_norm)

    def ray_norm(rays):
        total = group_sum(mesh, ("ray", "tile"), 0, jnp.sum(rays * rays, axis=1))
        return jnp.sqrt(total + eps_norm)

    beta_now = ray_norm(data)
    rays_dir = data / beta_now[:, None]
    model_dir = adjoint(rays_dir.astype(jnp.bfloat16))
    alpha_now = cell_norm(model_dir)
    model_dir = model_dir / alpha_now[:, None]
    search = model_dir
    solution = jnp.zeros_like(model_dir)
    phi_bar = beta_now
    rho_bar = alpha_now
    for step in range(ITERS):
        rounded = model_dir.astype(jnp.bfloat16)
        rays_dir = forward(rounded) - alpha_now[:, None] * rays_dir
        beta_now = ray_norm(rays_dir)
        rays_dir = rays_dir / beta_now[:, None]
        rho_now = jnp.sqrt(rho_bar * rho_bar + beta_now * beta_now)
        cosine = rho_bar / rho_now
        sine_part = beta_now / rho_now
        phi_now = cosine * phi_bar
        phi_bar = sine_part * phi_bar
        solution = solution + (phi_now / rho_now)[:, None] * search
        if step + 1 < ITERS:
            model_dir = adjoint(rays_dir.astype(jnp.bfloat16)) - beta_now[:, None] * model_dir
            alpha_now = cell_norm(model_dir)
            model_dir = model_dir / alpha_now[:, None]
            theta_now = sine_part * alpha_now
            rho_bar = -cosine * alpha_now
            search = model_dir - (theta_now / rho_now)[:, None] * search
    residual = data - forward(solution.astype(jnp.bfloat16))
    return (solution, residual)


def solution(mesh):
    return jax.shard_map(
        functools.partial(per_device, mesh),
        mesh=mesh,
        in_specs=(
            P(None, ("ray", "tile")),
            P(("ray", "tile"), None, None),
            P(("ray", "tile"), None, None),
            P(("ray", "tile"), None, None),
        ),
        out_specs=(P(None, "tile"), P(None, ("ray", "tile"))),
        check_vma=False,
    )
```

```python
import jax
import jax.numpy as jnp
from jax import lax
from jax.sharding import PartitionSpec as P

RB = 256
CB = 512
ITERS = 2
BUND_DEV = 8
TILE_DEV = 48


import functools
from jax.experimental import pallas as pl
from jax.experimental.pallas import tpu as pltpu

MESH = pl.DeviceIdType.MESH


def stage_plan(mesh, axes):
    plan = [(axis, mesh.shape[axis], 1) for axis in ("tile", "ray") if axis in axes]
    return tuple(stage for stage in plan if stage[1] > 1)


def reduce_kernel(plan, x_ref, o_ref, vals, send_sems, recv_sems):
    here = {"ray": lax.axis_index("ray"), "tile": lax.axis_index("tile")}

    def peer(axis, size, stride, k):
        idx = here[axis]
        pos = (idx // stride) % size
        other = idx + (((pos + k) % size) - pos) * stride
        coords = dict(here)
        coords[axis] = other
        return (coords["ray"], coords["tile"])

    barrier = pltpu.get_barrier_semaphore()
    count = 0
    for axis, size, stride in plan:
        for k in range(1, size):
            pl.semaphore_signal(barrier, inc=1, device_id=peer(axis, size, stride, k), device_id_type=MESH)
            count += 1
    pl.semaphore_wait(barrier, count)

    vals[0, 0] = x_ref[...]
    copies = []
    for s, (axis, size, stride) in enumerate(plan):
        src = x_ref if s == 0 else vals.at[s, 0]
        stage_copies = []
        for k in range(1, size):
            copy = pltpu.make_async_remote_copy(
                src_ref=src,
                dst_ref=vals.at[s, k],
                send_sem=send_sems.at[s, k],
                recv_sem=recv_sems.at[s, k],
                device_id=peer(axis, size, stride, (size - k) % size),
                device_id_type=MESH,
            )
            copy.start()
            stage_copies.append(copy)
        for copy in stage_copies:
            copy.wait_recv()
        copies += stage_copies
        pos = (here[axis] // stride) % size
        total = vals[s, (size - pos) % size]
        for q in range(1, size):
            total = total + vals[s, (q - pos + size) % size]
        if s + 1 < len(plan):
            vals[s + 1, 0] = total
        else:
            o_ref[...] = total
    for copy in copies:
        copy.wait_send()


def group_sum(mesh, axes, collective_id, partial):
    plan = stage_plan(mesh, axes)
    width = partial.shape[0]
    block = jnp.zeros((8, 128), jnp.float32).at[0, :width].set(partial)
    depth = max(size for _, size, _ in plan)
    out = pl.pallas_call(
        functools.partial(reduce_kernel, plan),
        out_shape=jax.ShapeDtypeStruct((8, 128), jnp.float32),
        in_specs=[pl.BlockSpec(memory_space=pltpu.VMEM)],
        out_specs=pl.BlockSpec(memory_space=pltpu.VMEM),
        scratch_shapes=[
            pltpu.VMEM((len(plan), depth, 8, 128), jnp.float32),
            pltpu.SemaphoreType.DMA((len(plan), depth)),
            pltpu.SemaphoreType.DMA((len(plan), depth)),
        ],
        compiler_params=pltpu.CompilerParams(collective_id=collective_id, has_side_effects=True),
    )(block)
    return out[0, :width]


def ray_axes(mesh):
    rays = mesh.shape["ray"]
    inner = 4 if rays % 4 == 0 else rays
    return ((inner, 1), (rays // inner, inner))


def allreduce_kernel(axes, x_ref, o_ref, part, rbuf1, acc1, rbuf2, send_sems, recv_sems):
    me = lax.axis_index("ray")
    tile = lax.axis_index("tile")
    half = x_ref.shape[0] // 2
    w1 = half // axes[0][0]
    w2 = w1 // axes[1][0]

    def pos(axis):
        size, stride = axis
        return (me // stride) % size

    def peer(axis, k):
        size, stride = axis
        p = pos(axis)
        return (me + (((p - k + size) % size) - p) * stride, tile)

    def cols(start, width):
        return pl.ds(start, width)

    def add_rows(dst, a, b):
        def body(r, carry):
            dst[r] = a[r] + b[r]
            return carry
        lax.fori_loop(0, dst.shape[0], body, 0)

    barrier = pltpu.get_barrier_semaphore()
    greeted = 0
    for axis in axes:
        for k in range(1, axis[0]):
            pl.semaphore_signal(barrier, inc=1, device_id=peer(axis, k), device_id_type=MESH)
            greeted += 1
    pl.semaphore_wait(barrier, greeted)

    plans = [(axes[0], axes[1]), (axes[1], axes[0])]
    sends = []

    def send(stage, h, d, s, axis, src, dst, landing):
        size = axis[0]
        k = size - 1 if d == 0 else 1
        sems = dict(send_sem=send_sems.at[stage, h, d, s], recv_sem=recv_sems.at[stage, h, d, s],
                    device_id=peer(axis, k), device_id_type=MESH)
        copy = pltpu.make_async_remote_copy(src_ref=src, dst_ref=dst, **sems)
        copy.start()
        sends.append(copy)
        return pltpu.make_async_remote_copy(src_ref=src, dst_ref=landing, **sems)

    def reduce_scatter(stage, segs, rbuf, acc):
        steps = segs[0][0][0] - 1
        for s in range(steps):
            waits = []
            for h, (axis, own, final) in enumerate(segs):
                size, p = axis[0], pos(axis)
                for d in range(2):
                    sign = 1 if d == 0 else -1
                    src = own((p - sign * (s + 1) + 2 * size) % size, d) if s == 0 else acc.at[h, d, s - 1]
                    waits.append((h, d, send(stage, h, d, s, axis, src, rbuf.at[h, d, s], rbuf.at[h, d, s])))
            for h, d, copy in waits:
                copy.wait_recv()
            for h, (axis, own, final) in enumerate(segs):
                size, p = axis[0], pos(axis)
                for d in range(2):
                    sign = 1 if d == 0 else -1
                    mine = own((p - sign * (s + 2) + 2 * size) % size, d)
                    dst = final(d) if s == steps - 1 else acc.at[h, d, s]
                    add_rows(dst, rbuf.at[h, d, s], mine)

    def all_gather(stage, segs):
        steps = segs[0][0][0] - 1
        for s in range(steps):
            waits = []
            for h, (axis, region) in enumerate(segs):
                size, p = axis[0], pos(axis)
                for d in range(2):
                    sign = 1 if d == 0 else -1
                    src = region((p - sign * s + 2 * size) % size, d)
                    landing = region((p - sign * (s + 1) + 2 * size) % size, d)
                    waits.append(send(stage, h, d, s, axis, src, src, landing))
            for copy in waits:
                copy.wait_recv()

    def direct_reduce_scatter(stage, segs, rbuf, width):
        waits = []
        for h, (axis, own, final) in enumerate(segs):
            size, p = axis[0], pos(axis)
            for k in range(1, size):
                slot = rbuf.at[h, k - 1]
                copy = pltpu.make_async_remote_copy(
                    src_ref=own((p - k + size) % size), dst_ref=slot,
                    send_sem=send_sems.at[stage, h, 0, k - 1], recv_sem=recv_sems.at[stage, h, 0, k - 1],
                    device_id=peer(axis, k), device_id_type=MESH)
                copy.start()
                sends.append(copy)
                waits.append(copy)
        for copy in waits:
            copy.wait_recv()
        for h, (axis, own, final) in enumerate(segs):
            size, p = axis[0], pos(axis)
            def body(r, carry, h=h, size=size, p=p, own=own, final=final):
                total = None
                for q in range(size):
                    k = (q - p + size) % size
                    mine = own(p)[r]
                    other = rbuf[h, jnp.maximum(k - 1, 0), r]
                    val = jnp.where(k == 0, mine, other)
                    total = val if total is None else total + val
                final[r] = total
                return carry
            lax.fori_loop(0, width, body, 0)

    def direct_all_gather(stage, segs):
        waits = []
        for h, (axis, region) in enumerate(segs):
            size, p = axis[0], pos(axis)
            for k in range(1, size):
                copy = pltpu.make_async_remote_copy(
                    src_ref=region(p), dst_ref=region(p),
                    send_sem=send_sems.at[stage, h, 0, k - 1], recv_sem=recv_sems.at[stage, h, 0, k - 1],
                    device_id=peer(axis, k), device_id_type=MESH)
                copy.start()
                sends.append(copy)
                waits.append(pltpu.make_async_remote_copy(
                    src_ref=region(p), dst_ref=region((p + k) % size),
                    send_sem=send_sems.at[stage, h, 0, k - 1], recv_sem=recv_sems.at[stage, h, 0, k - 1],
                    device_id=peer(axis, k), device_id_type=MESH))
        for copy in waits:
            copy.wait_recv()

    q1, q2 = w1 // 2, w2 // 2
    seg1, seg2, seg3, seg4 = [], [], [], []
    for h, (a1, a2) in enumerate(plans):
        p1, p2 = pos(a1), pos(a2)
        base = h * half + p1 * w1
        seg1.append((a1,
                     lambda j, d, h=h: x_ref.at[cols(h * half + j * w1 + d * q1, q1)],
                     lambda d, h=h: part.at[h, cols(d * q1, q1)]))
        seg2.append((a2,
                     lambda j, h=h: part.at[h, cols(j * w2, w2)],
                     o_ref.at[cols(base + p2 * w2, w2)]))
        seg3.append((a2, lambda j, base=base: o_ref.at[cols(base + j * w2, w2)]))
        seg4.append((a1, lambda j, d, h=h: o_ref.at[cols(h * half + j * w1 + d * q1, q1)]))
    reduce_scatter(0, seg1, rbuf1, acc1)
    direct_reduce_scatter(1, seg2, rbuf2, w2)
    direct_all_gather(2, seg3)
    all_gather(3, seg4)
    for copy in sends:
        copy.wait_send()


def ray_allreduce(mesh, owned):
    axes = ray_axes(mesh)
    rows = owned.shape[0]
    inner = owned.shape[1:]
    half = rows // 2
    w1 = half // axes[0][0]
    w2 = w1 // axes[1][0]
    steps = max(axes[0][0], axes[1][0]) - 1
    return pl.pallas_call(
        functools.partial(allreduce_kernel, axes),
        out_shape=jax.ShapeDtypeStruct(owned.shape, jnp.float32),
        in_specs=[pl.BlockSpec(memory_space=pltpu.VMEM)],
        out_specs=pl.BlockSpec(memory_space=pltpu.VMEM),
        scratch_shapes=[
            pltpu.VMEM((2, w1) + inner, jnp.float32),
            pltpu.VMEM((2, 2, steps, w1 // 2) + inner, jnp.float32),
            pltpu.VMEM((2, 2, steps, w1 // 2) + inner, jnp.float32),
            pltpu.VMEM((2, steps, w2) + inner, jnp.float32),
            pltpu.SemaphoreType.DMA((4, 2, 2, steps)),
            pltpu.SemaphoreType.DMA((4, 2, 2, steps)),
        ],
        compiler_params=pltpu.CompilerParams(
            collective_id=2, has_side_effects=True, vmem_limit_bytes=60 * 1024 * 1024),
    )(owned)


eps_norm = 1e-06


def per_device(mesh, data, sensitivity, block_tiles, block_bundles):
    columns = data.shape[0]
    bundles = block_bundles.reshape(-1)
    requests = lax.all_to_all(block_tiles, "tile", split_axis=1, concat_axis=1, tiled=True).reshape(
        -1
    )
    bundle_onehot = (bundles[:, None] == jnp.arange(BUND_DEV, dtype=jnp.int32)[None, :]).astype(
        jnp.float32
    )
    owner_onehot = (requests[:, None] == jnp.arange(TILE_DEV, dtype=jnp.int32)[None, :]).astype(
        jnp.bfloat16
    )

    def fetch(field_bf):
        owned = field_bf.reshape(columns, TILE_DEV, CB)
        outgoing = jnp.take(owned, requests, axis=1)
        tiles = lax.all_to_all(outgoing, "tile", split_axis=1, concat_axis=1, tiled=True)
        return tiles

    def forward(field_bf):
        tiles = fetch(field_bf)
        partial_value = jnp.einsum(
            "cnk,nrk->ncr", tiles, sensitivity, preferred_element_type=jnp.float32
        )
        summed = jnp.einsum(
            "ncr,nb->cbr", partial_value, bundle_onehot, precision=lax.Precision.HIGHEST
        )
        return summed.reshape(columns, BUND_DEV * RB)

    def adjoint(rays_bf):
        picked = jnp.take(rays_bf.reshape(columns, BUND_DEV, RB), bundles, axis=1)
        terms = jnp.einsum(
            "cnr,nrk->cnk", picked, sensitivity, preferred_element_type=jnp.float32
        ).astype(jnp.bfloat16)
        arrived = lax.all_to_all(terms, "tile", split_axis=1, concat_axis=1, tiled=True)
        owned = jnp.einsum(
            "cnk,nt->ctk", arrived, owner_onehot, preferred_element_type=jnp.float32
        )
        total = ray_allreduce(mesh, owned)
        return total

    def cell_norm(field):
        local = jnp.sum(field * field, axis=(1, 2))
        total = group_sum(mesh, ("tile",), 1, local)
        return jnp.sqrt(total + eps_norm)

    def ray_norm(rays):
        total = group_sum(mesh, ("ray", "tile"), 0, jnp.sum(rays * rays, axis=1))
        return jnp.sqrt(total + eps_norm)

    beta_now = ray_norm(data)
    rays_dir = data / beta_now[:, None]
    model_dir = adjoint(rays_dir.astype(jnp.bfloat16))
    alpha_now = cell_norm(model_dir)
    model_dir = model_dir / alpha_now[:, None, None]
    search = model_dir
    solution = jnp.zeros_like(model_dir)
    phi_bar = beta_now
    rho_bar = alpha_now
    for step in range(ITERS):
        rounded = model_dir.astype(jnp.bfloat16)
        rays_dir = forward(rounded) - alpha_now[:, None] * rays_dir
        beta_now = ray_norm(rays_dir)
        rays_dir = rays_dir / beta_now[:, None]
        rho_now = jnp.sqrt(rho_bar * rho_bar + beta_now * beta_now)
        cosine = rho_bar / rho_now
        sine_part = beta_now / rho_now
        phi_now = cosine * phi_bar
        phi_bar = sine_part * phi_bar
        solution = solution + (phi_now / rho_now)[:, None, None] * search
        if step + 1 < ITERS:
            model_dir = adjoint(rays_dir.astype(jnp.bfloat16)) - beta_now[:, None, None] * model_dir
            alpha_now = cell_norm(model_dir)
            model_dir = model_dir / alpha_now[:, None, None]
            theta_now = sine_part * alpha_now
            rho_bar = -cosine * alpha_now
            search = model_dir - (theta_now / rho_now)[:, None, None] * search
    residual = data - forward(solution.astype(jnp.bfloat16))
    return (solution.reshape(columns, TILE_DEV * CB), residual)


def solution(mesh):
    return jax.shard_map(
        functools.partial(per_device, mesh),
        mesh=mesh,
        in_specs=(
            P(None, ("ray", "tile")),
            P(("ray", "tile"), None, None),
            P(("ray", "tile"), None, None),
            P(("ray", "tile"), None, None),
        ),
        out_specs=(P(None, "tile"), P(None, ("ray", "tile"))),
        check_vma=False,
    )
```

```python
import jax
import jax.numpy as jnp
from jax import lax
from jax.sharding import PartitionSpec as P

RB = 256
CB = 512
ITERS = 2
BUND_DEV = 8
TILE_DEV = 48


import functools
from jax.experimental import pallas as pl
from jax.experimental.pallas import tpu as pltpu

MESH = pl.DeviceIdType.MESH


def stage_plan(mesh, axes):
    plan = [(axis, mesh.shape[axis], 1) for axis in ("tile", "ray") if axis in axes]
    return tuple(stage for stage in plan if stage[1] > 1)


def reduce_kernel(plan, x_ref, o_ref, vals, send_sems, recv_sems):
    here = {"ray": lax.axis_index("ray"), "tile": lax.axis_index("tile")}

    def peer(axis, size, stride, k):
        idx = here[axis]
        pos = (idx // stride) % size
        other = idx + (((pos + k) % size) - pos) * stride
        coords = dict(here)
        coords[axis] = other
        return (coords["ray"], coords["tile"])

    vals[0, 0] = x_ref[...]
    copies = []
    for s, (axis, size, stride) in enumerate(plan):
        src = x_ref if s == 0 else vals.at[s, 0]
        stage_copies = []
        for k in range(1, size):
            copy = pltpu.make_async_remote_copy(
                src_ref=src,
                dst_ref=vals.at[s, k],
                send_sem=send_sems.at[s, k],
                recv_sem=recv_sems.at[s, k],
                device_id=peer(axis, size, stride, (size - k) % size),
                device_id_type=MESH,
            )
            copy.start()
            stage_copies.append(copy)
        for copy in stage_copies:
            copy.wait_recv()
        copies += stage_copies
        pos = (here[axis] // stride) % size
        total = vals[s, (size - pos) % size]
        for q in range(1, size):
            total = total + vals[s, (q - pos + size) % size]
        if s + 1 < len(plan):
            vals[s + 1, 0] = total
        else:
            o_ref[...] = total
    for copy in copies:
        copy.wait_send()


def group_sum(mesh, axes, collective_id, partial):
    plan = stage_plan(mesh, axes)
    width = partial.shape[0]
    block = jnp.zeros((8, 128), jnp.float32).at[0, :width].set(partial)
    depth = max(size for _, size, _ in plan)
    out = pl.pallas_call(
        functools.partial(reduce_kernel, plan),
        out_shape=jax.ShapeDtypeStruct((8, 128), jnp.float32),
        in_specs=[pl.BlockSpec(memory_space=pltpu.VMEM)],
        out_specs=pl.BlockSpec(memory_space=pltpu.VMEM),
        scratch_shapes=[
            pltpu.VMEM((len(plan), depth, 8, 128), jnp.float32),
            pltpu.SemaphoreType.DMA((len(plan), depth)),
            pltpu.SemaphoreType.DMA((len(plan), depth)),
        ],
        compiler_params=pltpu.CompilerParams(has_side_effects=True),
    )(block)
    return out[0, :width]


def ray_axes(mesh):
    rays = mesh.shape["ray"]
    inner = 4 if rays % 4 == 0 else rays
    return ((inner, 1), (rays // inner, inner))


def allreduce_kernel(axes, x_ref, o_ref, part, rbuf1, acc1, rbuf2, send_sems, recv_sems):
    me = lax.axis_index("ray")
    tile = lax.axis_index("tile")
    rows = x_ref.shape[0]
    half = x_ref.shape[1] // 2
    w1 = half // axes[0][0]
    w2 = w1 // axes[1][0]

    def pos(axis):
        size, stride = axis
        return (me // stride) % size

    def peer(axis, k):
        size, stride = axis
        p = pos(axis)
        return (me + (((p - k + size) % size) - p) * stride, tile)

    def cols(start, width):
        return pl.ds(pl.multiple_of(start, 128), width)

    def add_rows(dst, a, b):
        def body(r, carry):
            block = pl.ds(pl.multiple_of(r * 8, 8), 8)
            dst[block, :] = a[block, :] + b[block, :]
            return carry
        lax.fori_loop(0, rows // 8, body, 0)

    barrier = pltpu.get_barrier_semaphore()
    greeted = 0
    for axis in axes:
        for k in range(1, axis[0]):
            pl.semaphore_signal(barrier, inc=1, device_id=peer(axis, k), device_id_type=MESH)
            greeted += 1
    pl.semaphore_wait(barrier, greeted)

    plans = [(axes[0], axes[1]), (axes[1], axes[0])]
    sends = []

    def send(stage, h, d, s, axis, src, dst, landing):
        size = axis[0]
        k = size - 1 if d == 0 else 1
        sems = dict(send_sem=send_sems.at[stage, h, d, s], recv_sem=recv_sems.at[stage, h, d, s],
                    device_id=peer(axis, k), device_id_type=MESH)
        copy = pltpu.make_async_remote_copy(src_ref=src, dst_ref=dst, **sems)
        copy.start()
        sends.append(copy)
        return pltpu.make_async_remote_copy(src_ref=src, dst_ref=landing, **sems)

    def reduce_scatter(stage, segs, rbuf, acc):
        steps = segs[0][0][0] - 1
        for s in range(steps):
            waits = []
            for h, (axis, own, final) in enumerate(segs):
                size, p = axis[0], pos(axis)
                for d in range(2):
                    sign = 1 if d == 0 else -1
                    src = own((p - sign * (s + 1) + 2 * size) % size, d) if s == 0 else acc.at[h, d, s - 1]
                    waits.append((h, d, send(stage, h, d, s, axis, src, rbuf.at[h, d, s], rbuf.at[h, d, s])))
            for h, d, copy in waits:
                copy.wait_recv()
            for h, (axis, own, final) in enumerate(segs):
                size, p = axis[0], pos(axis)
                for d in range(2):
                    sign = 1 if d == 0 else -1
                    mine = own((p - sign * (s + 2) + 2 * size) % size, d)
                    dst = final(d) if s == steps - 1 else acc.at[h, d, s]
                    add_rows(dst, rbuf.at[h, d, s], mine)

    def all_gather(stage, segs):
        steps = segs[0][0][0] - 1
        for s in range(steps):
            waits = []
            for h, (axis, region) in enumerate(segs):
                size, p = axis[0], pos(axis)
                for d in range(2):
                    sign = 1 if d == 0 else -1
                    src = region((p - sign * s + 2 * size) % size, d)
                    landing = region((p - sign * (s + 1) + 2 * size) % size, d)
                    waits.append(send(stage, h, d, s, axis, src, src, landing))
            for copy in waits:
                copy.wait_recv()

    def direct_reduce_scatter(stage, segs, rbuf, width):
        waits = []
        for h, (axis, own, final) in enumerate(segs):
            size, p = axis[0], pos(axis)
            for k in range(1, size):
                slot = rbuf.at[h, k - 1]
                copy = pltpu.make_async_remote_copy(
                    src_ref=own((p - k + size) % size), dst_ref=slot,
                    send_sem=send_sems.at[stage, h, 0, k - 1], recv_sem=recv_sems.at[stage, h, 0, k - 1],
                    device_id=peer(axis, k), device_id_type=MESH)
                copy.start()
                sends.append(copy)
                waits.append(copy)
        for copy in waits:
            copy.wait_recv()
        for h, (axis, own, final) in enumerate(segs):
            size, p = axis[0], pos(axis)
            def body(r, carry, h=h, size=size, p=p, own=own, final=final):
                block = pl.ds(pl.multiple_of(r * 8, 8), 8)
                total = None
                for q in range(size):
                    k = (q - p + size) % size
                    mine = own(p)[block, :]
                    other = rbuf[h, jnp.maximum(k - 1, 0), block, :]
                    val = jnp.where(k == 0, mine, other)
                    total = val if total is None else total + val
                final[block, :] = total
                return carry
            lax.fori_loop(0, rows // 8, body, 0)

    def direct_all_gather(stage, segs):
        waits = []
        for h, (axis, region) in enumerate(segs):
            size, p = axis[0], pos(axis)
            for k in range(1, size):
                copy = pltpu.make_async_remote_copy(
                    src_ref=region(p), dst_ref=region(p),
                    send_sem=send_sems.at[stage, h, 0, k - 1], recv_sem=recv_sems.at[stage, h, 0, k - 1],
                    device_id=peer(axis, k), device_id_type=MESH)
                copy.start()
                sends.append(copy)
                waits.append(pltpu.make_async_remote_copy(
                    src_ref=region(p), dst_ref=region((p + k) % size),
                    send_sem=send_sems.at[stage, h, 0, k - 1], recv_sem=recv_sems.at[stage, h, 0, k - 1],
                    device_id=peer(axis, k), device_id_type=MESH))
        for copy in waits:
            copy.wait_recv()

    q1, q2 = w1 // 2, w2 // 2
    seg1, seg2, seg3, seg4 = [], [], [], []
    for h, (a1, a2) in enumerate(plans):
        p1, p2 = pos(a1), pos(a2)
        base = h * half + p1 * w1
        seg1.append((a1,
                     lambda j, d, h=h: x_ref.at[:, cols(h * half + j * w1 + d * q1, q1)],
                     lambda d, h=h: part.at[h, :, cols(d * q1, q1)]))
        seg2.append((a2,
                     lambda j, h=h: part.at[h, :, cols(j * w2, w2)],
                     o_ref.at[:, cols(base + p2 * w2, w2)]))
        seg3.append((a2, lambda j, base=base: o_ref.at[:, cols(base + j * w2, w2)]))
        seg4.append((a1, lambda j, d, h=h: o_ref.at[:, cols(h * half + j * w1 + d * q1, q1)]))
    reduce_scatter(0, seg1, rbuf1, acc1)
    direct_reduce_scatter(1, seg2, rbuf2, w2)
    direct_all_gather(2, seg3)
    all_gather(3, seg4)
    for copy in sends:
        copy.wait_send()


def ray_allreduce(mesh, owned):
    axes = ray_axes(mesh)
    rows, width = owned.shape
    half = width // 2
    w1 = half // axes[0][0]
    w2 = w1 // axes[1][0]
    steps = max(axes[0][0], axes[1][0]) - 1
    return pl.pallas_call(
        functools.partial(allreduce_kernel, axes),
        out_shape=jax.ShapeDtypeStruct((rows, width), jnp.float32),
        in_specs=[pl.BlockSpec(memory_space=pltpu.VMEM)],
        out_specs=pl.BlockSpec(memory_space=pltpu.VMEM),
        scratch_shapes=[
            pltpu.VMEM((2, rows, w1), jnp.float32),
            pltpu.VMEM((2, 2, steps, rows, w1 // 2), jnp.float32),
            pltpu.VMEM((2, 2, steps, rows, w1 // 2), jnp.float32),
            pltpu.VMEM((2, steps, rows, w2), jnp.float32),
            pltpu.SemaphoreType.DMA((4, 2, 2, steps)),
            pltpu.SemaphoreType.DMA((4, 2, 2, steps)),
        ],
        compiler_params=pltpu.CompilerParams(
            collective_id=2, has_side_effects=True, vmem_limit_bytes=60 * 1024 * 1024),
    )(owned)


eps_norm = 1e-06


def per_device(mesh, data, sensitivity, block_tiles, block_bundles):
    columns = data.shape[0]
    bundles = block_bundles.reshape(-1)
    requests = lax.all_to_all(block_tiles, "tile", split_axis=1, concat_axis=1, tiled=True).reshape(
        -1
    )
    bundle_onehot = (bundles[:, None] == jnp.arange(BUND_DEV, dtype=jnp.int32)[None, :]).astype(
        jnp.float32
    )
    owner_onehot = (requests[:, None] == jnp.arange(TILE_DEV, dtype=jnp.int32)[None, :]).astype(
        jnp.bfloat16
    )

    def fetch(field_bf):
        owned = field_bf.reshape(columns, TILE_DEV, CB)
        outgoing = jnp.take(owned, requests, axis=1)
        tiles = lax.all_to_all(outgoing, "tile", split_axis=1, concat_axis=1, tiled=True)
        return tiles

    def forward(field_bf):
        tiles = fetch(field_bf)
        partial_value = jnp.einsum(
            "cnk,nrk->ncr", tiles, sensitivity, preferred_element_type=jnp.float32
        )
        summed = jnp.einsum(
            "ncr,nb->cbr", partial_value, bundle_onehot, precision=lax.Precision.HIGHEST
        )
        return summed.reshape(columns, BUND_DEV * RB)

    def adjoint(rays_bf):
        picked = jnp.take(rays_bf.reshape(columns, BUND_DEV, RB), bundles, axis=1)
        terms = jnp.einsum(
            "cnr,nrk->cnk", picked, sensitivity, preferred_element_type=jnp.float32
        ).astype(jnp.bfloat16)
        arrived = lax.all_to_all(terms, "tile", split_axis=1, concat_axis=1, tiled=True)
        owned = jnp.einsum(
            "cnk,nt->ctk", arrived, owner_onehot, preferred_element_type=jnp.float32
        ).reshape(columns, TILE_DEV * CB)
        total = ray_allreduce(mesh, owned)
        return total

    def cell_norm(field):
        local = jnp.sum(field * field, axis=1)
        total = group_sum(mesh, ("tile",), 1, local)
        return jnp.sqrt(total + eps_norm)

    def ray_norm(rays):
        total = group_sum(mesh, ("ray", "tile"), 0, jnp.sum(rays * rays, axis=1))
        return jnp.sqrt(total + eps_norm)

    beta_now = ray_norm(data)
    rays_dir = data / beta_now[:, None]
    model_dir = adjoint(rays_dir.astype(jnp.bfloat16))
    alpha_now = cell_norm(model_dir)
    model_dir = model_dir / alpha_now[:, None]
    search = model_dir
    solution = jnp.zeros_like(model_dir)
    phi_bar = beta_now
    rho_bar = alpha_now
    for step in range(ITERS):
        rounded = model_dir.astype(jnp.bfloat16)
        rays_dir = forward(rounded) - alpha_now[:, None] * rays_dir
        beta_now = ray_norm(rays_dir)
        rays_dir = rays_dir / beta_now[:, None]
        rho_now = jnp.sqrt(rho_bar * rho_bar + beta_now * beta_now)
        cosine = rho_bar / rho_now
        sine_part = beta_now / rho_now
        phi_now = cosine * phi_bar
        phi_bar = sine_part * phi_bar
        solution = solution + (phi_now / rho_now)[:, None] * search
        if step + 1 < ITERS:
            model_dir = adjoint(rays_dir.astype(jnp.bfloat16)) - beta_now[:, None] * model_dir
            alpha_now = cell_norm(model_dir)
            model_dir = model_dir / alpha_now[:, None]
            theta_now = sine_part * alpha_now
            rho_bar = -cosine * alpha_now
            search = model_dir - (theta_now / rho_now)[:, None] * search
    residual = data - forward(solution.astype(jnp.bfloat16))
    return (solution, residual)


def solution(mesh):
    return jax.shard_map(
        functools.partial(per_device, mesh),
        mesh=mesh,
        in_specs=(
            P(None, ("ray", "tile")),
            P(("ray", "tile"), None, None),
            P(("ray", "tile"), None, None),
            P(("ray", "tile"), None, None),
        ),
        out_specs=(P(None, "tile"), P(None, ("ray", "tile"))),
        check_vma=False,
    )
```

```python
import jax
import jax.numpy as jnp
from jax import lax
from jax.sharding import PartitionSpec as P

RB = 256
CB = 512
ITERS = 2
BUND_DEV = 8
TILE_DEV = 48


import functools
from jax.experimental import pallas as pl
from jax.experimental.pallas import tpu as pltpu

MESH = pl.DeviceIdType.MESH


def stage_plan(mesh, axes):
    plan = [(axis, mesh.shape[axis], 1) for axis in ("tile", "ray") if axis in axes]
    return tuple(stage for stage in plan if stage[1] > 1)


def reduce_kernel(plan, x_ref, o_ref, vals, send_sems, recv_sems):
    here = {"ray": lax.axis_index("ray"), "tile": lax.axis_index("tile")}

    def peer(axis, size, stride, k):
        idx = here[axis]
        pos = (idx // stride) % size
        other = idx + (((pos + k) % size) - pos) * stride
        coords = dict(here)
        coords[axis] = other
        return (coords["ray"], coords["tile"])

    barrier = pltpu.get_barrier_semaphore()
    count = 0
    for axis, size, stride in plan:
        def greet(k, carry, axis=axis, size=size, stride=stride):
            pl.semaphore_signal(barrier, inc=1, device_id=peer(axis, size, stride, k), device_id_type=MESH)
            return carry
        lax.fori_loop(1, size, greet, 0)
        count += size - 1
    pl.semaphore_wait(barrier, count)

    def copy_of(s, axis, size, stride, k):
        src = x_ref if s == 0 else vals.at[s, 0]
        return pltpu.make_async_remote_copy(
            src_ref=src,
            dst_ref=vals.at[s, k],
            send_sem=send_sems.at[s, k],
            recv_sem=recv_sems.at[s, k],
            device_id=peer(axis, size, stride, (size - k) % size),
            device_id_type=MESH,
        )

    for s, (axis, size, stride) in enumerate(plan):
        def start(k, carry, s=s, axis=axis, size=size, stride=stride):
            copy_of(s, axis, size, stride, k).start()
            return carry

        def arrive(k, carry, s=s, axis=axis, size=size, stride=stride):
            copy_of(s, axis, size, stride, k).wait_recv()
            return carry
        lax.fori_loop(1, size, start, 0)
        lax.fori_loop(1, size, arrive, 0)
        pos = (here[axis] // stride) % size
        own = x_ref[...] if s == 0 else vals[s, 0]
        total = jnp.where(pos == 0, own, vals[s, (size - pos) % size])
        for q in range(1, size):
            total = total + jnp.where(pos == q, own, vals[s, (q - pos + size) % size])
        if s + 1 < len(plan):
            vals[s + 1, 0] = total
        else:
            o_ref[...] = total
    for s, (axis, size, stride) in enumerate(plan):
        def sent(k, carry, s=s, axis=axis, size=size, stride=stride):
            copy_of(s, axis, size, stride, k).wait_send()
            return carry
        lax.fori_loop(1, size, sent, 0)


def group_sum(mesh, axes, collective_id, partial):
    plan = stage_plan(mesh, axes)
    width = partial.shape[0]
    block = jnp.zeros((8, 128), jnp.float32).at[0, :width].set(partial)
    depth = max(size for _, size, _ in plan)
    out = pl.pallas_call(
        functools.partial(reduce_kernel, plan),
        out_shape=jax.ShapeDtypeStruct((8, 128), jnp.float32),
        in_specs=[pl.BlockSpec(memory_space=pltpu.VMEM)],
        out_specs=pl.BlockSpec(memory_space=pltpu.VMEM),
        scratch_shapes=[
            pltpu.VMEM((len(plan), depth, 8, 128), jnp.float32),
            pltpu.SemaphoreType.DMA((len(plan), depth)),
            pltpu.SemaphoreType.DMA((len(plan), depth)),
        ],
        compiler_params=pltpu.CompilerParams(collective_id=collective_id, has_side_effects=True),
    )(block)
    return out[0, :width]


def ray_axes(mesh):
    rays = mesh.shape["ray"]
    inner = 4 if rays % 4 == 0 else rays
    return ((inner, 1), (rays // inner, inner))


def allreduce_kernel(axes, x_ref, o_ref, part, rbuf1, acc1, rbuf2, send_sems, recv_sems):
    me = lax.axis_index("ray")
    tile = lax.axis_index("tile")
    rows = x_ref.shape[0]
    half = x_ref.shape[1] // 2
    w1 = half // axes[0][0]
    w2 = w1 // axes[1][0]

    def pos(axis):
        size, stride = axis
        return (me // stride) % size

    def peer(axis, k):
        size, stride = axis
        p = pos(axis)
        return (me + (((p - k + size) % size) - p) * stride, tile)

    def cols(start, width):
        return pl.ds(pl.multiple_of(start, 128), width)

    def add_rows(dst, a, b):
        def body(r, carry):
            block = pl.ds(pl.multiple_of(r * 8, 8), 8)
            dst[block, :] = a[block, :] + b[block, :]
            return carry
        lax.fori_loop(0, rows // 8, body, 0)

    barrier = pltpu.get_barrier_semaphore()
    greeted = 0
    for axis in axes:
        for k in range(1, axis[0]):
            pl.semaphore_signal(barrier, inc=1, device_id=peer(axis, k), device_id_type=MESH)
            greeted += 1
    pl.semaphore_wait(barrier, greeted)

    plans = [(axes[0], axes[1]), (axes[1], axes[0])]
    sends = []

    def send(stage, h, d, s, axis, src, dst, landing):
        size = axis[0]
        k = size - 1 if d == 0 else 1
        sems = dict(send_sem=send_sems.at[stage, h, d, s], recv_sem=recv_sems.at[stage, h, d, s],
                    device_id=peer(axis, k), device_id_type=MESH)
        copy = pltpu.make_async_remote_copy(src_ref=src, dst_ref=dst, **sems)
        copy.start()
        sends.append(copy)
        return pltpu.make_async_remote_copy(src_ref=src, dst_ref=landing, **sems)

    def reduce_scatter(stage, segs, rbuf, acc):
        steps = segs[0][0][0] - 1
        for s in range(steps):
            waits = []
            for h, (axis, own, final) in enumerate(segs):
                size, p = axis[0], pos(axis)
                for d in range(2):
                    sign = 1 if d == 0 else -1
                    src = own((p - sign * (s + 1) + 2 * size) % size, d) if s == 0 else acc.at[h, d, s - 1]
                    waits.append((h, d, send(stage, h, d, s, axis, src, rbuf.at[h, d, s], rbuf.at[h, d, s])))
            for h, d, copy in waits:
                copy.wait_recv()
            for h, (axis, own, final) in enumerate(segs):
                size, p = axis[0], pos(axis)
                for d in range(2):
                    sign = 1 if d == 0 else -1
                    mine = own((p - sign * (s + 2) + 2 * size) % size, d)
                    dst = final(d) if s == steps - 1 else acc.at[h, d, s]
                    add_rows(dst, rbuf.at[h, d, s], mine)

    def all_gather(stage, segs):
        steps = segs[0][0][0] - 1
        for s in range(steps):
            waits = []
            for h, (axis, region) in enumerate(segs):
                size, p = axis[0], pos(axis)
                for d in range(2):
                    sign = 1 if d == 0 else -1
                    src = region((p - sign * s + 2 * size) % size, d)
                    landing = region((p - sign * (s + 1) + 2 * size) % size, d)
                    waits.append(send(stage, h, d, s, axis, src, src, landing))
            for copy in waits:
                copy.wait_recv()

    def direct_reduce_scatter(stage, segs, rbuf, width):
        waits = []
        for h, (axis, own, final) in enumerate(segs):
            size, p = axis[0], pos(axis)
            for k in range(1, size):
                slot = rbuf.at[h, k - 1]
                copy = pltpu.make_async_remote_copy(
                    src_ref=own((p - k + size) % size), dst_ref=slot,
                    send_sem=send_sems.at[stage, h, 0, k - 1], recv_sem=recv_sems.at[stage, h, 0, k - 1],
                    device_id=peer(axis, k), device_id_type=MESH)
                copy.start()
                sends.append(copy)
                waits.append(copy)
        for copy in waits:
            copy.wait_recv()
        for h, (axis, own, final) in enumerate(segs):
            size, p = axis[0], pos(axis)
            def body(r, carry, h=h, size=size, p=p, own=own, final=final):
                block = pl.ds(pl.multiple_of(r * 8, 8), 8)
                total = None
                for q in range(size):
                    k = (q - p + size) % size
                    mine = own(p)[block, :]
                    other = rbuf[h, jnp.maximum(k - 1, 0), block, :]
                    val = jnp.where(k == 0, mine, other)
                    total = val if total is None else total + val
                final[block, :] = total
                return carry
            lax.fori_loop(0, rows // 8, body, 0)

    def direct_all_gather(stage, segs):
        waits = []
        for h, (axis, region) in enumerate(segs):
            size, p = axis[0], pos(axis)
            for k in range(1, size):
                copy = pltpu.make_async_remote_copy(
                    src_ref=region(p), dst_ref=region(p),
                    send_sem=send_sems.at[stage, h, 0, k - 1], recv_sem=recv_sems.at[stage, h, 0, k - 1],
                    device_id=peer(axis, k), device_id_type=MESH)
                copy.start()
                sends.append(copy)
                waits.append(pltpu.make_async_remote_copy(
                    src_ref=region(p), dst_ref=region((p + k) % size),
                    send_sem=send_sems.at[stage, h, 0, k - 1], recv_sem=recv_sems.at[stage, h, 0, k - 1],
                    device_id=peer(axis, k), device_id_type=MESH))
        for copy in waits:
            copy.wait_recv()

    q1, q2 = w1 // 2, w2 // 2
    seg1, seg2, seg3, seg4 = [], [], [], []
    for h, (a1, a2) in enumerate(plans):
        p1, p2 = pos(a1), pos(a2)
        base = h * half + p1 * w1
        seg1.append((a1,
                     lambda j, d, h=h: x_ref.at[:, cols(h * half + j * w1 + d * q1, q1)],
                     lambda d, h=h: part.at[h, :, cols(d * q1, q1)]))
        seg2.append((a2,
                     lambda j, h=h: part.at[h, :, cols(j * w2, w2)],
                     o_ref.at[:, cols(base + p2 * w2, w2)]))
        seg3.append((a2, lambda j, base=base: o_ref.at[:, cols(base + j * w2, w2)]))
        seg4.append((a1, lambda j, d, h=h: o_ref.at[:, cols(h * half + j * w1 + d * q1, q1)]))
    reduce_scatter(0, seg1, rbuf1, acc1)
    direct_reduce_scatter(1, seg2, rbuf2, w2)
    direct_all_gather(2, seg3)
    all_gather(3, seg4)
    for copy in sends:
        copy.wait_send()


def ray_allreduce(mesh, owned):
    axes = ray_axes(mesh)
    rows, width = owned.shape
    half = width // 2
    w1 = half // axes[0][0]
    w2 = w1 // axes[1][0]
    steps = max(axes[0][0], axes[1][0]) - 1
    return pl.pallas_call(
        functools.partial(allreduce_kernel, axes),
        out_shape=jax.ShapeDtypeStruct((rows, width), jnp.float32),
        in_specs=[pl.BlockSpec(memory_space=pltpu.VMEM)],
        out_specs=pl.BlockSpec(memory_space=pltpu.VMEM),
        scratch_shapes=[
            pltpu.VMEM((2, rows, w1), jnp.float32),
            pltpu.VMEM((2, 2, steps, rows, w1 // 2), jnp.float32),
            pltpu.VMEM((2, 2, steps, rows, w1 // 2), jnp.float32),
            pltpu.VMEM((2, steps, rows, w2), jnp.float32),
            pltpu.SemaphoreType.DMA((4, 2, 2, steps)),
            pltpu.SemaphoreType.DMA((4, 2, 2, steps)),
        ],
        compiler_params=pltpu.CompilerParams(
            collective_id=2, has_side_effects=True, vmem_limit_bytes=60 * 1024 * 1024),
    )(owned)


eps_norm = 1e-06


def per_device(mesh, data, sensitivity, block_tiles, block_bundles):
    columns = data.shape[0]
    bundles = block_bundles.reshape(-1)
    requests = lax.all_to_all(block_tiles, "tile", split_axis=1, concat_axis=1, tiled=True).reshape(
        -1
    )
    bundle_onehot = (bundles[:, None] == jnp.arange(BUND_DEV, dtype=jnp.int32)[None, :]).astype(
        jnp.float32
    )
    owner_onehot = (requests[:, None] == jnp.arange(TILE_DEV, dtype=jnp.int32)[None, :]).astype(
        jnp.bfloat16
    )

    def fetch(field_bf):
        owned = field_bf.reshape(columns, TILE_DEV, CB)
        outgoing = jnp.take(owned, requests, axis=1)
        tiles = lax.all_to_all(outgoing, "tile", split_axis=1, concat_axis=1, tiled=True)
        return tiles

    def forward(field_bf):
        tiles = fetch(field_bf)
        partial_value = jnp.einsum(
            "cnk,nrk->ncr", tiles, sensitivity, preferred_element_type=jnp.float32
        )
        summed = jnp.einsum(
            "ncr,nb->cbr", partial_value, bundle_onehot, precision=lax.Precision.HIGHEST
        )
        return summed.reshape(columns, BUND_DEV * RB)

    def adjoint(rays_bf):
        picked = jnp.take(rays_bf.reshape(columns, BUND_DEV, RB), bundles, axis=1)
        terms = jnp.einsum(
            "cnr,nrk->cnk", picked, sensitivity, preferred_element_type=jnp.float32
        ).astype(jnp.bfloat16)
        arrived = lax.all_to_all(terms, "tile", split_axis=1, concat_axis=1, tiled=True)
        owned = jnp.einsum(
            "cnk,nt->ctk", arrived, owner_onehot, preferred_element_type=jnp.float32
        ).reshape(columns, TILE_DEV * CB)
        total = ray_allreduce(mesh, owned)
        return total

    def cell_norm(field):
        local = jnp.sum(field * field, axis=1)
        total = group_sum(mesh, ("tile",), 1, local)
        return jnp.sqrt(total + eps_norm)

    def ray_norm(rays):
        total = group_sum(mesh, ("ray", "tile"), 0, jnp.sum(rays * rays, axis=1))
        return jnp.sqrt(total + eps_norm)

    beta_now = ray_norm(data)
    rays_dir = data / beta_now[:, None]
    model_dir = adjoint(rays_dir.astype(jnp.bfloat16))
    alpha_now = cell_norm(model_dir)
    model_dir = model_dir / alpha_now[:, None]
    search = model_dir
    solution = jnp.zeros_like(model_dir)
    phi_bar = beta_now
    rho_bar = alpha_now
    for step in range(ITERS):
        rounded = model_dir.astype(jnp.bfloat16)
        rays_dir = forward(rounded) - alpha_now[:, None] * rays_dir
        beta_now = ray_norm(rays_dir)
        rays_dir = rays_dir / beta_now[:, None]
        rho_now = jnp.sqrt(rho_bar * rho_bar + beta_now * beta_now)
        cosine = rho_bar / rho_now
        sine_part = beta_now / rho_now
        phi_now = cosine * phi_bar
        phi_bar = sine_part * phi_bar
        solution = solution + (phi_now / rho_now)[:, None] * search
        if step + 1 < ITERS:
            model_dir = adjoint(rays_dir.astype(jnp.bfloat16)) - beta_now[:, None] * model_dir
            alpha_now = cell_norm(model_dir)
            model_dir = model_dir / alpha_now[:, None]
            theta_now = sine_part * alpha_now
            rho_bar = -cosine * alpha_now
            search = model_dir - (theta_now / rho_now)[:, None] * search
    residual = data - forward(solution.astype(jnp.bfloat16))
    return (solution, residual)


def solution(mesh):
    return jax.shard_map(
        functools.partial(per_device, mesh),
        mesh=mesh,
        in_specs=(
            P(None, ("ray", "tile")),
            P(("ray", "tile"), None, None),
            P(("ray", "tile"), None, None),
            P(("ray", "tile"), None, None),
        ),
        out_specs=(P(None, "tile"), P(None, ("ray", "tile"))),
        check_vma=False,
    )
```

```python
import jax
import jax.numpy as jnp
from jax import lax
from jax.sharding import PartitionSpec as P

RB = 256
CB = 512
ITERS = 2
BUND_DEV = 8
TILE_DEV = 48


import functools
from jax.experimental import pallas as pl
from jax.experimental.pallas import tpu as pltpu

MESH = pl.DeviceIdType.MESH


def stage_plan(mesh, axes):
    plan = [(axis, mesh.shape[axis], 1) for axis in ("tile", "ray") if axis in axes]
    return tuple(stage for stage in plan if stage[1] > 1)


def reduce_kernel(plan, x_ref, o_ref, vals, send_sems, recv_sems):
    here = {"ray": lax.axis_index("ray"), "tile": lax.axis_index("tile")}

    def peer(axis, size, stride, k):
        idx = here[axis]
        pos = (idx // stride) % size
        other = idx + (((pos + k) % size) - pos) * stride
        coords = dict(here)
        coords[axis] = other
        return (coords["ray"], coords["tile"])

    barrier = pltpu.get_barrier_semaphore()
    count = 0
    for axis, size, stride in plan:
        for k in range(1, size):
            pl.semaphore_signal(barrier, inc=1, device_id=peer(axis, size, stride, k), device_id_type=MESH)
            count += 1
    pl.semaphore_wait(barrier, count)

    vals[0, 0] = x_ref[...]
    copies = []
    for s, (axis, size, stride) in enumerate(plan):
        src = x_ref if s == 0 else vals.at[s, 0]
        stage_copies = []
        for k in range(1, size):
            copy = pltpu.make_async_remote_copy(
                src_ref=src,
                dst_ref=vals.at[s, k],
                send_sem=send_sems.at[s, k],
                recv_sem=recv_sems.at[s, k],
                device_id=peer(axis, size, stride, (size - k) % size),
                device_id_type=MESH,
            )
            copy.start()
            stage_copies.append(copy)
        for copy in stage_copies:
            copy.wait_recv()
        copies += stage_copies
        pos = (here[axis] // stride) % size
        total = vals[s, (size - pos) % size]
        for q in range(1, size):
            total = total + vals[s, (q - pos + size) % size]
        if s + 1 < len(plan):
            vals[s + 1, 0] = total
        else:
            o_ref[...] = total
    for copy in copies:
        copy.wait_send()


def group_sum(mesh, axes, collective_id, partial):
    plan = stage_plan(mesh, axes)
    width = partial.shape[0]
    block = jnp.zeros((8, 128), jnp.float32).at[0, :width].set(partial)
    depth = max(size for _, size, _ in plan)
    out = pl.pallas_call(
        functools.partial(reduce_kernel, plan),
        out_shape=jax.ShapeDtypeStruct((8, 128), jnp.float32),
        in_specs=[pl.BlockSpec(memory_space=pltpu.VMEM)],
        out_specs=pl.BlockSpec(memory_space=pltpu.VMEM),
        scratch_shapes=[
            pltpu.VMEM((len(plan), depth, 8, 128), jnp.float32),
            pltpu.SemaphoreType.DMA((len(plan), depth)),
            pltpu.SemaphoreType.DMA((len(plan), depth)),
        ],
        compiler_params=pltpu.CompilerParams(collective_id=collective_id, has_side_effects=True),
    )(block)
    return out[0, :width]


def ray_axes(mesh):
    rays = mesh.shape["ray"]
    inner = 4 if rays % 4 == 0 else rays
    return ((inner, 1), (rays // inner, inner))


def allreduce_kernel(axes, x_ref, o_ref, part, rbuf1, acc1, rbuf2, send_sems, recv_sems):
    me = lax.axis_index("ray")
    tile = lax.axis_index("tile")
    rows = x_ref.shape[0]
    half = x_ref.shape[1] // 2
    w1 = half // axes[0][0]
    w2 = w1 // axes[1][0]

    def pos(axis):
        size, stride = axis
        return (me // stride) % size

    def peer(axis, k):
        size, stride = axis
        p = pos(axis)
        return (me + (((p - k + size) % size) - p) * stride, tile)

    def cols(start, width):
        return pl.ds(pl.multiple_of(start, 128), width)

    def add_rows(dst, a, b):
        def body(r, carry):
            block = pl.ds(pl.multiple_of(r * 8, 8), 8)
            dst[block, :] = a[block, :] + b[block, :]
            return carry
        lax.fori_loop(0, rows // 8, body, 0)

    barrier = pltpu.get_barrier_semaphore()
    greeted = 0
    for axis in axes:
        for k in range(1, axis[0]):
            pl.semaphore_signal(barrier, inc=1, device_id=peer(axis, k), device_id_type=MESH)
            greeted += 1
    pl.semaphore_wait(barrier, greeted)

    plans = [(axes[0], axes[1]), (axes[1], axes[0])]
    sends = []

    def send(stage, h, d, s, axis, src, dst, landing):
        size = axis[0]
        k = size - 1 if d == 0 else 1
        sems = dict(send_sem=send_sems.at[stage, h, d, s], recv_sem=recv_sems.at[stage, h, d, s],
                    device_id=peer(axis, k), device_id_type=MESH)
        copy = pltpu.make_async_remote_copy(src_ref=src, dst_ref=dst, **sems)
        copy.start()
        sends.append(copy)
        return pltpu.make_async_remote_copy(src_ref=src, dst_ref=landing, **sems)

    def reduce_scatter(stage, segs, rbuf, acc):
        steps = segs[0][0][0] - 1
        for s in range(steps):
            waits = []
            for h, (axis, own, final) in enumerate(segs):
                size, p = axis[0], pos(axis)
                for d in range(2):
                    sign = 1 if d == 0 else -1
                    src = own((p - sign * (s + 1) + 2 * size) % size, d) if s == 0 else acc.at[h, d, s - 1]
                    waits.append((h, d, send(stage, h, d, s, axis, src, rbuf.at[h, d, s], rbuf.at[h, d, s])))
            for h, d, copy in waits:
                copy.wait_recv()
            for h, (axis, own, final) in enumerate(segs):
                size, p = axis[0], pos(axis)
                for d in range(2):
                    sign = 1 if d == 0 else -1
                    mine = own((p - sign * (s + 2) + 2 * size) % size, d)
                    dst = final(d) if s == steps - 1 else acc.at[h, d, s]
                    add_rows(dst, rbuf.at[h, d, s], mine)

    def all_gather(stage, segs):
        steps = segs[0][0][0] - 1
        for s in range(steps):
            waits = []
            for h, (axis, region) in enumerate(segs):
                size, p = axis[0], pos(axis)
                for d in range(2):
                    sign = 1 if d == 0 else -1
                    src = region((p - sign * s + 2 * size) % size, d)
                    landing = region((p - sign * (s + 1) + 2 * size) % size, d)
                    waits.append(send(stage, h, d, s, axis, src, src, landing))
            for copy in waits:
                copy.wait_recv()

    def direct_reduce_scatter(stage, segs, rbuf, width):
        waits = []
        for h, (axis, own, final) in enumerate(segs):
            size, p = axis[0], pos(axis)
            for k in range(1, size):
                slot = rbuf.at[h, k - 1]
                copy = pltpu.make_async_remote_copy(
                    src_ref=own((p - k + size) % size), dst_ref=slot,
                    send_sem=send_sems.at[stage, h, 0, k - 1], recv_sem=recv_sems.at[stage, h, 0, k - 1],
                    device_id=peer(axis, k), device_id_type=MESH)
                copy.start()
                sends.append(copy)
                waits.append(copy)
        for copy in waits:
            copy.wait_recv()
        for h, (axis, own, final) in enumerate(segs):
            size, p = axis[0], pos(axis)
            def body(r, carry, h=h, size=size, p=p, own=own, final=final):
                block = pl.ds(pl.multiple_of(r * 8, 8), 8)
                total = None
                for q in range(size):
                    k = (q - p + size) % size
                    mine = own(p)[block, :]
                    other = rbuf[h, jnp.maximum(k - 1, 0), block, :]
                    val = jnp.where(k == 0, mine, other)
                    total = val if total is None else total + val
                final[block, :] = total
                return carry
            lax.fori_loop(0, rows // 8, body, 0)

    def direct_all_gather(stage, segs):
        waits = []
        for h, (axis, region) in enumerate(segs):
            size, p = axis[0], pos(axis)
            for k in range(1, size):
                copy = pltpu.make_async_remote_copy(
                    src_ref=region(p), dst_ref=region(p),
                    send_sem=send_sems.at[stage, h, 0, k - 1], recv_sem=recv_sems.at[stage, h, 0, k - 1],
                    device_id=peer(axis, k), device_id_type=MESH)
                copy.start()
                sends.append(copy)
                waits.append(pltpu.make_async_remote_copy(
                    src_ref=region(p), dst_ref=region((p + k) % size),
                    send_sem=send_sems.at[stage, h, 0, k - 1], recv_sem=recv_sems.at[stage, h, 0, k - 1],
                    device_id=peer(axis, k), device_id_type=MESH))
        for copy in waits:
            copy.wait_recv()

    q1, q2 = w1 // 2, w2 // 2
    seg1, seg2, seg3, seg4 = [], [], [], []
    for h, (a1, a2) in enumerate(plans):
        p1, p2 = pos(a1), pos(a2)
        base = h * half + p1 * w1
        seg1.append((a1,
                     lambda j, d, h=h: x_ref.at[:, cols(h * half + j * w1 + d * q1, q1)],
                     lambda d, h=h: part.at[h, :, cols(d * q1, q1)]))
        seg2.append((a2,
                     lambda j, h=h: part.at[h, :, cols(j * w2, w2)],
                     o_ref.at[:, cols(base + p2 * w2, w2)]))
        seg3.append((a2, lambda j, base=base: o_ref.at[:, cols(base + j * w2, w2)]))
        seg4.append((a1, lambda j, h=h: o_ref.at[:, cols(h * half + j * w1, w1)]))
    reduce_scatter(0, seg1, rbuf1, acc1)
    direct_reduce_scatter(1, seg2, rbuf2, w2)
    direct_all_gather(2, seg3)
    direct_all_gather(3, seg4)
    for copy in sends:
        copy.wait_send()


def ray_allreduce(mesh, owned):
    axes = ray_axes(mesh)
    rows, width = owned.shape
    half = width // 2
    w1 = half // axes[0][0]
    w2 = w1 // axes[1][0]
    steps = max(axes[0][0], axes[1][0]) - 1
    return pl.pallas_call(
        functools.partial(allreduce_kernel, axes),
        out_shape=jax.ShapeDtypeStruct((rows, width), jnp.float32),
        in_specs=[pl.BlockSpec(memory_space=pltpu.VMEM)],
        out_specs=pl.BlockSpec(memory_space=pltpu.VMEM),
        scratch_shapes=[
            pltpu.VMEM((2, rows, w1), jnp.float32),
            pltpu.VMEM((2, 2, steps, rows, w1 // 2), jnp.float32),
            pltpu.VMEM((2, 2, steps, rows, w1 // 2), jnp.float32),
            pltpu.VMEM((2, steps, rows, w2), jnp.float32),
            pltpu.SemaphoreType.DMA((4, 2, 2, steps)),
            pltpu.SemaphoreType.DMA((4, 2, 2, steps)),
        ],
        compiler_params=pltpu.CompilerParams(
            collective_id=2, has_side_effects=True, vmem_limit_bytes=60 * 1024 * 1024),
    )(owned)


eps_norm = 1e-06


def per_device(mesh, data, sensitivity, block_tiles, block_bundles):
    columns = data.shape[0]
    bundles = block_bundles.reshape(-1)
    requests = lax.all_to_all(block_tiles, "tile", split_axis=1, concat_axis=1, tiled=True).reshape(
        -1
    )
    bundle_onehot = (bundles[:, None] == jnp.arange(BUND_DEV, dtype=jnp.int32)[None, :]).astype(
        jnp.float32
    )
    owner_onehot = (requests[:, None] == jnp.arange(TILE_DEV, dtype=jnp.int32)[None, :]).astype(
        jnp.bfloat16
    )

    def fetch(field_bf):
        owned = field_bf.reshape(columns, TILE_DEV, CB)
        outgoing = jnp.take(owned, requests, axis=1)
        tiles = lax.all_to_all(outgoing, "tile", split_axis=1, concat_axis=1, tiled=True)
        return tiles

    def forward(field_bf):
        tiles = fetch(field_bf)
        partial_value = jnp.einsum(
            "cnk,nrk->ncr", tiles, sensitivity, preferred_element_type=jnp.float32
        )
        summed = jnp.einsum(
            "ncr,nb->cbr", partial_value, bundle_onehot, precision=lax.Precision.HIGHEST
        )
        return summed.reshape(columns, BUND_DEV * RB)

    def adjoint(rays_bf):
        picked = jnp.take(rays_bf.reshape(columns, BUND_DEV, RB), bundles, axis=1)
        terms = jnp.einsum(
            "cnr,nrk->cnk", picked, sensitivity, preferred_element_type=jnp.float32
        ).astype(jnp.bfloat16)
        arrived = lax.all_to_all(terms, "tile", split_axis=1, concat_axis=1, tiled=True)
        owned = jnp.einsum(
            "cnk,nt->ctk", arrived, owner_onehot, preferred_element_type=jnp.float32
        ).reshape(columns, TILE_DEV * CB)
        total = ray_allreduce(mesh, owned)
        return total

    def cell_norm(field):
        local = jnp.sum(field * field, axis=1)
        total = group_sum(mesh, ("tile",), 1, local)
        return jnp.sqrt(total + eps_norm)

    def ray_norm(rays):
        total = group_sum(mesh, ("ray", "tile"), 0, jnp.sum(rays * rays, axis=1))
        return jnp.sqrt(total + eps_norm)

    beta_now = ray_norm(data)
    rays_dir = data / beta_now[:, None]
    model_dir = adjoint(rays_dir.astype(jnp.bfloat16))
    alpha_now = cell_norm(model_dir)
    model_dir = model_dir / alpha_now[:, None]
    search = model_dir
    solution = jnp.zeros_like(model_dir)
    phi_bar = beta_now
    rho_bar = alpha_now
    for step in range(ITERS):
        rounded = model_dir.astype(jnp.bfloat16)
        rays_dir = forward(rounded) - alpha_now[:, None] * rays_dir
        beta_now = ray_norm(rays_dir)
        rays_dir = rays_dir / beta_now[:, None]
        rho_now = jnp.sqrt(rho_bar * rho_bar + beta_now * beta_now)
        cosine = rho_bar / rho_now
        sine_part = beta_now / rho_now
        phi_now = cosine * phi_bar
        phi_bar = sine_part * phi_bar
        solution = solution + (phi_now / rho_now)[:, None] * search
        if step + 1 < ITERS:
            model_dir = adjoint(rays_dir.astype(jnp.bfloat16)) - beta_now[:, None] * model_dir
            alpha_now = cell_norm(model_dir)
            model_dir = model_dir / alpha_now[:, None]
            theta_now = sine_part * alpha_now
            rho_bar = -cosine * alpha_now
            search = model_dir - (theta_now / rho_now)[:, None] * search
    residual = data - forward(solution.astype(jnp.bfloat16))
    return (solution, residual)


def solution(mesh):
    return jax.shard_map(
        functools.partial(per_device, mesh),
        mesh=mesh,
        in_specs=(
            P(None, ("ray", "tile")),
            P(("ray", "tile"), None, None),
            P(("ray", "tile"), None, None),
            P(("ray", "tile"), None, None),
        ),
        out_specs=(P(None, "tile"), P(None, ("ray", "tile"))),
        check_vma=False,
    )
```

```python
import jax
import jax.numpy as jnp
from jax import lax
from jax.sharding import PartitionSpec as P

RB = 256
CB = 512
ITERS = 2
BUND_DEV = 8
TILE_DEV = 48


import functools
from jax.experimental import pallas as pl
from jax.experimental.pallas import tpu as pltpu

MESH = pl.DeviceIdType.MESH


def stage_plan(mesh, axes):
    plan = [(axis, mesh.shape[axis], 1) for axis in ("tile", "ray") if axis in axes]
    return tuple(stage for stage in plan if stage[1] > 1)


def reduce_kernel(plan, x_ref, o_ref, vals, send_sems, recv_sems):
    here = {"ray": lax.axis_index("ray"), "tile": lax.axis_index("tile")}

    def peer(axis, size, stride, k):
        idx = here[axis]
        pos = (idx // stride) % size
        other = idx + (((pos + k) % size) - pos) * stride
        coords = dict(here)
        coords[axis] = other
        return (coords["ray"], coords["tile"])

    barrier = pltpu.get_barrier_semaphore()
    count = 0
    for axis, size, stride in plan:
        for k in range(1, size):
            pl.semaphore_signal(barrier, inc=1, device_id=peer(axis, size, stride, k), device_id_type=MESH)
            count += 1
    pl.semaphore_wait(barrier, count)

    vals[0, 0] = x_ref[...]
    copies = []
    for s, (axis, size, stride) in enumerate(plan):
        src = x_ref if s == 0 else vals.at[s, 0]
        stage_copies = []
        for k in range(1, size):
            copy = pltpu.make_async_remote_copy(
                src_ref=src,
                dst_ref=vals.at[s, k],
                send_sem=send_sems.at[s, k],
                recv_sem=recv_sems.at[s, k],
                device_id=peer(axis, size, stride, (size - k) % size),
                device_id_type=MESH,
            )
            copy.start()
            stage_copies.append(copy)
        for copy in stage_copies:
            copy.wait_recv()
        copies += stage_copies
        pos = (here[axis] // stride) % size
        total = vals[s, (size - pos) % size]
        for q in range(1, size):
            total = total + vals[s, (q - pos + size) % size]
        if s + 1 < len(plan):
            vals[s + 1, 0] = total
        else:
            o_ref[...] = total
    for copy in copies:
        copy.wait_send()


def group_sum(mesh, axes, collective_id, partial):
    plan = stage_plan(mesh, axes)
    width = partial.shape[0]
    block = jnp.zeros((8, 128), jnp.float32).at[0, :width].set(partial)
    depth = max(size for _, size, _ in plan)
    out = pl.pallas_call(
        functools.partial(reduce_kernel, plan),
        out_shape=jax.ShapeDtypeStruct((8, 128), jnp.float32),
        in_specs=[pl.BlockSpec(memory_space=pltpu.VMEM)],
        out_specs=pl.BlockSpec(memory_space=pltpu.VMEM),
        scratch_shapes=[
            pltpu.VMEM((len(plan), depth, 8, 128), jnp.float32),
            pltpu.SemaphoreType.DMA((len(plan), depth)),
            pltpu.SemaphoreType.DMA((len(plan), depth)),
        ],
        compiler_params=pltpu.CompilerParams(collective_id=collective_id, has_side_effects=True),
    )(block)
    return out[0, :width]


def ray_axes(mesh):
    rays = mesh.shape["ray"]
    inner = 4 if rays % 4 == 0 else rays
    return ((inner, 1), (rays // inner, inner))


def allreduce_kernel(axes, x_ref, o_ref, part, rbuf1, acc1, rbuf2, send_sems, recv_sems):
    me = lax.axis_index("ray")
    tile = lax.axis_index("tile")
    rows = x_ref.shape[0]
    half = x_ref.shape[1] // 2
    w1 = half // axes[0][0]
    w2 = w1 // axes[1][0]

    def pos(axis):
        size, stride = axis
        return (me // stride) % size

    def peer(axis, k):
        size, stride = axis
        p = pos(axis)
        return (me + (((p - k + size) % size) - p) * stride, tile)

    def cols(start, width):
        return pl.ds(pl.multiple_of(start, 128), width)

    def add_rows(dst, a, b):
        def body(r, carry):
            block = pl.ds(pl.multiple_of(r * 8, 8), 8)
            dst[block, :] = a[block, :] + b[block, :]
            return carry
        lax.fori_loop(0, rows // 8, body, 0)

    barrier = pltpu.get_barrier_semaphore()
    greeted = 0
    for axis in axes:
        for k in range(1, axis[0]):
            pl.semaphore_signal(barrier, inc=1, device_id=peer(axis, k), device_id_type=MESH)
            greeted += 1
    pl.semaphore_wait(barrier, greeted)

    plans = [(axes[0], axes[1]), (axes[1], axes[0])]
    sends = []

    pieces = 4

    def send(stage, h, d, s, axis, src, dst, landing):
        size = axis[0]
        k = size - 1 if d % 2 == 0 else 1
        sems = dict(send_sem=send_sems.at[stage, h, d, s], recv_sem=recv_sems.at[stage, h, d, s],
                    device_id=peer(axis, k), device_id_type=MESH)
        copy = pltpu.make_async_remote_copy(src_ref=src, dst_ref=dst, **sems)
        copy.start()
        sends.append(copy)
        return pltpu.make_async_remote_copy(src_ref=src, dst_ref=landing, **sems)

    order = [(h, d) for d in range(pieces) for h in range(2)]

    def reduce_scatter(stage, segs, rbuf, acc):
        steps = segs[0][0][0] - 1

        def start(h, d, s):
            axis, own, final = segs[h]
            size, p = axis[0], pos(axis)
            sign = 1 if d % 2 == 0 else -1
            src = own((p - sign * (s + 1) + 2 * size) % size, d) if s == 0 else acc.at[h, d, s - 1]
            return send(stage, h, d, s, axis, src, rbuf.at[h, d, s], rbuf.at[h, d, s])

        pending = {hd: start(*hd, 0) for hd in order}
        for s in range(steps):
            for h, d in order:
                axis, own, final = segs[h]
                size, p = axis[0], pos(axis)
                sign = 1 if d % 2 == 0 else -1
                pending[(h, d)].wait_recv()
                mine = own((p - sign * (s + 2) + 2 * size) % size, d)
                dst = final(d) if s == steps - 1 else acc.at[h, d, s]
                add_rows(dst, rbuf.at[h, d, s], mine)
                if s + 1 < steps:
                    pending[(h, d)] = start(h, d, s + 1)

    def all_gather(stage, segs):
        steps = segs[0][0][0] - 1

        def start(h, d, s):
            axis, region = segs[h]
            size, p = axis[0], pos(axis)
            sign = 1 if d % 2 == 0 else -1
            src = region((p - sign * s + 2 * size) % size, d)
            landing = region((p - sign * (s + 1) + 2 * size) % size, d)
            return send(stage, h, d, s, axis, src, src, landing)

        pending = {hd: start(*hd, 0) for hd in order}
        for s in range(steps):
            for h, d in order:
                pending[(h, d)].wait_recv()
                if s + 1 < steps:
                    pending[(h, d)] = start(h, d, s + 1)

    def direct_reduce_scatter(stage, segs, rbuf, width):
        waits = []
        for h, (axis, own, final) in enumerate(segs):
            size, p = axis[0], pos(axis)
            for k in range(1, size):
                slot = rbuf.at[h, k - 1]
                copy = pltpu.make_async_remote_copy(
                    src_ref=own((p - k + size) % size), dst_ref=slot,
                    send_sem=send_sems.at[stage, h, 0, k - 1], recv_sem=recv_sems.at[stage, h, 0, k - 1],
                    device_id=peer(axis, k), device_id_type=MESH)
                copy.start()
                sends.append(copy)
                waits.append(copy)
        for copy in waits:
            copy.wait_recv()
        for h, (axis, own, final) in enumerate(segs):
            size, p = axis[0], pos(axis)
            def body(r, carry, h=h, size=size, p=p, own=own, final=final):
                block = pl.ds(pl.multiple_of(r * 8, 8), 8)
                total = None
                for q in range(size):
                    k = (q - p + size) % size
                    mine = own(p)[block, :]
                    other = rbuf[h, jnp.maximum(k - 1, 0), block, :]
                    val = jnp.where(k == 0, mine, other)
                    total = val if total is None else total + val
                final[block, :] = total
                return carry
            lax.fori_loop(0, rows // 8, body, 0)

    def direct_all_gather(stage, segs):
        waits = []
        for h, (axis, region) in enumerate(segs):
            size, p = axis[0], pos(axis)
            for k in range(1, size):
                copy = pltpu.make_async_remote_copy(
                    src_ref=region(p), dst_ref=region(p),
                    send_sem=send_sems.at[stage, h, 0, k - 1], recv_sem=recv_sems.at[stage, h, 0, k - 1],
                    device_id=peer(axis, k), device_id_type=MESH)
                copy.start()
                sends.append(copy)
                waits.append(pltpu.make_async_remote_copy(
                    src_ref=region(p), dst_ref=region((p + k) % size),
                    send_sem=send_sems.at[stage, h, 0, k - 1], recv_sem=recv_sems.at[stage, h, 0, k - 1],
                    device_id=peer(axis, k), device_id_type=MESH))
        for copy in waits:
            copy.wait_recv()

    q1, q2 = w1 // pieces, w2 // 2
    seg1, seg2, seg3, seg4 = [], [], [], []
    for h, (a1, a2) in enumerate(plans):
        p1, p2 = pos(a1), pos(a2)
        base = h * half + p1 * w1
        seg1.append((a1,
                     lambda j, d, h=h: x_ref.at[:, cols(h * half + j * w1 + d * q1, q1)],
                     lambda d, h=h: part.at[h, :, cols(d * q1, q1)]))
        seg2.append((a2,
                     lambda j, h=h: part.at[h, :, cols(j * w2, w2)],
                     o_ref.at[:, cols(base + p2 * w2, w2)]))
        seg3.append((a2, lambda j, base=base: o_ref.at[:, cols(base + j * w2, w2)]))
        seg4.append((a1, lambda j, d, h=h: o_ref.at[:, cols(h * half + j * w1 + d * q1, q1)]))
    reduce_scatter(0, seg1, rbuf1, acc1)
    direct_reduce_scatter(1, seg2, rbuf2, w2)
    direct_all_gather(2, seg3)
    all_gather(3, seg4)
    for copy in sends:
        copy.wait_send()


def ray_allreduce(mesh, owned):
    axes = ray_axes(mesh)
    rows, width = owned.shape
    half = width // 2
    w1 = half // axes[0][0]
    w2 = w1 // axes[1][0]
    steps = max(axes[0][0], axes[1][0]) - 1
    return pl.pallas_call(
        functools.partial(allreduce_kernel, axes),
        out_shape=jax.ShapeDtypeStruct((rows, width), jnp.float32),
        in_specs=[pl.BlockSpec(memory_space=pltpu.VMEM)],
        out_specs=pl.BlockSpec(memory_space=pltpu.VMEM),
        scratch_shapes=[
            pltpu.VMEM((2, rows, w1), jnp.float32),
            pltpu.VMEM((2, 4, steps, rows, w1 // 4), jnp.float32),
            pltpu.VMEM((2, 4, steps, rows, w1 // 4), jnp.float32),
            pltpu.VMEM((2, steps, rows, w2), jnp.float32),
            pltpu.SemaphoreType.DMA((4, 2, 4, steps)),
            pltpu.SemaphoreType.DMA((4, 2, 4, steps)),
        ],
        compiler_params=pltpu.CompilerParams(
            collective_id=2, has_side_effects=True, vmem_limit_bytes=60 * 1024 * 1024),
    )(owned)


eps_norm = 1e-06


def per_device(mesh, data, sensitivity, block_tiles, block_bundles):
    columns = data.shape[0]
    bundles = block_bundles.reshape(-1)
    requests = lax.all_to_all(block_tiles, "tile", split_axis=1, concat_axis=1, tiled=True).reshape(
        -1
    )
    bundle_onehot = (bundles[:, None] == jnp.arange(BUND_DEV, dtype=jnp.int32)[None, :]).astype(
        jnp.float32
    )
    owner_onehot = (requests[:, None] == jnp.arange(TILE_DEV, dtype=jnp.int32)[None, :]).astype(
        jnp.bfloat16
    )

    def fetch(field_bf):
        owned = field_bf.reshape(columns, TILE_DEV, CB)
        outgoing = jnp.take(owned, requests, axis=1)
        tiles = lax.all_to_all(outgoing, "tile", split_axis=1, concat_axis=1, tiled=True)
        return tiles

    def forward(field_bf):
        tiles = fetch(field_bf)
        partial_value = jnp.einsum(
            "cnk,nrk->ncr", tiles, sensitivity, preferred_element_type=jnp.float32
        )
        summed = jnp.einsum(
            "ncr,nb->cbr", partial_value, bundle_onehot, precision=lax.Precision.HIGHEST
        )
        return summed.reshape(columns, BUND_DEV * RB)

    def adjoint(rays_bf):
        picked = jnp.take(rays_bf.reshape(columns, BUND_DEV, RB), bundles, axis=1)
        terms = jnp.einsum(
            "cnr,nrk->cnk", picked, sensitivity, preferred_element_type=jnp.float32
        ).astype(jnp.bfloat16)
        arrived = lax.all_to_all(terms, "tile", split_axis=1, concat_axis=1, tiled=True)
        owned = jnp.einsum(
            "cnk,nt->ctk", arrived, owner_onehot, preferred_element_type=jnp.float32
        ).reshape(columns, TILE_DEV * CB)
        total = ray_allreduce(mesh, owned)
        return total

    def cell_norm(field):
        local = jnp.sum(field * field, axis=1)
        total = group_sum(mesh, ("tile",), 1, local)
        return jnp.sqrt(total + eps_norm)

    def ray_norm(rays):
        total = group_sum(mesh, ("ray", "tile"), 0, jnp.sum(rays * rays, axis=1))
        return jnp.sqrt(total + eps_norm)

    beta_now = ray_norm(data)
    rays_dir = data / beta_now[:, None]
    model_dir = adjoint(rays_dir.astype(jnp.bfloat16))
    alpha_now = cell_norm(model_dir)
    model_dir = model_dir / alpha_now[:, None]
    search = model_dir
    solution = jnp.zeros_like(model_dir)
    phi_bar = beta_now
    rho_bar = alpha_now
    for step in range(ITERS):
        rounded = model_dir.astype(jnp.bfloat16)
        rays_dir = forward(rounded) - alpha_now[:, None] * rays_dir
        beta_now = ray_norm(rays_dir)
        rays_dir = rays_dir / beta_now[:, None]
        rho_now = jnp.sqrt(rho_bar * rho_bar + beta_now * beta_now)
        cosine = rho_bar / rho_now
        sine_part = beta_now / rho_now
        phi_now = cosine * phi_bar
        phi_bar = sine_part * phi_bar
        solution = solution + (phi_now / rho_now)[:, None] * search
        if step + 1 < ITERS:
            model_dir = adjoint(rays_dir.astype(jnp.bfloat16)) - beta_now[:, None] * model_dir
            alpha_now = cell_norm(model_dir)
            model_dir = model_dir / alpha_now[:, None]
            theta_now = sine_part * alpha_now
            rho_bar = -cosine * alpha_now
            search = model_dir - (theta_now / rho_now)[:, None] * search
    residual = data - forward(solution.astype(jnp.bfloat16))
    return (solution, residual)


def solution(mesh):
    return jax.shard_map(
        functools.partial(per_device, mesh),
        mesh=mesh,
        in_specs=(
            P(None, ("ray", "tile")),
            P(("ray", "tile"), None, None),
            P(("ray", "tile"), None, None),
            P(("ray", "tile"), None, None),
        ),
        out_specs=(P(None, "tile"), P(None, ("ray", "tile"))),
        check_vma=False,
    )
```

```python
import jax
import jax.numpy as jnp
from jax import lax
from jax.sharding import PartitionSpec as P

RB = 256
CB = 512
ITERS = 2
BUND_DEV = 8
TILE_DEV = 48


import functools
from jax.experimental import pallas as pl
from jax.experimental.pallas import tpu as pltpu

MESH = pl.DeviceIdType.MESH


def stage_plan(mesh, axes):
    plan = [(axis, mesh.shape[axis], 1) for axis in ("tile", "ray") if axis in axes]
    return tuple(stage for stage in plan if stage[1] > 1)


def reduce_kernel(plan, x_ref, o_ref, vals, send_sems, recv_sems):
    here = {"ray": lax.axis_index("ray"), "tile": lax.axis_index("tile")}

    def peer(axis, size, stride, k):
        idx = here[axis]
        pos = (idx // stride) % size
        other = idx + (((pos + k) % size) - pos) * stride
        coords = dict(here)
        coords[axis] = other
        return (coords["ray"], coords["tile"])

    barrier = pltpu.get_barrier_semaphore()
    count = 0
    for axis, size, stride in plan:
        for k in range(1, size):
            pl.semaphore_signal(barrier, inc=1, device_id=peer(axis, size, stride, k), device_id_type=MESH)
            count += 1
    pl.semaphore_wait(barrier, count)

    vals[0, 0] = x_ref[...]
    copies = []
    for s, (axis, size, stride) in enumerate(plan):
        src = x_ref if s == 0 else vals.at[s, 0]
        stage_copies = []
        for k in range(1, size):
            copy = pltpu.make_async_remote_copy(
                src_ref=src,
                dst_ref=vals.at[s, k],
                send_sem=send_sems.at[s, k],
                recv_sem=recv_sems.at[s, k],
                device_id=peer(axis, size, stride, (size - k) % size),
                device_id_type=MESH,
            )
            copy.start()
            stage_copies.append(copy)
        for copy in stage_copies:
            copy.wait_recv()
        copies += stage_copies
        pos = (here[axis] // stride) % size
        total = vals[s, (size - pos) % size]
        for q in range(1, size):
            total = total + vals[s, (q - pos + size) % size]
        if s + 1 < len(plan):
            vals[s + 1, 0] = total
        else:
            o_ref[...] = total
    for copy in copies:
        copy.wait_send()


def group_sum(mesh, axes, collective_id, partial):
    plan = stage_plan(mesh, axes)
    width = partial.shape[0]
    block = jnp.zeros((8, 128), jnp.float32).at[0, :width].set(partial)
    depth = max(size for _, size, _ in plan)
    out = pl.pallas_call(
        functools.partial(reduce_kernel, plan),
        out_shape=jax.ShapeDtypeStruct((8, 128), jnp.float32),
        in_specs=[pl.BlockSpec(memory_space=pltpu.VMEM)],
        out_specs=pl.BlockSpec(memory_space=pltpu.VMEM),
        scratch_shapes=[
            pltpu.VMEM((len(plan), depth, 8, 128), jnp.float32),
            pltpu.SemaphoreType.DMA((len(plan), depth)),
            pltpu.SemaphoreType.DMA((len(plan), depth)),
        ],
        compiler_params=pltpu.CompilerParams(collective_id=collective_id, has_side_effects=True),
    )(block)
    return out[0, :width]


def ray_axes(mesh):
    rays = mesh.shape["ray"]
    inner = 4 if rays % 4 == 0 else rays
    return ((inner, 1), (rays // inner, inner))


def allreduce_kernel(axes, tiles, has_prev, *refs):
    if has_prev:
        x_ref, prev_ref, scale_ref, o_ref, ss_ref = refs[:5]
    else:
        x_ref, o_ref, ss_ref = refs[:3]
    part, rbuf1, acc1, rbuf2, tbuf, send_sems, recv_sems, tsend, trecv = refs[-9:]
    me = lax.axis_index("ray")
    tile = lax.axis_index("tile")
    rows = x_ref.shape[0]
    half = x_ref.shape[1] // 2
    w1 = half // axes[0][0]
    w2 = w1 // axes[1][0]

    def pos(axis):
        size, stride = axis
        return (me // stride) % size

    def peer(axis, k):
        size, stride = axis
        p = pos(axis)
        return (me + (((p - k + size) % size) - p) * stride, tile)

    def cols(start, width):
        return pl.ds(pl.multiple_of(start, 128), width)

    def add_rows(dst, a, b):
        def body(r, carry):
            block = pl.ds(pl.multiple_of(r * 8, 8), 8)
            dst[block, :] = a[block, :] + b[block, :]
            return carry
        lax.fori_loop(0, rows // 8, body, 0)

    barrier = pltpu.get_barrier_semaphore()
    greeted = 0
    for axis in axes:
        for k in range(1, axis[0]):
            pl.semaphore_signal(barrier, inc=1, device_id=peer(axis, k), device_id_type=MESH)
            greeted += 1
    for k in range(1, tiles):
        pl.semaphore_signal(barrier, inc=1, device_id=(me, (tile - k + tiles) % tiles), device_id_type=MESH)
        greeted += 1
    pl.semaphore_wait(barrier, greeted)

    plans = [(axes[0], axes[1]), (axes[1], axes[0])]
    sends = []

    def send(stage, h, d, s, axis, src, dst, landing):
        size = axis[0]
        k = size - 1 if d == 0 else 1
        sems = dict(send_sem=send_sems.at[stage, h, d, s], recv_sem=recv_sems.at[stage, h, d, s],
                    device_id=peer(axis, k), device_id_type=MESH)
        copy = pltpu.make_async_remote_copy(src_ref=src, dst_ref=dst, **sems)
        copy.start()
        sends.append(copy)
        return pltpu.make_async_remote_copy(src_ref=src, dst_ref=landing, **sems)

    def reduce_scatter(stage, segs, rbuf, acc):
        steps = segs[0][0][0] - 1
        for s in range(steps):
            waits = []
            for h, (axis, own, final) in enumerate(segs):
                size, p = axis[0], pos(axis)
                for d in range(2):
                    sign = 1 if d == 0 else -1
                    src = own((p - sign * (s + 1) + 2 * size) % size, d) if s == 0 else acc.at[h, d, s - 1]
                    waits.append((h, d, send(stage, h, d, s, axis, src, rbuf.at[h, d, s], rbuf.at[h, d, s])))
            for h, d, copy in waits:
                copy.wait_recv()
            for h, (axis, own, final) in enumerate(segs):
                size, p = axis[0], pos(axis)
                for d in range(2):
                    sign = 1 if d == 0 else -1
                    mine = own((p - sign * (s + 2) + 2 * size) % size, d)
                    dst = final(d) if s == steps - 1 else acc.at[h, d, s]
                    add_rows(dst, rbuf.at[h, d, s], mine)

    def all_gather(stage, segs):
        steps = segs[0][0][0] - 1
        for s in range(steps):
            waits = []
            for h, (axis, region) in enumerate(segs):
                size, p = axis[0], pos(axis)
                for d in range(2):
                    sign = 1 if d == 0 else -1
                    src = region((p - sign * s + 2 * size) % size, d)
                    landing = region((p - sign * (s + 1) + 2 * size) % size, d)
                    waits.append(send(stage, h, d, s, axis, src, src, landing))
            for copy in waits:
                copy.wait_recv()

    def direct_reduce_scatter(stage, segs, rbuf, width):
        waits = []
        for h, (axis, own, final) in enumerate(segs):
            size, p = axis[0], pos(axis)
            for k in range(1, size):
                slot = rbuf.at[h, k - 1]
                copy = pltpu.make_async_remote_copy(
                    src_ref=own((p - k + size) % size), dst_ref=slot,
                    send_sem=send_sems.at[stage, h, 0, k - 1], recv_sem=recv_sems.at[stage, h, 0, k - 1],
                    device_id=peer(axis, k), device_id_type=MESH)
                copy.start()
                sends.append(copy)
                waits.append(copy)
        for copy in waits:
            copy.wait_recv()
        for h, (axis, own, final) in enumerate(segs):
            size, p = axis[0], pos(axis)
            def body(r, carry, h=h, size=size, p=p, own=own, final=final):
                block = pl.ds(pl.multiple_of(r * 8, 8), 8)
                total = None
                for q in range(size):
                    k = (q - p + size) % size
                    mine = own(p)[block, :]
                    other = rbuf[h, jnp.maximum(k - 1, 0), block, :]
                    val = jnp.where(k == 0, mine, other)
                    total = val if total is None else total + val
                final[block, :] = total
                return carry
            lax.fori_loop(0, rows // 8, body, 0)

    def direct_all_gather(stage, segs):
        waits = []
        for h, (axis, region) in enumerate(segs):
            size, p = axis[0], pos(axis)
            for k in range(1, size):
                copy = pltpu.make_async_remote_copy(
                    src_ref=region(p), dst_ref=region(p),
                    send_sem=send_sems.at[stage, h, 0, k - 1], recv_sem=recv_sems.at[stage, h, 0, k - 1],
                    device_id=peer(axis, k), device_id_type=MESH)
                copy.start()
                sends.append(copy)
                waits.append(pltpu.make_async_remote_copy(
                    src_ref=region(p), dst_ref=region((p + k) % size),
                    send_sem=send_sems.at[stage, h, 0, k - 1], recv_sem=recv_sems.at[stage, h, 0, k - 1],
                    device_id=peer(axis, k), device_id_type=MESH))
        for copy in waits:
            copy.wait_recv()

    q1, q2 = w1 // 2, w2 // 2
    seg1, seg2, seg3, seg4 = [], [], [], []
    for h, (a1, a2) in enumerate(plans):
        p1, p2 = pos(a1), pos(a2)
        base = h * half + p1 * w1
        seg1.append((a1,
                     lambda j, d, h=h: x_ref.at[:, cols(h * half + j * w1 + d * q1, q1)],
                     lambda d, h=h: part.at[h, :, cols(d * q1, q1)]))
        seg2.append((a2,
                     lambda j, h=h: part.at[h, :, cols(j * w2, w2)],
                     o_ref.at[:, cols(base + p2 * w2, w2)]))
        seg3.append((a2, lambda j, base=base: o_ref.at[:, cols(base + j * w2, w2)]))
        seg4.append((a1, lambda j, d, h=h: o_ref.at[:, cols(h * half + j * w1 + d * q1, q1)]))
    reduce_scatter(0, seg1, rbuf1, acc1)
    direct_reduce_scatter(1, seg2, rbuf2, w2)
    direct_all_gather(2, seg3)
    all_gather(3, seg4)
    for copy in sends:
        copy.wait_send()

    width = o_ref.shape[1]
    span = 2048

    def rows_body(r, carry):
        block = pl.ds(pl.multiple_of(r * 8, 8), 8)

        def cols_body(c, acc):
            cs = pl.ds(pl.multiple_of(c * span, span), span)
            v = o_ref[block, cs]
            if has_prev:
                v = v - scale_ref[block, 0:1] * prev_ref[block, cs]
                o_ref[block, cs] = v
            sq = v * v
            for i in range(span // 128):
                acc = acc + sq[:, i * 128:(i + 1) * 128]
            return acc
        acc = lax.fori_loop(0, width // span, cols_body, jnp.zeros((8, 128), jnp.float32))
        tbuf[0, block, :] = jnp.broadcast_to(jnp.sum(acc, axis=1, keepdims=True), (8, 128))
        return carry
    lax.fori_loop(0, rows // 8, rows_body, 0)

    copies = []
    for k in range(1, tiles):
        copy = pltpu.make_async_remote_copy(
            src_ref=tbuf.at[0], dst_ref=tbuf.at[k], send_sem=tsend.at[k], recv_sem=trecv.at[k],
            device_id=(me, (tile - k + tiles) % tiles), device_id_type=MESH)
        copy.start()
        copies.append(copy)
    for copy in copies:
        copy.wait_recv()
    total = tbuf[(tiles - tile) % tiles]
    for q in range(1, tiles):
        total = total + tbuf[(q - tile + tiles) % tiles]
    ss_ref[...] = total
    for copy in copies:
        copy.wait_send()


def ray_allreduce(mesh, owned, prev=None, beta=None):
    axes = ray_axes(mesh)
    rows, width = owned.shape
    half = width // 2
    w1 = half // axes[0][0]
    w2 = w1 // axes[1][0]
    steps = max(axes[0][0], axes[1][0]) - 1
    tiles = mesh.shape["tile"]
    has_prev = prev is not None
    operands = (owned, prev, jnp.broadcast_to(beta[:, None], (rows, 128))) if has_prev else (owned,)
    return pl.pallas_call(
        functools.partial(allreduce_kernel, axes, tiles, has_prev),
        out_shape=(jax.ShapeDtypeStruct((rows, width), jnp.float32),
                   jax.ShapeDtypeStruct((rows, 128), jnp.float32)),
        in_specs=[pl.BlockSpec(memory_space=pltpu.VMEM)] * len(operands),
        out_specs=(pl.BlockSpec(memory_space=pltpu.VMEM), pl.BlockSpec(memory_space=pltpu.VMEM)),
        scratch_shapes=[
            pltpu.VMEM((2, rows, w1), jnp.float32),
            pltpu.VMEM((2, 2, steps, rows, w1 // 2), jnp.float32),
            pltpu.VMEM((2, 2, steps, rows, w1 // 2), jnp.float32),
            pltpu.VMEM((2, steps, rows, w2), jnp.float32),
            pltpu.VMEM((tiles, rows, 128), jnp.float32),
            pltpu.SemaphoreType.DMA((4, 2, 2, steps)),
            pltpu.SemaphoreType.DMA((4, 2, 2, steps)),
            pltpu.SemaphoreType.DMA((tiles,)),
            pltpu.SemaphoreType.DMA((tiles,)),
        ],
        compiler_params=pltpu.CompilerParams(
            collective_id=3 if has_prev else 2, has_side_effects=True, vmem_limit_bytes=60 * 1024 * 1024),
    )(*operands)


eps_norm = 1e-06


def per_device(mesh, data, sensitivity, block_tiles, block_bundles):
    columns = data.shape[0]
    bundles = block_bundles.reshape(-1)
    requests = lax.all_to_all(block_tiles, "tile", split_axis=1, concat_axis=1, tiled=True).reshape(
        -1
    )
    bundle_onehot = (bundles[:, None] == jnp.arange(BUND_DEV, dtype=jnp.int32)[None, :]).astype(
        jnp.float32
    )
    owner_onehot = (requests[:, None] == jnp.arange(TILE_DEV, dtype=jnp.int32)[None, :]).astype(
        jnp.bfloat16
    )

    def fetch(field_bf):
        owned = field_bf.reshape(columns, TILE_DEV, CB)
        outgoing = jnp.take(owned, requests, axis=1)
        tiles = lax.all_to_all(outgoing, "tile", split_axis=1, concat_axis=1, tiled=True)
        return tiles

    def forward(field_bf):
        tiles = fetch(field_bf)
        partial_value = jnp.einsum(
            "cnk,nrk->ncr", tiles, sensitivity, preferred_element_type=jnp.float32
        )
        summed = jnp.einsum(
            "ncr,nb->cbr", partial_value, bundle_onehot, precision=lax.Precision.HIGHEST
        )
        return summed.reshape(columns, BUND_DEV * RB)

    def adjoint(rays_bf, prev=None, beta=None):
        picked = jnp.take(rays_bf.reshape(columns, BUND_DEV, RB), bundles, axis=1)
        terms = jnp.einsum(
            "cnr,nrk->cnk", picked, sensitivity, preferred_element_type=jnp.float32
        ).astype(jnp.bfloat16)
        arrived = lax.all_to_all(terms, "tile", split_axis=1, concat_axis=1, tiled=True)
        owned = jnp.einsum(
            "cnk,nt->ctk", arrived, owner_onehot, preferred_element_type=jnp.float32
        ).reshape(columns, TILE_DEV * CB)
        field, squares = ray_allreduce(mesh, owned, prev, beta)
        return field, jnp.sqrt(squares[:, 0] + eps_norm)

    def cell_norm(field):
        local = jnp.sum(field * field, axis=1)
        total = group_sum(mesh, ("tile",), 1, local)
        return jnp.sqrt(total + eps_norm)

    def ray_norm(rays):
        total = group_sum(mesh, ("ray", "tile"), 0, jnp.sum(rays * rays, axis=1))
        return jnp.sqrt(total + eps_norm)

    beta_now = ray_norm(data)
    rays_dir = data / beta_now[:, None]
    model_dir, alpha_now = adjoint(rays_dir.astype(jnp.bfloat16))
    model_dir = model_dir / alpha_now[:, None]
    search = model_dir
    solution = jnp.zeros_like(model_dir)
    phi_bar = beta_now
    rho_bar = alpha_now
    for step in range(ITERS):
        rounded = model_dir.astype(jnp.bfloat16)
        rays_dir = forward(rounded) - alpha_now[:, None] * rays_dir
        beta_now = ray_norm(rays_dir)
        rays_dir = rays_dir / beta_now[:, None]
        rho_now = jnp.sqrt(rho_bar * rho_bar + beta_now * beta_now)
        cosine = rho_bar / rho_now
        sine_part = beta_now / rho_now
        phi_now = cosine * phi_bar
        phi_bar = sine_part * phi_bar
        solution = solution + (phi_now / rho_now)[:, None] * search
        if step + 1 < ITERS:
            model_dir, alpha_now = adjoint(rays_dir.astype(jnp.bfloat16), model_dir, beta_now)
            model_dir = model_dir / alpha_now[:, None]
            theta_now = sine_part * alpha_now
            rho_bar = -cosine * alpha_now
            search = model_dir - (theta_now / rho_now)[:, None] * search
    residual = data - forward(solution.astype(jnp.bfloat16))
    return (solution, residual)


def solution(mesh):
    return jax.shard_map(
        functools.partial(per_device, mesh),
        mesh=mesh,
        in_specs=(
            P(None, ("ray", "tile")),
            P(("ray", "tile"), None, None),
            P(("ray", "tile"), None, None),
            P(("ray", "tile"), None, None),
        ),
        out_specs=(P(None, "tile"), P(None, ("ray", "tile"))),
        check_vma=False,
    )
```

```python
import jax
import jax.numpy as jnp
from jax import lax
from jax.sharding import PartitionSpec as P

RB = 256
CB = 512
ITERS = 2
BUND_DEV = 8
TILE_DEV = 48


import functools
from jax.experimental import pallas as pl
from jax.experimental.pallas import tpu as pltpu

MESH = pl.DeviceIdType.MESH


def stage_plan(mesh, axes):
    plan = [(axis, mesh.shape[axis], 1) for axis in ("tile", "ray") if axis in axes]
    return tuple(stage for stage in plan if stage[1] > 1)


def reduce_kernel(plan, x_ref, o_ref, vals, send_sems, recv_sems):
    here = {"ray": lax.axis_index("ray"), "tile": lax.axis_index("tile")}

    def peer(axis, size, stride, k):
        idx = here[axis]
        pos = (idx // stride) % size
        other = idx + (((pos + k) % size) - pos) * stride
        coords = dict(here)
        coords[axis] = other
        return (coords["ray"], coords["tile"])

    barrier = pltpu.get_barrier_semaphore()
    count = 0
    for axis, size, stride in plan:
        for k in range(1, size):
            pl.semaphore_signal(barrier, inc=1, device_id=peer(axis, size, stride, k), device_id_type=MESH)
            count += 1
    pl.semaphore_wait(barrier, count)

    vals[0, 0] = x_ref[...]
    copies = []
    for s, (axis, size, stride) in enumerate(plan):
        src = x_ref if s == 0 else vals.at[s, 0]
        stage_copies = []
        for k in range(1, size):
            copy = pltpu.make_async_remote_copy(
                src_ref=src,
                dst_ref=vals.at[s, k],
                send_sem=send_sems.at[s, k],
                recv_sem=recv_sems.at[s, k],
                device_id=peer(axis, size, stride, (size - k) % size),
                device_id_type=MESH,
            )
            copy.start()
            stage_copies.append(copy)
        for copy in stage_copies:
            copy.wait_recv()
        copies += stage_copies
        pos = (here[axis] // stride) % size
        total = vals[s, (size - pos) % size]
        for q in range(1, size):
            total = total + vals[s, (q - pos + size) % size]
        if s + 1 < len(plan):
            vals[s + 1, 0] = total
        else:
            o_ref[...] = total
    for copy in copies:
        copy.wait_send()


def group_sum(mesh, axes, collective_id, partial):
    plan = stage_plan(mesh, axes)
    width = partial.shape[0]
    block = jnp.zeros((8, 128), jnp.float32).at[0, :width].set(partial)
    depth = max(size for _, size, _ in plan)
    out = pl.pallas_call(
        functools.partial(reduce_kernel, plan),
        out_shape=jax.ShapeDtypeStruct((8, 128), jnp.float32),
        in_specs=[pl.BlockSpec(memory_space=pltpu.VMEM)],
        out_specs=pl.BlockSpec(memory_space=pltpu.VMEM),
        scratch_shapes=[
            pltpu.VMEM((len(plan), depth, 8, 128), jnp.float32),
            pltpu.SemaphoreType.DMA((len(plan), depth)),
            pltpu.SemaphoreType.DMA((len(plan), depth)),
        ],
        compiler_params=pltpu.CompilerParams(collective_id=collective_id, has_side_effects=True),
    )(block)
    return out[0, :width]


def ray_axes(mesh):
    rays = mesh.shape["ray"]
    inner = 4 if rays % 4 == 0 else rays
    return ((inner, 1), (rays // inner, inner))


def allreduce_kernel(axes, x_hbm, o_ref, x_ref, part, rbuf1, acc1, rbuf2, load_sem, send_sems, recv_sems):
    me = lax.axis_index("ray")
    tile = lax.axis_index("tile")
    rows = x_hbm.shape[0]
    half = x_hbm.shape[1] // 2
    w1 = half // axes[0][0]
    w2 = w1 // axes[1][0]

    def pos(axis):
        size, stride = axis
        return (me // stride) % size

    def peer(axis, k):
        size, stride = axis
        p = pos(axis)
        return (me + (((p - k + size) % size) - p) * stride, tile)

    def cols(start, width):
        return pl.ds(pl.multiple_of(start, 128), width)

    def add_rows(dst, a, b):
        def body(r, carry):
            block = pl.ds(pl.multiple_of(r * 8, 8), 8)
            dst[block, :] = a[block, :] + b[block, :]
            return carry
        lax.fori_loop(0, rows // 8, body, 0)

    load = pltpu.make_async_copy(x_hbm, x_ref, load_sem)
    load.start()
    barrier = pltpu.get_barrier_semaphore()
    greeted = 0
    for axis in axes:
        for k in range(1, axis[0]):
            pl.semaphore_signal(barrier, inc=1, device_id=peer(axis, k), device_id_type=MESH)
            greeted += 1
    pl.semaphore_wait(barrier, greeted)

    plans = [(axes[0], axes[1]), (axes[1], axes[0])]
    sends = []

    def send(stage, h, d, s, axis, src, dst, landing):
        size = axis[0]
        k = size - 1 if d == 0 else 1
        sems = dict(send_sem=send_sems.at[stage, h, d, s], recv_sem=recv_sems.at[stage, h, d, s],
                    device_id=peer(axis, k), device_id_type=MESH)
        copy = pltpu.make_async_remote_copy(src_ref=src, dst_ref=dst, **sems)
        copy.start()
        sends.append(copy)
        return pltpu.make_async_remote_copy(src_ref=src, dst_ref=landing, **sems)

    def reduce_scatter(stage, segs, rbuf, acc, first):
        steps = segs[0][0][0] - 1
        for s in range(steps):
            waits = []
            for h, (axis, own, final) in enumerate(segs):
                size, p = axis[0], pos(axis)
                for d in range(2):
                    sign = 1 if d == 0 else -1
                    src = first[h]((p - sign * (s + 1) + 2 * size) % size, d) if s == 0 else acc.at[h, d, s - 1]
                    waits.append((h, d, send(stage, h, d, s, axis, src, rbuf.at[h, d, s], rbuf.at[h, d, s])))
            for h, d, copy in waits:
                copy.wait_recv()
            if s == 0:
                load.wait()
            for h, (axis, own, final) in enumerate(segs):
                size, p = axis[0], pos(axis)
                for d in range(2):
                    sign = 1 if d == 0 else -1
                    mine = own((p - sign * (s + 2) + 2 * size) % size, d)
                    dst = final(d) if s == steps - 1 else acc.at[h, d, s]
                    add_rows(dst, rbuf.at[h, d, s], mine)

    def all_gather(stage, segs):
        steps = segs[0][0][0] - 1
        for s in range(steps):
            waits = []
            for h, (axis, region) in enumerate(segs):
                size, p = axis[0], pos(axis)
                for d in range(2):
                    sign = 1 if d == 0 else -1
                    src = region((p - sign * s + 2 * size) % size, d)
                    landing = region((p - sign * (s + 1) + 2 * size) % size, d)
                    waits.append(send(stage, h, d, s, axis, src, src, landing))
            for copy in waits:
                copy.wait_recv()

    def direct_reduce_scatter(stage, segs, rbuf, width):
        waits = []
        for h, (axis, own, final) in enumerate(segs):
            size, p = axis[0], pos(axis)
            for k in range(1, size):
                slot = rbuf.at[h, k - 1]
                copy = pltpu.make_async_remote_copy(
                    src_ref=own((p - k + size) % size), dst_ref=slot,
                    send_sem=send_sems.at[stage, h, 0, k - 1], recv_sem=recv_sems.at[stage, h, 0, k - 1],
                    device_id=peer(axis, k), device_id_type=MESH)
                copy.start()
                sends.append(copy)
                waits.append(copy)
        for copy in waits:
            copy.wait_recv()
        for h, (axis, own, final) in enumerate(segs):
            size, p = axis[0], pos(axis)
            def body(r, carry, h=h, size=size, p=p, own=own, final=final):
                block = pl.ds(pl.multiple_of(r * 8, 8), 8)
                total = None
                for q in range(size):
                    k = (q - p + size) % size
                    mine = own(p)[block, :]
                    other = rbuf[h, jnp.maximum(k - 1, 0), block, :]
                    val = jnp.where(k == 0, mine, other)
                    total = val if total is None else total + val
                final[block, :] = total
                return carry
            lax.fori_loop(0, rows // 8, body, 0)

    def direct_all_gather(stage, segs):
        waits = []
        for h, (axis, region) in enumerate(segs):
            size, p = axis[0], pos(axis)
            for k in range(1, size):
                copy = pltpu.make_async_remote_copy(
                    src_ref=region(p), dst_ref=region(p),
                    send_sem=send_sems.at[stage, h, 0, k - 1], recv_sem=recv_sems.at[stage, h, 0, k - 1],
                    device_id=peer(axis, k), device_id_type=MESH)
                copy.start()
                sends.append(copy)
                waits.append(pltpu.make_async_remote_copy(
                    src_ref=region(p), dst_ref=region((p + k) % size),
                    send_sem=send_sems.at[stage, h, 0, k - 1], recv_sem=recv_sems.at[stage, h, 0, k - 1],
                    device_id=peer(axis, k), device_id_type=MESH))
        for copy in waits:
            copy.wait_recv()

    q1, q2 = w1 // 2, w2 // 2
    seg1, seg2, seg3, seg4 = [], [], [], []
    for h, (a1, a2) in enumerate(plans):
        p1, p2 = pos(a1), pos(a2)
        base = h * half + p1 * w1
        seg1.append((a1,
                     lambda j, d, h=h: x_ref.at[:, cols(h * half + j * w1 + d * q1, q1)],
                     lambda d, h=h: part.at[h, :, cols(d * q1, q1)]))
        seg2.append((a2,
                     lambda j, h=h: part.at[h, :, cols(j * w2, w2)],
                     o_ref.at[:, cols(base + p2 * w2, w2)]))
        seg3.append((a2, lambda j, base=base: o_ref.at[:, cols(base + j * w2, w2)]))
        seg4.append((a1, lambda j, d, h=h: o_ref.at[:, cols(h * half + j * w1 + d * q1, q1)]))
    firsts = [lambda j, d, h=h: x_hbm.at[:, cols(h * half + j * w1 + d * q1, q1)] for h in range(2)]
    reduce_scatter(0, seg1, rbuf1, acc1, firsts)
    direct_reduce_scatter(1, seg2, rbuf2, w2)
    direct_all_gather(2, seg3)
    all_gather(3, seg4)
    for copy in sends:
        copy.wait_send()


def ray_allreduce(mesh, owned):
    axes = ray_axes(mesh)
    rows, width = owned.shape
    half = width // 2
    w1 = half // axes[0][0]
    w2 = w1 // axes[1][0]
    steps = max(axes[0][0], axes[1][0]) - 1
    return pl.pallas_call(
        functools.partial(allreduce_kernel, axes),
        out_shape=jax.ShapeDtypeStruct((rows, width), jnp.float32),
        in_specs=[pl.BlockSpec(memory_space=pl.ANY)],
        out_specs=pl.BlockSpec(memory_space=pltpu.VMEM),
        scratch_shapes=[
            pltpu.VMEM((rows, width), jnp.float32),
            pltpu.VMEM((2, rows, w1), jnp.float32),
            pltpu.VMEM((2, 2, steps, rows, w1 // 2), jnp.float32),
            pltpu.VMEM((2, 2, steps, rows, w1 // 2), jnp.float32),
            pltpu.VMEM((2, steps, rows, w2), jnp.float32),
            pltpu.SemaphoreType.DMA(()),
            pltpu.SemaphoreType.DMA((4, 2, 2, steps)),
            pltpu.SemaphoreType.DMA((4, 2, 2, steps)),
        ],
        compiler_params=pltpu.CompilerParams(
            collective_id=2, has_side_effects=True, vmem_limit_bytes=60 * 1024 * 1024),
    )(owned)


eps_norm = 1e-06


def per_device(mesh, data, sensitivity, block_tiles, block_bundles):
    columns = data.shape[0]
    bundles = block_bundles.reshape(-1)
    requests = lax.all_to_all(block_tiles, "tile", split_axis=1, concat_axis=1, tiled=True).reshape(
        -1
    )
    bundle_onehot = (bundles[:, None] == jnp.arange(BUND_DEV, dtype=jnp.int32)[None, :]).astype(
        jnp.float32
    )
    owner_onehot = (requests[:, None] == jnp.arange(TILE_DEV, dtype=jnp.int32)[None, :]).astype(
        jnp.bfloat16
    )

    def fetch(field_bf):
        owned = field_bf.reshape(columns, TILE_DEV, CB)
        outgoing = jnp.take(owned, requests, axis=1)
        tiles = lax.all_to_all(outgoing, "tile", split_axis=1, concat_axis=1, tiled=True)
        return tiles

    def forward(field_bf):
        tiles = fetch(field_bf)
        partial_value = jnp.einsum(
            "cnk,nrk->ncr", tiles, sensitivity, preferred_element_type=jnp.float32
        )
        summed = jnp.einsum(
            "ncr,nb->cbr", partial_value, bundle_onehot, precision=lax.Precision.HIGHEST
        )
        return summed.reshape(columns, BUND_DEV * RB)

    def adjoint(rays_bf):
        picked = jnp.take(rays_bf.reshape(columns, BUND_DEV, RB), bundles, axis=1)
        terms = jnp.einsum(
            "cnr,nrk->cnk", picked, sensitivity, preferred_element_type=jnp.float32
        ).astype(jnp.bfloat16)
        arrived = lax.all_to_all(terms, "tile", split_axis=1, concat_axis=1, tiled=True)
        owned = jnp.einsum(
            "cnk,nt->ctk", arrived, owner_onehot, preferred_element_type=jnp.float32
        ).reshape(columns, TILE_DEV * CB)
        total = ray_allreduce(mesh, owned)
        return total

    def cell_norm(field):
        local = jnp.sum(field * field, axis=1)
        total = group_sum(mesh, ("tile",), 1, local)
        return jnp.sqrt(total + eps_norm)

    def ray_norm(rays):
        total = group_sum(mesh, ("ray", "tile"), 0, jnp.sum(rays * rays, axis=1))
        return jnp.sqrt(total + eps_norm)

    beta_now = ray_norm(data)
    rays_dir = data / beta_now[:, None]
    model_dir = adjoint(rays_dir.astype(jnp.bfloat16))
    alpha_now = cell_norm(model_dir)
    model_dir = model_dir / alpha_now[:, None]
    search = model_dir
    solution = jnp.zeros_like(model_dir)
    phi_bar = beta_now
    rho_bar = alpha_now
    for step in range(ITERS):
        rounded = model_dir.astype(jnp.bfloat16)
        rays_dir = forward(rounded) - alpha_now[:, None] * rays_dir
        beta_now = ray_norm(rays_dir)
        rays_dir = rays_dir / beta_now[:, None]
        rho_now = jnp.sqrt(rho_bar * rho_bar + beta_now * beta_now)
        cosine = rho_bar / rho_now
        sine_part = beta_now / rho_now
        phi_now = cosine * phi_bar
        phi_bar = sine_part * phi_bar
        solution = solution + (phi_now / rho_now)[:, None] * search
        if step + 1 < ITERS:
            model_dir = adjoint(rays_dir.astype(jnp.bfloat16)) - beta_now[:, None] * model_dir
            alpha_now = cell_norm(model_dir)
            model_dir = model_dir / alpha_now[:, None]
            theta_now = sine_part * alpha_now
            rho_bar = -cosine * alpha_now
            search = model_dir - (theta_now / rho_now)[:, None] * search
    residual = data - forward(solution.astype(jnp.bfloat16))
    return (solution, residual)


def solution(mesh):
    return jax.shard_map(
        functools.partial(per_device, mesh),
        mesh=mesh,
        in_specs=(
            P(None, ("ray", "tile")),
            P(("ray", "tile"), None, None),
            P(("ray", "tile"), None, None),
            P(("ray", "tile"), None, None),
        ),
        out_specs=(P(None, "tile"), P(None, ("ray", "tile"))),
        check_vma=False,
    )
```

```python
import jax
import jax.numpy as jnp
from jax import lax
from jax.sharding import PartitionSpec as P

RB = 256
CB = 512
ITERS = 2
BUND_DEV = 8
TILE_DEV = 48


import functools
from jax.experimental import pallas as pl
from jax.experimental.pallas import tpu as pltpu

MESH = pl.DeviceIdType.MESH


def stage_plan(mesh, axes):
    plan = [(axis, mesh.shape[axis], 1) for axis in ("tile", "ray") if axis in axes]
    return tuple(stage for stage in plan if stage[1] > 1)


def reduce_kernel(plan, x_ref, o_ref, vals, send_sems, recv_sems):
    here = {"ray": lax.axis_index("ray"), "tile": lax.axis_index("tile")}

    def peer(axis, size, stride, k):
        idx = here[axis]
        pos = (idx // stride) % size
        other = idx + (((pos + k) % size) - pos) * stride
        coords = dict(here)
        coords[axis] = other
        return (coords["ray"], coords["tile"])

    barrier = pltpu.get_barrier_semaphore()
    count = 0
    for axis, size, stride in plan:
        for k in range(1, size):
            pl.semaphore_signal(barrier, inc=1, device_id=peer(axis, size, stride, k), device_id_type=MESH)
            count += 1
    pl.semaphore_wait(barrier, count)

    vals[0, 0] = x_ref[...]
    copies = []
    for s, (axis, size, stride) in enumerate(plan):
        src = x_ref if s == 0 else vals.at[s, 0]
        stage_copies = []
        for k in range(1, size):
            copy = pltpu.make_async_remote_copy(
                src_ref=src,
                dst_ref=vals.at[s, k],
                send_sem=send_sems.at[s, k],
                recv_sem=recv_sems.at[s, k],
                device_id=peer(axis, size, stride, (size - k) % size),
                device_id_type=MESH,
            )
            copy.start()
            stage_copies.append(copy)
        for copy in stage_copies:
            copy.wait_recv()
        copies += stage_copies
        pos = (here[axis] // stride) % size
        total = vals[s, (size - pos) % size]
        for q in range(1, size):
            total = total + vals[s, (q - pos + size) % size]
        if s + 1 < len(plan):
            vals[s + 1, 0] = total
        else:
            o_ref[...] = total
    for copy in copies:
        copy.wait_send()


def group_sum(mesh, axes, collective_id, partial):
    plan = stage_plan(mesh, axes)
    width = partial.shape[0]
    block = jnp.zeros((8, 128), jnp.float32).at[0, :width].set(partial)
    depth = max(size for _, size, _ in plan)
    out = pl.pallas_call(
        functools.partial(reduce_kernel, plan),
        out_shape=jax.ShapeDtypeStruct((8, 128), jnp.float32),
        in_specs=[pl.BlockSpec(memory_space=pltpu.VMEM)],
        out_specs=pl.BlockSpec(memory_space=pltpu.VMEM),
        scratch_shapes=[
            pltpu.VMEM((len(plan), depth, 8, 128), jnp.float32),
            pltpu.SemaphoreType.DMA((len(plan), depth)),
            pltpu.SemaphoreType.DMA((len(plan), depth)),
        ],
        compiler_params=pltpu.CompilerParams(collective_id=collective_id, has_side_effects=True),
    )(block)
    return out[0, :width]


def ray_axes(mesh):
    rays = mesh.shape["ray"]
    inner = 4 if rays % 4 == 0 else rays
    return ((inner, 1), (rays // inner, inner))


def allreduce_kernel(axes, x_hbm, o_hbm, x_ref, o_ref, part, rbuf1, acc1, rbuf2, load_sem, store_sems, send_sems, recv_sems):
    me = lax.axis_index("ray")
    tile = lax.axis_index("tile")
    rows = x_hbm.shape[0]
    half = x_hbm.shape[1] // 2
    w1 = half // axes[0][0]
    w2 = w1 // axes[1][0]

    def pos(axis):
        size, stride = axis
        return (me // stride) % size

    def peer(axis, k):
        size, stride = axis
        p = pos(axis)
        return (me + (((p - k + size) % size) - p) * stride, tile)

    def cols(start, width):
        return pl.ds(pl.multiple_of(start, 128), width)

    def add_rows(dst, a, b):
        def body(r, carry):
            block = pl.ds(pl.multiple_of(r * 8, 8), 8)
            dst[block, :] = a[block, :] + b[block, :]
            return carry
        lax.fori_loop(0, rows // 8, body, 0)

    load = pltpu.make_async_copy(x_hbm, x_ref, load_sem)
    load.start()
    barrier = pltpu.get_barrier_semaphore()
    greeted = 0
    for axis in axes:
        for k in range(1, axis[0]):
            pl.semaphore_signal(barrier, inc=1, device_id=peer(axis, k), device_id_type=MESH)
            greeted += 1
    pl.semaphore_wait(barrier, greeted)

    plans = [(axes[0], axes[1]), (axes[1], axes[0])]
    sends = []

    def send(stage, h, d, s, axis, src, dst, landing):
        size = axis[0]
        k = size - 1 if d == 0 else 1
        sems = dict(send_sem=send_sems.at[stage, h, d, s], recv_sem=recv_sems.at[stage, h, d, s],
                    device_id=peer(axis, k), device_id_type=MESH)
        copy = pltpu.make_async_remote_copy(src_ref=src, dst_ref=dst, **sems)
        copy.start()
        sends.append(copy)
        return pltpu.make_async_remote_copy(src_ref=src, dst_ref=landing, **sems)

    def reduce_scatter(stage, segs, rbuf, acc, first):
        steps = segs[0][0][0] - 1
        for s in range(steps):
            waits = []
            for h, (axis, own, final) in enumerate(segs):
                size, p = axis[0], pos(axis)
                for d in range(2):
                    sign = 1 if d == 0 else -1
                    src = first[h]((p - sign * (s + 1) + 2 * size) % size, d) if s == 0 else acc.at[h, d, s - 1]
                    waits.append((h, d, send(stage, h, d, s, axis, src, rbuf.at[h, d, s], rbuf.at[h, d, s])))
            for h, d, copy in waits:
                copy.wait_recv()
            if s == 0:
                load.wait()
            for h, (axis, own, final) in enumerate(segs):
                size, p = axis[0], pos(axis)
                for d in range(2):
                    sign = 1 if d == 0 else -1
                    mine = own((p - sign * (s + 2) + 2 * size) % size, d)
                    dst = final(d) if s == steps - 1 else acc.at[h, d, s]
                    add_rows(dst, rbuf.at[h, d, s], mine)

    def all_gather(stage, segs):
        steps = segs[0][0][0] - 1
        for s in range(steps):
            waits = []
            for h, (axis, region) in enumerate(segs):
                size, p = axis[0], pos(axis)
                for d in range(2):
                    sign = 1 if d == 0 else -1
                    src = region((p - sign * s + 2 * size) % size, d)
                    landing = region((p - sign * (s + 1) + 2 * size) % size, d)
                    waits.append(send(stage, h, d, s, axis, src, src, landing))
            for copy in waits:
                copy.wait_recv()
            for h, (axis, region) in enumerate(segs):
                size, p = axis[0], pos(axis)
                for d in range(2):
                    sign = 1 if d == 0 else -1
                    store(h, (p - sign * (s + 1) + 2 * size) % size, d)

    def direct_reduce_scatter(stage, segs, rbuf, width):
        waits = []
        for h, (axis, own, final) in enumerate(segs):
            size, p = axis[0], pos(axis)
            for k in range(1, size):
                slot = rbuf.at[h, k - 1]
                copy = pltpu.make_async_remote_copy(
                    src_ref=own((p - k + size) % size), dst_ref=slot,
                    send_sem=send_sems.at[stage, h, 0, k - 1], recv_sem=recv_sems.at[stage, h, 0, k - 1],
                    device_id=peer(axis, k), device_id_type=MESH)
                copy.start()
                sends.append(copy)
                waits.append(copy)
        for copy in waits:
            copy.wait_recv()
        for h, (axis, own, final) in enumerate(segs):
            size, p = axis[0], pos(axis)
            def body(r, carry, h=h, size=size, p=p, own=own, final=final):
                block = pl.ds(pl.multiple_of(r * 8, 8), 8)
                total = None
                for q in range(size):
                    k = (q - p + size) % size
                    mine = own(p)[block, :]
                    other = rbuf[h, jnp.maximum(k - 1, 0), block, :]
                    val = jnp.where(k == 0, mine, other)
                    total = val if total is None else total + val
                final[block, :] = total
                return carry
            lax.fori_loop(0, rows // 8, body, 0)

    def direct_all_gather(stage, segs):
        waits = []
        for h, (axis, region) in enumerate(segs):
            size, p = axis[0], pos(axis)
            for k in range(1, size):
                copy = pltpu.make_async_remote_copy(
                    src_ref=region(p), dst_ref=region(p),
                    send_sem=send_sems.at[stage, h, 0, k - 1], recv_sem=recv_sems.at[stage, h, 0, k - 1],
                    device_id=peer(axis, k), device_id_type=MESH)
                copy.start()
                sends.append(copy)
                waits.append(pltpu.make_async_remote_copy(
                    src_ref=region(p), dst_ref=region((p + k) % size),
                    send_sem=send_sems.at[stage, h, 0, k - 1], recv_sem=recv_sems.at[stage, h, 0, k - 1],
                    device_id=peer(axis, k), device_id_type=MESH))
        for copy in waits:
            copy.wait_recv()

    q1, q2 = w1 // 2, w2 // 2
    stores = []

    def store(h, j, d):
        region = cols(h * half + j * w1 + d * q1, q1)
        copy = pltpu.make_async_copy(o_ref.at[:, region], o_hbm.at[:, region], store_sems.at[h, j, d])
        copy.start()
        stores.append(copy)
    seg1, seg2, seg3, seg4 = [], [], [], []
    for h, (a1, a2) in enumerate(plans):
        p1, p2 = pos(a1), pos(a2)
        base = h * half + p1 * w1
        seg1.append((a1,
                     lambda j, d, h=h: x_ref.at[:, cols(h * half + j * w1 + d * q1, q1)],
                     lambda d, h=h: part.at[h, :, cols(d * q1, q1)]))
        seg2.append((a2,
                     lambda j, h=h: part.at[h, :, cols(j * w2, w2)],
                     o_ref.at[:, cols(base + p2 * w2, w2)]))
        seg3.append((a2, lambda j, base=base: o_ref.at[:, cols(base + j * w2, w2)]))
        seg4.append((a1, lambda j, d, h=h: o_ref.at[:, cols(h * half + j * w1 + d * q1, q1)]))
    firsts = [lambda j, d, h=h: x_hbm.at[:, cols(h * half + j * w1 + d * q1, q1)] for h in range(2)]
    reduce_scatter(0, seg1, rbuf1, acc1, firsts)
    direct_reduce_scatter(1, seg2, rbuf2, w2)
    direct_all_gather(2, seg3)
    for h, (a1, a2) in enumerate(plans):
        for d in range(2):
            store(h, pos(a1), d)
    all_gather(3, seg4)
    for copy in sends:
        copy.wait_send()
    for copy in stores:
        copy.wait()


def ray_allreduce(mesh, owned):
    axes = ray_axes(mesh)
    rows, width = owned.shape
    half = width // 2
    w1 = half // axes[0][0]
    w2 = w1 // axes[1][0]
    steps = max(axes[0][0], axes[1][0]) - 1
    return pl.pallas_call(
        functools.partial(allreduce_kernel, axes),
        out_shape=jax.ShapeDtypeStruct((rows, width), jnp.float32),
        in_specs=[pl.BlockSpec(memory_space=pl.ANY)],
        out_specs=pl.BlockSpec(memory_space=pl.ANY),
        scratch_shapes=[
            pltpu.VMEM((rows, width), jnp.float32),
            pltpu.VMEM((rows, width), jnp.float32),
            pltpu.VMEM((2, rows, w1), jnp.float32),
            pltpu.VMEM((2, 2, steps, rows, w1 // 2), jnp.float32),
            pltpu.VMEM((2, 2, steps, rows, w1 // 2), jnp.float32),
            pltpu.VMEM((2, steps, rows, w2), jnp.float32),
            pltpu.SemaphoreType.DMA(()),
            pltpu.SemaphoreType.DMA((2, axes[0][0], 2)),
            pltpu.SemaphoreType.DMA((4, 2, 2, steps)),
            pltpu.SemaphoreType.DMA((4, 2, 2, steps)),
        ],
        compiler_params=pltpu.CompilerParams(
            collective_id=2, has_side_effects=True, vmem_limit_bytes=60 * 1024 * 1024),
    )(owned)


eps_norm = 1e-06


def per_device(mesh, data, sensitivity, block_tiles, block_bundles):
    columns = data.shape[0]
    bundles = block_bundles.reshape(-1)
    requests = lax.all_to_all(block_tiles, "tile", split_axis=1, concat_axis=1, tiled=True).reshape(
        -1
    )
    bundle_onehot = (bundles[:, None] == jnp.arange(BUND_DEV, dtype=jnp.int32)[None, :]).astype(
        jnp.float32
    )
    owner_onehot = (requests[:, None] == jnp.arange(TILE_DEV, dtype=jnp.int32)[None, :]).astype(
        jnp.bfloat16
    )

    def fetch(field_bf):
        owned = field_bf.reshape(columns, TILE_DEV, CB)
        outgoing = jnp.take(owned, requests, axis=1)
        tiles = lax.all_to_all(outgoing, "tile", split_axis=1, concat_axis=1, tiled=True)
        return tiles

    def forward(field_bf):
        tiles = fetch(field_bf)
        partial_value = jnp.einsum(
            "cnk,nrk->ncr", tiles, sensitivity, preferred_element_type=jnp.float32
        )
        summed = jnp.einsum(
            "ncr,nb->cbr", partial_value, bundle_onehot, precision=lax.Precision.HIGHEST
        )
        return summed.reshape(columns, BUND_DEV * RB)

    def adjoint(rays_bf):
        picked = jnp.take(rays_bf.reshape(columns, BUND_DEV, RB), bundles, axis=1)
        terms = jnp.einsum(
            "cnr,nrk->cnk", picked, sensitivity, preferred_element_type=jnp.float32
        ).astype(jnp.bfloat16)
        arrived = lax.all_to_all(terms, "tile", split_axis=1, concat_axis=1, tiled=True)
        owned = jnp.einsum(
            "cnk,nt->ctk", arrived, owner_onehot, preferred_element_type=jnp.float32
        ).reshape(columns, TILE_DEV * CB)
        total = ray_allreduce(mesh, owned)
        return total

    def cell_norm(field):
        local = jnp.sum(field * field, axis=1)
        total = group_sum(mesh, ("tile",), 1, local)
        return jnp.sqrt(total + eps_norm)

    def ray_norm(rays):
        total = group_sum(mesh, ("ray", "tile"), 0, jnp.sum(rays * rays, axis=1))
        return jnp.sqrt(total + eps_norm)

    beta_now = ray_norm(data)
    rays_dir = data / beta_now[:, None]
    model_dir = adjoint(rays_dir.astype(jnp.bfloat16))
    alpha_now = cell_norm(model_dir)
    model_dir = model_dir / alpha_now[:, None]
    search = model_dir
    solution = jnp.zeros_like(model_dir)
    phi_bar = beta_now
    rho_bar = alpha_now
    for step in range(ITERS):
        rounded = model_dir.astype(jnp.bfloat16)
        rays_dir = forward(rounded) - alpha_now[:, None] * rays_dir
        beta_now = ray_norm(rays_dir)
        rays_dir = rays_dir / beta_now[:, None]
        rho_now = jnp.sqrt(rho_bar * rho_bar + beta_now * beta_now)
        cosine = rho_bar / rho_now
        sine_part = beta_now / rho_now
        phi_now = cosine * phi_bar
        phi_bar = sine_part * phi_bar
        solution = solution + (phi_now / rho_now)[:, None] * search
        if step + 1 < ITERS:
            model_dir = adjoint(rays_dir.astype(jnp.bfloat16)) - beta_now[:, None] * model_dir
            alpha_now = cell_norm(model_dir)
            model_dir = model_dir / alpha_now[:, None]
            theta_now = sine_part * alpha_now
            rho_bar = -cosine * alpha_now
            search = model_dir - (theta_now / rho_now)[:, None] * search
    residual = data - forward(solution.astype(jnp.bfloat16))
    return (solution, residual)


def solution(mesh):
    return jax.shard_map(
        functools.partial(per_device, mesh),
        mesh=mesh,
        in_specs=(
            P(None, ("ray", "tile")),
            P(("ray", "tile"), None, None),
            P(("ray", "tile"), None, None),
            P(("ray", "tile"), None, None),
        ),
        out_specs=(P(None, "tile"), P(None, ("ray", "tile"))),
        check_vma=False,
    )
```

```python
import jax
import jax.numpy as jnp
from jax import lax
from jax.sharding import PartitionSpec as P

RB = 256
CB = 512
ITERS = 2
BUND_DEV = 8
TILE_DEV = 48


import functools
from jax.experimental import pallas as pl
from jax.experimental.pallas import tpu as pltpu

MESH = pl.DeviceIdType.MESH


def stage_plan(mesh, axes):
    plan = [(axis, mesh.shape[axis], 1) for axis in ("tile", "ray") if axis in axes]
    return tuple(stage for stage in plan if stage[1] > 1)


def reduce_kernel(plan, x_ref, o_ref, vals, send_sems, recv_sems):
    here = {"ray": lax.axis_index("ray"), "tile": lax.axis_index("tile")}

    def peer(axis, size, stride, k):
        idx = here[axis]
        pos = (idx // stride) % size
        other = idx + (((pos + k) % size) - pos) * stride
        coords = dict(here)
        coords[axis] = other
        return (coords["ray"], coords["tile"])

    barrier = pltpu.get_barrier_semaphore()
    count = 0
    for axis, size, stride in plan:
        for k in range(1, size):
            pl.semaphore_signal(barrier, inc=1, device_id=peer(axis, size, stride, k), device_id_type=MESH)
            count += 1
    pl.semaphore_wait(barrier, count)

    vals[0, 0] = x_ref[...]
    copies = []
    for s, (axis, size, stride) in enumerate(plan):
        src = x_ref if s == 0 else vals.at[s, 0]
        stage_copies = []
        for k in range(1, size):
            copy = pltpu.make_async_remote_copy(
                src_ref=src,
                dst_ref=vals.at[s, k],
                send_sem=send_sems.at[s, k],
                recv_sem=recv_sems.at[s, k],
                device_id=peer(axis, size, stride, (size - k) % size),
                device_id_type=MESH,
            )
            copy.start()
            stage_copies.append(copy)
        for copy in stage_copies:
            copy.wait_recv()
        copies += stage_copies
        pos = (here[axis] // stride) % size
        total = vals[s, (size - pos) % size]
        for q in range(1, size):
            total = total + vals[s, (q - pos + size) % size]
        if s + 1 < len(plan):
            vals[s + 1, 0] = total
        else:
            o_ref[...] = total
    for copy in copies:
        copy.wait_send()


def group_sum(mesh, axes, collective_id, partial):
    plan = stage_plan(mesh, axes)
    width = partial.shape[0]
    block = jnp.zeros((8, 128), jnp.float32).at[0, :width].set(partial)
    depth = max(size for _, size, _ in plan)
    out = pl.pallas_call(
        functools.partial(reduce_kernel, plan),
        out_shape=jax.ShapeDtypeStruct((8, 128), jnp.float32),
        in_specs=[pl.BlockSpec(memory_space=pltpu.VMEM)],
        out_specs=pl.BlockSpec(memory_space=pltpu.VMEM),
        scratch_shapes=[
            pltpu.VMEM((len(plan), depth, 8, 128), jnp.float32),
            pltpu.SemaphoreType.DMA((len(plan), depth)),
            pltpu.SemaphoreType.DMA((len(plan), depth)),
        ],
        compiler_params=pltpu.CompilerParams(collective_id=collective_id, has_side_effects=True),
    )(block)
    return out[0, :width]


def ray_axes(mesh):
    rays = mesh.shape["ray"]
    inner = 4 if rays % 4 == 0 else rays
    return ((inner, 1), (rays // inner, inner))


def allreduce_kernel(axes, x_hbm, o_hbm, x_ref, o_ref, part, rbuf1, acc1, rbuf2, load_sem, store_sems, send_sems, recv_sems):
    me = lax.axis_index("ray")
    tile = lax.axis_index("tile")
    rows = x_hbm.shape[0]
    half = x_hbm.shape[1] // 2
    w1 = half // axes[0][0]
    w2 = w1 // axes[1][0]

    def pos(axis):
        size, stride = axis
        return (me // stride) % size

    def peer(axis, k):
        size, stride = axis
        p = pos(axis)
        return (me + (((p - k + size) % size) - p) * stride, tile)

    def cols(start, width):
        return pl.ds(pl.multiple_of(start, 128), width)

    def add_rows(dst, a, b):
        def body(r, carry):
            block = pl.ds(pl.multiple_of(r * 8, 8), 8)
            dst[block, :] = a[block, :] + b[block, :]
            return carry
        lax.fori_loop(0, rows // 8, body, 0)

    load = pltpu.make_async_copy(x_hbm, x_ref, load_sem)
    load.start()
    barrier = pltpu.get_barrier_semaphore()
    greeted = 0
    for axis in axes:
        for k in range(1, axis[0]):
            pl.semaphore_signal(barrier, inc=1, device_id=peer(axis, k), device_id_type=MESH)
            greeted += 1
    pl.semaphore_wait(barrier, greeted)

    plans = [(axes[0], axes[1]), (axes[1], axes[0])]
    sends = []

    def send(stage, h, d, s, axis, src, dst, landing):
        size = axis[0]
        k = size - 1 if d == 0 else 1
        sems = dict(send_sem=send_sems.at[stage, h, d, s], recv_sem=recv_sems.at[stage, h, d, s],
                    device_id=peer(axis, k), device_id_type=MESH)
        copy = pltpu.make_async_remote_copy(src_ref=src, dst_ref=dst, **sems)
        copy.start()
        sends.append(copy)
        return pltpu.make_async_remote_copy(src_ref=src, dst_ref=landing, **sems)

    def reduce_scatter(stage, segs, rbuf, acc, first):
        steps = segs[0][0][0] - 1
        for s in range(steps):
            waits = []
            for h, (axis, own, final) in enumerate(segs):
                size, p = axis[0], pos(axis)
                for d in range(2):
                    sign = 1 if d == 0 else -1
                    src = first[h]((p - sign * (s + 1) + 2 * size) % size, d) if s == 0 else acc.at[h, d, s - 1]
                    waits.append((h, d, send(stage, h, d, s, axis, src, rbuf.at[h, d, s], rbuf.at[h, d, s])))
            for h, d, copy in waits:
                copy.wait_recv()
            if s == 0:
                load.wait()
            for h, (axis, own, final) in enumerate(segs):
                size, p = axis[0], pos(axis)
                for d in range(2):
                    sign = 1 if d == 0 else -1
                    mine = own((p - sign * (s + 2) + 2 * size) % size, d)
                    dst = final(d) if s == steps - 1 else acc.at[h, d, s]
                    add_rows(dst, rbuf.at[h, d, s], mine)

    def all_gather(stage, segs):
        steps = segs[0][0][0] - 1
        for s in range(steps):
            waits = []
            for h, (axis, region) in enumerate(segs):
                size, p = axis[0], pos(axis)
                for d in range(2):
                    sign = 1 if d == 0 else -1
                    src = region((p - sign * s + 2 * size) % size, d)
                    landing = region((p - sign * (s + 1) + 2 * size) % size, d)
                    waits.append(send(stage, h, d, s, axis, src, src, landing))
            for copy in waits:
                copy.wait_recv()
            for h, (axis, region) in enumerate(segs):
                size, p = axis[0], pos(axis)
                for d in range(2):
                    sign = 1 if d == 0 else -1
                    store(h, (p - sign * (s + 1) + 2 * size) % size, d)

    def direct_reduce_scatter(stage, segs, rbuf, width):
        waits = []
        for h, (axis, own, final) in enumerate(segs):
            size, p = axis[0], pos(axis)
            for k in range(1, size):
                slot = rbuf.at[h, k - 1]
                copy = pltpu.make_async_remote_copy(
                    src_ref=own((p - k + size) % size), dst_ref=slot,
                    send_sem=send_sems.at[stage, h, 0, k - 1], recv_sem=recv_sems.at[stage, h, 0, k - 1],
                    device_id=peer(axis, k), device_id_type=MESH)
                copy.start()
                sends.append(copy)
                waits.append(copy)
        for copy in waits:
            copy.wait_recv()
        for h, (axis, own, final) in enumerate(segs):
            size, p = axis[0], pos(axis)
            def body(r, carry, h=h, size=size, p=p, own=own, final=final):
                block = pl.ds(pl.multiple_of(r * 8, 8), 8)
                total = None
                for q in range(size):
                    k = (q - p + size) % size
                    mine = own(p)[block, :]
                    other = rbuf[h, jnp.maximum(k - 1, 0), block, :]
                    val = jnp.where(k == 0, mine, other)
                    total = val if total is None else total + val
                final[block, :] = total
                return carry
            lax.fori_loop(0, rows // 8, body, 0)

    def direct_all_gather(stage, segs):
        waits = []
        for h, (axis, region) in enumerate(segs):
            size, p = axis[0], pos(axis)
            for k in range(1, size):
                copy = pltpu.make_async_remote_copy(
                    src_ref=region(p), dst_ref=region(p),
                    send_sem=send_sems.at[stage, h, 0, k - 1], recv_sem=recv_sems.at[stage, h, 0, k - 1],
                    device_id=peer(axis, k), device_id_type=MESH)
                copy.start()
                sends.append(copy)
                waits.append(pltpu.make_async_remote_copy(
                    src_ref=region(p), dst_ref=region((p + k) % size),
                    send_sem=send_sems.at[stage, h, 0, k - 1], recv_sem=recv_sems.at[stage, h, 0, k - 1],
                    device_id=peer(axis, k), device_id_type=MESH))
        for copy in waits:
            copy.wait_recv()

    q1, q2 = w1 // 2, w2 // 2
    stores = []

    def store(h, j, d):
        region = cols(h * half + j * w1 + d * q1, q1)
        copy = pltpu.make_async_copy(o_ref.at[:, region], o_hbm.at[:, region], store_sems.at[h, j, d])
        copy.start()
        stores.append(copy)
    seg1, seg2, seg3, seg4 = [], [], [], []
    for h, (a1, a2) in enumerate(plans):
        p1, p2 = pos(a1), pos(a2)
        base = h * half + p1 * w1
        seg1.append((a1,
                     lambda j, d, h=h: x_ref.at[:, cols(h * half + j * w1 + d * q1, q1)],
                     lambda d, h=h: part.at[h, :, cols(d * q1, q1)]))
        seg2.append((a2,
                     lambda j, h=h: part.at[h, :, cols(j * w2, w2)],
                     o_ref.at[:, cols(base + p2 * w2, w2)]))
        seg3.append((a2, lambda j, base=base: o_ref.at[:, cols(base + j * w2, w2)]))
        seg4.append((a1, lambda j, d, h=h: o_ref.at[:, cols(h * half + j * w1 + d * q1, q1)]))
    firsts = [lambda j, d, h=h: x_hbm.at[:, cols(h * half + j * w1 + d * q1, q1)] for h in range(2)]
    reduce_scatter(0, seg1, rbuf1, acc1, firsts)
    direct_reduce_scatter(1, seg2, rbuf2, w2)
    direct_all_gather(2, seg3)
    for h, (a1, a2) in enumerate(plans):
        for d in range(2):
            store(h, pos(a1), d)
    all_gather(3, seg4)
    for copy in sends:
        copy.wait_send()
    for copy in stores:
        copy.wait()


def ray_allreduce(mesh, owned):
    axes = ray_axes(mesh)
    rows, width = owned.shape
    half = width // 2
    w1 = half // axes[0][0]
    w2 = w1 // axes[1][0]
    steps = max(axes[0][0], axes[1][0]) - 1
    return pl.pallas_call(
        functools.partial(allreduce_kernel, axes),
        out_shape=jax.ShapeDtypeStruct((rows, width), jnp.float32),
        in_specs=[pl.BlockSpec(memory_space=pl.ANY)],
        out_specs=pl.BlockSpec(memory_space=pl.ANY),
        scratch_shapes=[
            pltpu.VMEM((rows, width), jnp.float32),
            pltpu.VMEM((rows, width), jnp.float32),
            pltpu.VMEM((2, rows, w1), jnp.float32),
            pltpu.VMEM((2, 2, steps, rows, w1 // 2), jnp.float32),
            pltpu.VMEM((2, 2, steps, rows, w1 // 2), jnp.float32),
            pltpu.VMEM((2, steps, rows, w2), jnp.float32),
            pltpu.SemaphoreType.DMA(()),
            pltpu.SemaphoreType.DMA((2, axes[0][0], 2)),
            pltpu.SemaphoreType.DMA((4, 2, 2, steps)),
            pltpu.SemaphoreType.DMA((4, 2, 2, steps)),
        ],
        compiler_params=pltpu.CompilerParams(
            collective_id=2, has_side_effects=True, vmem_limit_bytes=60 * 1024 * 1024),
    )(owned)


eps_norm = 1e-06


def per_device(mesh, data, sensitivity, block_tiles, block_bundles):
    columns = data.shape[0]
    bundles = block_bundles.reshape(-1)
    requests = lax.all_to_all(block_tiles, "tile", split_axis=1, concat_axis=1, tiled=True).reshape(
        -1
    )
    bundle_onehot = (bundles[:, None] == jnp.arange(BUND_DEV, dtype=jnp.int32)[None, :]).astype(
        jnp.float32
    )
    owner_onehot = (requests[:, None] == jnp.arange(TILE_DEV, dtype=jnp.int32)[None, :]).astype(
        jnp.bfloat16
    )

    def fetch(field_bf):
        owned = field_bf.reshape(columns, TILE_DEV, CB)
        outgoing = jnp.take(owned, requests, axis=1, mode="clip")
        tiles = lax.all_to_all(outgoing, "tile", split_axis=1, concat_axis=1, tiled=True)
        return tiles

    def forward(field_bf):
        tiles = fetch(field_bf)
        partial_value = jnp.einsum(
            "cnk,nrk->ncr", tiles, sensitivity, preferred_element_type=jnp.float32
        )
        summed = jnp.einsum(
            "ncr,nb->cbr", partial_value, bundle_onehot, precision=lax.Precision.HIGHEST
        )
        return summed.reshape(columns, BUND_DEV * RB)

    def adjoint(rays_bf):
        picked = jnp.take(rays_bf.reshape(columns, BUND_DEV, RB), bundles, axis=1, mode="clip")
        terms = jnp.einsum(
            "cnr,nrk->cnk", picked, sensitivity, preferred_element_type=jnp.float32
        ).astype(jnp.bfloat16)
        arrived = lax.all_to_all(terms, "tile", split_axis=1, concat_axis=1, tiled=True)
        owned = jnp.einsum(
            "cnk,nt->ctk", arrived, owner_onehot, preferred_element_type=jnp.float32
        ).reshape(columns, TILE_DEV * CB)
        total = ray_allreduce(mesh, owned)
        return total

    def cell_norm(field):
        local = jnp.sum(field * field, axis=1)
        total = group_sum(mesh, ("tile",), 1, local)
        return jnp.sqrt(total + eps_norm)

    def ray_norm(rays):
        total = group_sum(mesh, ("ray", "tile"), 0, jnp.sum(rays * rays, axis=1))
        return jnp.sqrt(total + eps_norm)

    beta_now = ray_norm(data)
    rays_dir = data / beta_now[:, None]
    model_dir = adjoint(rays_dir.astype(jnp.bfloat16))
    alpha_now = cell_norm(model_dir)
    model_dir = model_dir / alpha_now[:, None]
    search = model_dir
    solution = jnp.zeros_like(model_dir)
    phi_bar = beta_now
    rho_bar = alpha_now
    for step in range(ITERS):
        rounded = model_dir.astype(jnp.bfloat16)
        rays_dir = forward(rounded) - alpha_now[:, None] * rays_dir
        beta_now = ray_norm(rays_dir)
        rays_dir = rays_dir / beta_now[:, None]
        rho_now = jnp.sqrt(rho_bar * rho_bar + beta_now * beta_now)
        cosine = rho_bar / rho_now
        sine_part = beta_now / rho_now
        phi_now = cosine * phi_bar
        phi_bar = sine_part * phi_bar
        solution = solution + (phi_now / rho_now)[:, None] * search
        if step + 1 < ITERS:
            model_dir = adjoint(rays_dir.astype(jnp.bfloat16)) - beta_now[:, None] * model_dir
            alpha_now = cell_norm(model_dir)
            model_dir = model_dir / alpha_now[:, None]
            theta_now = sine_part * alpha_now
            rho_bar = -cosine * alpha_now
            search = model_dir - (theta_now / rho_now)[:, None] * search
    residual = data - forward(solution.astype(jnp.bfloat16))
    return (solution, residual)


def solution(mesh):
    return jax.shard_map(
        functools.partial(per_device, mesh),
        mesh=mesh,
        in_specs=(
            P(None, ("ray", "tile")),
            P(("ray", "tile"), None, None),
            P(("ray", "tile"), None, None),
            P(("ray", "tile"), None, None),
        ),
        out_specs=(P(None, "tile"), P(None, ("ray", "tile"))),
        check_vma=False,
    )
```

```python
import jax
import jax.numpy as jnp
from jax import lax
from jax.sharding import PartitionSpec as P

RB = 256
CB = 512
ITERS = 2
BUND_DEV = 8
TILE_DEV = 48


import functools
from jax.experimental import pallas as pl
from jax.experimental.pallas import tpu as pltpu

MESH = pl.DeviceIdType.MESH


def stage_plan(mesh, axes):
    plan = [(axis, mesh.shape[axis], 1) for axis in ("tile", "ray") if axis in axes]
    return tuple(stage for stage in plan if stage[1] > 1)


def reduce_kernel(plan, x_ref, o_ref, vals, send_sems, recv_sems):
    here = {"ray": lax.axis_index("ray"), "tile": lax.axis_index("tile")}

    def peer(axis, size, stride, k):
        idx = here[axis]
        pos = (idx // stride) % size
        other = idx + (((pos + k) % size) - pos) * stride
        coords = dict(here)
        coords[axis] = other
        return (coords["ray"], coords["tile"])

    barrier = pltpu.get_barrier_semaphore()
    count = 0
    for axis, size, stride in plan:
        def greet(k, carry, axis=axis, size=size, stride=stride):
            pl.semaphore_signal(barrier, inc=1, device_id=peer(axis, size, stride, k), device_id_type=MESH)
            return carry
        lax.fori_loop(1, size, greet, 0)
        count += size - 1
    pl.semaphore_wait(barrier, count)

    def copy_of(s, axis, size, stride, k):
        src = x_ref if s == 0 else vals.at[s, 0]
        return pltpu.make_async_remote_copy(
            src_ref=src,
            dst_ref=vals.at[s, k],
            send_sem=send_sems.at[s, k],
            recv_sem=recv_sems.at[s, k],
            device_id=peer(axis, size, stride, (size - k) % size),
            device_id_type=MESH,
        )

    for s, (axis, size, stride) in enumerate(plan):
        def start(k, carry, s=s, axis=axis, size=size, stride=stride):
            copy_of(s, axis, size, stride, k).start()
            return carry

        def arrive(k, carry, s=s, axis=axis, size=size, stride=stride):
            copy_of(s, axis, size, stride, k).wait_recv()
            return carry
        lax.fori_loop(1, size, start, 0)
        lax.fori_loop(1, size, arrive, 0)
        pos = (here[axis] // stride) % size
        own = x_ref[...] if s == 0 else vals[s, 0]
        total = jnp.where(pos == 0, own, vals[s, (size - pos) % size])
        for q in range(1, size):
            total = total + jnp.where(pos == q, own, vals[s, (q - pos + size) % size])
        if s + 1 < len(plan):
            vals[s + 1, 0] = total
        else:
            o_ref[...] = total
    for s, (axis, size, stride) in enumerate(plan):
        def sent(k, carry, s=s, axis=axis, size=size, stride=stride):
            copy_of(s, axis, size, stride, k).wait_send()
            return carry
        lax.fori_loop(1, size, sent, 0)


def group_sum(mesh, axes, collective_id, partial):
    plan = stage_plan(mesh, axes)
    width = partial.shape[0]
    block = jnp.zeros((8, 128), jnp.float32).at[0, :width].set(partial)
    depth = max(size for _, size, _ in plan)
    out = pl.pallas_call(
        functools.partial(reduce_kernel, plan),
        out_shape=jax.ShapeDtypeStruct((8, 128), jnp.float32),
        in_specs=[pl.BlockSpec(memory_space=pltpu.VMEM)],
        out_specs=pl.BlockSpec(memory_space=pltpu.VMEM),
        scratch_shapes=[
            pltpu.VMEM((len(plan), depth, 8, 128), jnp.float32),
            pltpu.SemaphoreType.DMA((len(plan), depth)),
            pltpu.SemaphoreType.DMA((len(plan), depth)),
        ],
        compiler_params=pltpu.CompilerParams(collective_id=collective_id, has_side_effects=True),
    )(block)
    return out[0, :width]


def ray_axes(mesh):
    rays = mesh.shape["ray"]
    inner = 4 if rays % 4 == 0 else rays
    return ((inner, 1), (rays // inner, inner))


def allreduce_kernel(axes, x_hbm, o_hbm, x_ref, o_ref, part, rbuf1, acc1, rbuf2, load_sem, store_sems, send_sems, recv_sems):
    me = lax.axis_index("ray")
    tile = lax.axis_index("tile")
    rows = x_hbm.shape[0]
    half = x_hbm.shape[1] // 2
    w1 = half // axes[0][0]
    w2 = w1 // axes[1][0]

    def pos(axis):
        size, stride = axis
        return (me // stride) % size

    def peer(axis, k):
        size, stride = axis
        p = pos(axis)
        return (me + (((p - k + size) % size) - p) * stride, tile)

    def cols(start, width):
        return pl.ds(pl.multiple_of(start, 128), width)

    def add_rows(dst, a, b):
        def body(r, carry):
            block = pl.ds(pl.multiple_of(r * 8, 8), 8)
            dst[block, :] = a[block, :] + b[block, :]
            return carry
        lax.fori_loop(0, rows // 8, body, 0)

    load = pltpu.make_async_copy(x_hbm, x_ref, load_sem)
    load.start()
    barrier = pltpu.get_barrier_semaphore()
    greeted = 0
    for axis in axes:
        for k in range(1, axis[0]):
            pl.semaphore_signal(barrier, inc=1, device_id=peer(axis, k), device_id_type=MESH)
            greeted += 1
    pl.semaphore_wait(barrier, greeted)

    plans = [(axes[0], axes[1]), (axes[1], axes[0])]
    sends = []

    def send(stage, h, d, s, axis, src, dst, landing):
        size = axis[0]
        k = size - 1 if d == 0 else 1
        sems = dict(send_sem=send_sems.at[stage, h, d, s], recv_sem=recv_sems.at[stage, h, d, s],
                    device_id=peer(axis, k), device_id_type=MESH)
        copy = pltpu.make_async_remote_copy(src_ref=src, dst_ref=dst, **sems)
        copy.start()
        sends.append(copy)
        return pltpu.make_async_remote_copy(src_ref=src, dst_ref=landing, **sems)

    def reduce_scatter(stage, segs, rbuf, acc, first):
        steps = segs[0][0][0] - 1
        for s in range(steps):
            waits = []
            for h, (axis, own, final) in enumerate(segs):
                size, p = axis[0], pos(axis)
                for d in range(2):
                    sign = 1 if d == 0 else -1
                    src = first[h]((p - sign * (s + 1) + 2 * size) % size, d) if s == 0 else acc.at[h, d, s - 1]
                    waits.append((h, d, send(stage, h, d, s, axis, src, rbuf.at[h, d, s], rbuf.at[h, d, s])))
            for h, d, copy in waits:
                copy.wait_recv()
            if s == 0:
                load.wait()
            for h, (axis, own, final) in enumerate(segs):
                size, p = axis[0], pos(axis)
                for d in range(2):
                    sign = 1 if d == 0 else -1
                    mine = own((p - sign * (s + 2) + 2 * size) % size, d)
                    dst = final(d) if s == steps - 1 else acc.at[h, d, s]
                    add_rows(dst, rbuf.at[h, d, s], mine)

    def all_gather(stage, segs):
        steps = segs[0][0][0] - 1
        for s in range(steps):
            waits = []
            for h, (axis, region) in enumerate(segs):
                size, p = axis[0], pos(axis)
                for d in range(2):
                    sign = 1 if d == 0 else -1
                    src = region((p - sign * s + 2 * size) % size, d)
                    landing = region((p - sign * (s + 1) + 2 * size) % size, d)
                    waits.append(send(stage, h, d, s, axis, src, src, landing))
            for copy in waits:
                copy.wait_recv()
            for h, (axis, region) in enumerate(segs):
                size, p = axis[0], pos(axis)
                for d in range(2):
                    sign = 1 if d == 0 else -1
                    store(h, (p - sign * (s + 1) + 2 * size) % size, d)

    def direct_reduce_scatter(stage, segs, rbuf, width):
        waits = []
        for h, (axis, own, final) in enumerate(segs):
            size, p = axis[0], pos(axis)
            for k in range(1, size):
                slot = rbuf.at[h, k - 1]
                copy = pltpu.make_async_remote_copy(
                    src_ref=own((p - k + size) % size), dst_ref=slot,
                    send_sem=send_sems.at[stage, h, 0, k - 1], recv_sem=recv_sems.at[stage, h, 0, k - 1],
                    device_id=peer(axis, k), device_id_type=MESH)
                copy.start()
                sends.append(copy)
                waits.append(copy)
        for copy in waits:
            copy.wait_recv()
        for h, (axis, own, final) in enumerate(segs):
            size, p = axis[0], pos(axis)
            def body(r, carry, h=h, size=size, p=p, own=own, final=final):
                block = pl.ds(pl.multiple_of(r * 8, 8), 8)
                total = None
                for q in range(size):
                    k = (q - p + size) % size
                    mine = own(p)[block, :]
                    other = rbuf[h, jnp.maximum(k - 1, 0), block, :]
                    val = jnp.where(k == 0, mine, other)
                    total = val if total is None else total + val
                final[block, :] = total
                return carry
            lax.fori_loop(0, rows // 8, body, 0)

    def direct_all_gather(stage, segs):
        waits = []
        for h, (axis, region) in enumerate(segs):
            size, p = axis[0], pos(axis)
            for k in range(1, size):
                copy = pltpu.make_async_remote_copy(
                    src_ref=region(p), dst_ref=region(p),
                    send_sem=send_sems.at[stage, h, 0, k - 1], recv_sem=recv_sems.at[stage, h, 0, k - 1],
                    device_id=peer(axis, k), device_id_type=MESH)
                copy.start()
                sends.append(copy)
                waits.append(pltpu.make_async_remote_copy(
                    src_ref=region(p), dst_ref=region((p + k) % size),
                    send_sem=send_sems.at[stage, h, 0, k - 1], recv_sem=recv_sems.at[stage, h, 0, k - 1],
                    device_id=peer(axis, k), device_id_type=MESH))
        for copy in waits:
            copy.wait_recv()

    q1, q2 = w1 // 2, w2 // 2
    stores = []

    def store(h, j, d):
        region = cols(h * half + j * w1 + d * q1, q1)
        copy = pltpu.make_async_copy(o_ref.at[:, region], o_hbm.at[:, region], store_sems.at[h, j, d])
        copy.start()
        stores.append(copy)
    seg1, seg2, seg3, seg4 = [], [], [], []
    for h, (a1, a2) in enumerate(plans):
        p1, p2 = pos(a1), pos(a2)
        base = h * half + p1 * w1
        seg1.append((a1,
                     lambda j, d, h=h: x_ref.at[:, cols(h * half + j * w1 + d * q1, q1)],
                     lambda d, h=h: part.at[h, :, cols(d * q1, q1)]))
        seg2.append((a2,
                     lambda j, h=h: part.at[h, :, cols(j * w2, w2)],
                     o_ref.at[:, cols(base + p2 * w2, w2)]))
        seg3.append((a2, lambda j, base=base: o_ref.at[:, cols(base + j * w2, w2)]))
        seg4.append((a1, lambda j, d, h=h: o_ref.at[:, cols(h * half + j * w1 + d * q1, q1)]))
    firsts = [lambda j, d, h=h: x_hbm.at[:, cols(h * half + j * w1 + d * q1, q1)] for h in range(2)]
    reduce_scatter(0, seg1, rbuf1, acc1, firsts)
    direct_reduce_scatter(1, seg2, rbuf2, w2)
    direct_all_gather(2, seg3)
    for h, (a1, a2) in enumerate(plans):
        for d in range(2):
            store(h, pos(a1), d)
    all_gather(3, seg4)
    for copy in sends:
        copy.wait_send()
    for copy in stores:
        copy.wait()


def ray_allreduce(mesh, owned):
    axes = ray_axes(mesh)
    rows, width = owned.shape
    half = width // 2
    w1 = half // axes[0][0]
    w2 = w1 // axes[1][0]
    steps = max(axes[0][0], axes[1][0]) - 1
    return pl.pallas_call(
        functools.partial(allreduce_kernel, axes),
        out_shape=jax.ShapeDtypeStruct((rows, width), jnp.float32),
        in_specs=[pl.BlockSpec(memory_space=pl.ANY)],
        out_specs=pl.BlockSpec(memory_space=pl.ANY),
        scratch_shapes=[
            pltpu.VMEM((rows, width), jnp.float32),
            pltpu.VMEM((rows, width), jnp.float32),
            pltpu.VMEM((2, rows, w1), jnp.float32),
            pltpu.VMEM((2, 2, steps, rows, w1 // 2), jnp.float32),
            pltpu.VMEM((2, 2, steps, rows, w1 // 2), jnp.float32),
            pltpu.VMEM((2, steps, rows, w2), jnp.float32),
            pltpu.SemaphoreType.DMA(()),
            pltpu.SemaphoreType.DMA((2, axes[0][0], 2)),
            pltpu.SemaphoreType.DMA((4, 2, 2, steps)),
            pltpu.SemaphoreType.DMA((4, 2, 2, steps)),
        ],
        compiler_params=pltpu.CompilerParams(
            collective_id=2, has_side_effects=True, vmem_limit_bytes=60 * 1024 * 1024),
    )(owned)


eps_norm = 1e-06


def per_device(mesh, data, sensitivity, block_tiles, block_bundles):
    columns = data.shape[0]
    bundles = block_bundles.reshape(-1)
    requests = lax.all_to_all(block_tiles, "tile", split_axis=1, concat_axis=1, tiled=True).reshape(
        -1
    )
    bundle_onehot = (bundles[:, None] == jnp.arange(BUND_DEV, dtype=jnp.int32)[None, :]).astype(
        jnp.float32
    )
    owner_onehot = (requests[:, None] == jnp.arange(TILE_DEV, dtype=jnp.int32)[None, :]).astype(
        jnp.bfloat16
    )

    def fetch(field_bf):
        owned = field_bf.reshape(columns, TILE_DEV, CB)
        outgoing = jnp.take(owned, requests, axis=1, mode="clip")
        tiles = lax.all_to_all(outgoing, "tile", split_axis=1, concat_axis=1, tiled=True)
        return tiles

    def forward(field_bf):
        tiles = fetch(field_bf)
        partial_value = jnp.einsum(
            "cnk,nrk->ncr", tiles, sensitivity, preferred_element_type=jnp.float32
        )
        summed = jnp.einsum(
            "ncr,nb->cbr", partial_value, bundle_onehot, precision=lax.Precision.HIGHEST
        )
        return summed.reshape(columns, BUND_DEV * RB)

    def adjoint(rays_bf):
        picked = jnp.take(rays_bf.reshape(columns, BUND_DEV, RB), bundles, axis=1, mode="clip")
        terms = jnp.einsum(
            "cnr,nrk->cnk", picked, sensitivity, preferred_element_type=jnp.float32
        ).astype(jnp.bfloat16)
        arrived = lax.all_to_all(terms, "tile", split_axis=1, concat_axis=1, tiled=True)
        owned = jnp.einsum(
            "cnk,nt->ctk", arrived, owner_onehot, preferred_element_type=jnp.float32
        ).reshape(columns, TILE_DEV * CB)
        total = ray_allreduce(mesh, owned)
        return total

    def cell_norm(field):
        local = jnp.sum(field * field, axis=1)
        total = group_sum(mesh, ("tile",), 1, local)
        return jnp.sqrt(total + eps_norm)

    def ray_norm(rays):
        total = group_sum(mesh, ("ray", "tile"), 0, jnp.sum(rays * rays, axis=1))
        return jnp.sqrt(total + eps_norm)

    beta_now = ray_norm(data)
    rays_dir = data / beta_now[:, None]
    model_dir = adjoint(rays_dir.astype(jnp.bfloat16))
    alpha_now = cell_norm(model_dir)
    model_dir = model_dir / alpha_now[:, None]
    search = model_dir
    solution = jnp.zeros_like(model_dir)
    phi_bar = beta_now
    rho_bar = alpha_now
    for step in range(ITERS):
        rounded = model_dir.astype(jnp.bfloat16)
        rays_dir = forward(rounded) - alpha_now[:, None] * rays_dir
        beta_now = ray_norm(rays_dir)
        rays_dir = rays_dir / beta_now[:, None]
        rho_now = jnp.sqrt(rho_bar * rho_bar + beta_now * beta_now)
        cosine = rho_bar / rho_now
        sine_part = beta_now / rho_now
        phi_now = cosine * phi_bar
        phi_bar = sine_part * phi_bar
        solution = solution + (phi_now / rho_now)[:, None] * search
        if step + 1 < ITERS:
            model_dir = adjoint(rays_dir.astype(jnp.bfloat16)) - beta_now[:, None] * model_dir
            alpha_now = cell_norm(model_dir)
            model_dir = model_dir / alpha_now[:, None]
            theta_now = sine_part * alpha_now
            rho_bar = -cosine * alpha_now
            search = model_dir - (theta_now / rho_now)[:, None] * search
    residual = data - forward(solution.astype(jnp.bfloat16))
    return (solution, residual)


def solution(mesh):
    return jax.shard_map(
        functools.partial(per_device, mesh),
        mesh=mesh,
        in_specs=(
            P(None, ("ray", "tile")),
            P(("ray", "tile"), None, None),
            P(("ray", "tile"), None, None),
            P(("ray", "tile"), None, None),
        ),
        out_specs=(P(None, "tile"), P(None, ("ray", "tile"))),
        check_vma=False,
    )
```

```python
import jax
import jax.numpy as jnp
from jax import lax
from jax.sharding import PartitionSpec as P

RB = 256
CB = 512
ITERS = 2
BUND_DEV = 8
TILE_DEV = 48


import functools
from jax.experimental import pallas as pl
from jax.experimental.pallas import tpu as pltpu

MESH = pl.DeviceIdType.MESH


def stage_plan(mesh, axes):
    plan = [(axis, mesh.shape[axis], 1) for axis in ("tile", "ray") if axis in axes]
    return tuple(stage for stage in plan if stage[1] > 1)


def reduce_kernel(plan, x_ref, o_ref, vals, send_sems, recv_sems):
    here = {"ray": lax.axis_index("ray"), "tile": lax.axis_index("tile")}

    def peer(axis, size, stride, k):
        idx = here[axis]
        pos = (idx // stride) % size
        other = idx + (((pos + k) % size) - pos) * stride
        coords = dict(here)
        coords[axis] = other
        return (coords["ray"], coords["tile"])

    barrier = pltpu.get_barrier_semaphore()
    count = 0
    for axis, size, stride in plan:
        def greet(k, carry, axis=axis, size=size, stride=stride):
            pl.semaphore_signal(barrier, inc=1, device_id=peer(axis, size, stride, k), device_id_type=MESH)
            return carry
        lax.fori_loop(1, size, greet, 0)
        count += size - 1
    pl.semaphore_wait(barrier, count)

    def copy_of(s, axis, size, stride, k):
        src = x_ref if s == 0 else vals.at[s, 0]
        return pltpu.make_async_remote_copy(
            src_ref=src,
            dst_ref=vals.at[s, k],
            send_sem=send_sems.at[s, k],
            recv_sem=recv_sems.at[s, k],
            device_id=peer(axis, size, stride, (size - k) % size),
            device_id_type=MESH,
        )

    for s, (axis, size, stride) in enumerate(plan):
        def start(k, carry, s=s, axis=axis, size=size, stride=stride):
            copy_of(s, axis, size, stride, k).start()
            return carry

        def arrive(k, carry, s=s, axis=axis, size=size, stride=stride):
            copy_of(s, axis, size, stride, k).wait_recv()
            return carry
        lax.fori_loop(1, size, start, 0)
        lax.fori_loop(1, size, arrive, 0)
        pos = (here[axis] // stride) % size
        own = x_ref[...] if s == 0 else vals[s, 0]
        total = jnp.where(pos == 0, own, vals[s, (size - pos) % size])
        for q in range(1, size):
            total = total + jnp.where(pos == q, own, vals[s, (q - pos + size) % size])
        if s + 1 < len(plan):
            vals[s + 1, 0] = total
        else:
            o_ref[...] = total
    for s, (axis, size, stride) in enumerate(plan):
        def sent(k, carry, s=s, axis=axis, size=size, stride=stride):
            copy_of(s, axis, size, stride, k).wait_send()
            return carry
        lax.fori_loop(1, size, sent, 0)


def group_sum(mesh, axes, collective_id, partial):
    plan = stage_plan(mesh, axes)
    width = partial.shape[0]
    block = jnp.zeros((8, 128), jnp.float32).at[0, :width].set(partial)
    depth = max(size for _, size, _ in plan)
    out = pl.pallas_call(
        functools.partial(reduce_kernel, plan),
        out_shape=jax.ShapeDtypeStruct((8, 128), jnp.float32),
        in_specs=[pl.BlockSpec(memory_space=pltpu.VMEM)],
        out_specs=pl.BlockSpec(memory_space=pltpu.VMEM),
        scratch_shapes=[
            pltpu.VMEM((len(plan), depth, 8, 128), jnp.float32),
            pltpu.SemaphoreType.DMA((len(plan), depth)),
            pltpu.SemaphoreType.DMA((len(plan), depth)),
        ],
        compiler_params=pltpu.CompilerParams(collective_id=collective_id, has_side_effects=True),
    )(block)
    return out[0, :width]


def ray_axes(mesh):
    rays = mesh.shape["ray"]
    inner = 4 if rays % 4 == 0 else rays
    return ((inner, 1), (rays // inner, inner))


def allreduce_kernel(axes, x_hbm, o_hbm, x_ref, o_ref, part, rbuf1, acc1, rbuf2, load_sem, store_sems, send_sems, recv_sems):
    me = lax.axis_index("ray")
    tile = lax.axis_index("tile")
    rows = x_hbm.shape[0]
    half = x_hbm.shape[1] // 2
    w1 = half // axes[0][0]
    w2 = w1 // axes[1][0]

    def pos(axis):
        size, stride = axis
        return (me // stride) % size

    def peer(axis, k):
        size, stride = axis
        p = pos(axis)
        return (me + (((p - k + size) % size) - p) * stride, tile)

    def cols(start, width):
        return pl.ds(pl.multiple_of(start, 128), width)

    def add_rows(dst, a, b):
        def body(r, carry):
            block = pl.ds(pl.multiple_of(r * 8, 8), 8)
            dst[block, :] = a[block, :] + b[block, :]
            return carry
        lax.fori_loop(0, rows // 8, body, 0)

    load = pltpu.make_async_copy(x_hbm, x_ref, load_sem)
    load.start()
    barrier = pltpu.get_barrier_semaphore()
    greeted = 0
    for axis in axes:
        for k in range(1, axis[0]):
            pl.semaphore_signal(barrier, inc=1, device_id=peer(axis, k), device_id_type=MESH)
            greeted += 1
    pl.semaphore_wait(barrier, greeted)

    plans = [(axes[0], axes[1]), (axes[1], axes[0])]
    sends = []

    def send(stage, h, d, s, axis, src, dst, landing):
        size = axis[0]
        k = size - 1 if d == 0 else 1
        sems = dict(send_sem=send_sems.at[stage, h, d, s], recv_sem=recv_sems.at[stage, h, d, s],
                    device_id=peer(axis, k), device_id_type=MESH)
        copy = pltpu.make_async_remote_copy(src_ref=src, dst_ref=dst, **sems)
        copy.start()
        sends.append(copy)
        return pltpu.make_async_remote_copy(src_ref=src, dst_ref=landing, **sems)

    def reduce_scatter(stage, segs, rbuf, acc, first):
        steps = segs[0][0][0] - 1
        for s in range(steps):
            waits = []
            for h, (axis, own, final) in enumerate(segs):
                size, p = axis[0], pos(axis)
                for d in range(2):
                    sign = 1 if d == 0 else -1
                    src = first[h]((p - sign * (s + 1) + 2 * size) % size, d) if s == 0 else acc.at[h, d, s - 1]
                    waits.append((h, d, send(stage, h, d, s, axis, src, rbuf.at[h, d, s], rbuf.at[h, d, s])))
            for h, d, copy in waits:
                copy.wait_recv()
            if s == 0:
                load.wait()
            for h, (axis, own, final) in enumerate(segs):
                size, p = axis[0], pos(axis)
                for d in range(2):
                    sign = 1 if d == 0 else -1
                    mine = own((p - sign * (s + 2) + 2 * size) % size, d)
                    dst = final(d) if s == steps - 1 else acc.at[h, d, s]
                    add_rows(dst, rbuf.at[h, d, s], mine)

    def all_gather(stage, segs):
        steps = segs[0][0][0] - 1
        for s in range(steps):
            waits = []
            for h, (axis, region) in enumerate(segs):
                size, p = axis[0], pos(axis)
                for d in range(2):
                    sign = 1 if d == 0 else -1
                    src = region((p - sign * s + 2 * size) % size, d)
                    landing = region((p - sign * (s + 1) + 2 * size) % size, d)
                    waits.append(send(stage, h, d, s, axis, src, src, landing))
            for copy in waits:
                copy.wait_recv()
            for h, (axis, region) in enumerate(segs):
                size, p = axis[0], pos(axis)
                for d in range(2):
                    sign = 1 if d == 0 else -1
                    store(h, (p - sign * (s + 1) + 2 * size) % size, d)

    def direct_reduce_scatter(stage, segs, rbuf, width):
        waits = []
        for h, (axis, own, final) in enumerate(segs):
            size, p = axis[0], pos(axis)
            for k in range(1, size):
                slot = rbuf.at[h, k - 1]
                copy = pltpu.make_async_remote_copy(
                    src_ref=own((p - k + size) % size), dst_ref=slot,
                    send_sem=send_sems.at[stage, h, 0, k - 1], recv_sem=recv_sems.at[stage, h, 0, k - 1],
                    device_id=peer(axis, k), device_id_type=MESH)
                copy.start()
                sends.append(copy)
                waits.append(copy)
        for copy in waits:
            copy.wait_recv()
        for h, (axis, own, final) in enumerate(segs):
            size, p = axis[0], pos(axis)
            def body(r, carry, h=h, size=size, p=p, own=own, final=final):
                block = pl.ds(pl.multiple_of(r * 8, 8), 8)
                total = None
                for q in range(size):
                    k = (q - p + size) % size
                    mine = own(p)[block, :]
                    other = rbuf[h, jnp.maximum(k - 1, 0), block, :]
                    val = jnp.where(k == 0, mine, other)
                    total = val if total is None else total + val
                final[block, :] = total
                return carry
            lax.fori_loop(0, rows // 8, body, 0)

    def direct_all_gather(stage, segs):
        waits = []
        for h, (axis, region) in enumerate(segs):
            size, p = axis[0], pos(axis)
            for k in range(1, size):
                copy = pltpu.make_async_remote_copy(
                    src_ref=region(p), dst_ref=region(p),
                    send_sem=send_sems.at[stage, h, 0, k - 1], recv_sem=recv_sems.at[stage, h, 0, k - 1],
                    device_id=peer(axis, k), device_id_type=MESH)
                copy.start()
                sends.append(copy)
                waits.append(pltpu.make_async_remote_copy(
                    src_ref=region(p), dst_ref=region((p + k) % size),
                    send_sem=send_sems.at[stage, h, 0, k - 1], recv_sem=recv_sems.at[stage, h, 0, k - 1],
                    device_id=peer(axis, k), device_id_type=MESH))
        for copy in waits:
            copy.wait_recv()

    q1, q2 = w1 // 2, w2 // 2
    stores = []

    def store(h, j, d):
        region = cols(h * half + j * w1 + d * q1, q1)
        copy = pltpu.make_async_copy(o_ref.at[:, region], o_hbm.at[:, region], store_sems.at[h, j, d])
        copy.start()
        stores.append(copy)
    seg1, seg2, seg3, seg4 = [], [], [], []
    for h, (a1, a2) in enumerate(plans):
        p1, p2 = pos(a1), pos(a2)
        base = h * half + p1 * w1
        seg1.append((a1,
                     lambda j, d, h=h: x_ref.at[:, cols(h * half + j * w1 + d * q1, q1)],
                     lambda d, h=h: part.at[h, :, cols(d * q1, q1)]))
        seg2.append((a2,
                     lambda j, h=h: part.at[h, :, cols(j * w2, w2)],
                     o_ref.at[:, cols(base + p2 * w2, w2)]))
        seg3.append((a2, lambda j, base=base: o_ref.at[:, cols(base + j * w2, w2)]))
        seg4.append((a1, lambda j, d, h=h: o_ref.at[:, cols(h * half + j * w1 + d * q1, q1)]))
    firsts = [lambda j, d, h=h: x_hbm.at[:, cols(h * half + j * w1 + d * q1, q1)] for h in range(2)]
    reduce_scatter(0, seg1, rbuf1, acc1, firsts)
    direct_reduce_scatter(1, seg2, rbuf2, w2)
    direct_all_gather(2, seg3)
    for h, (a1, a2) in enumerate(plans):
        for d in range(2):
            store(h, pos(a1), d)
    all_gather(3, seg4)
    for copy in sends:
        copy.wait_send()
    for copy in stores:
        copy.wait()


def ray_allreduce(mesh, owned):
    axes = ray_axes(mesh)
    rows, width = owned.shape
    half = width // 2
    w1 = half // axes[0][0]
    w2 = w1 // axes[1][0]
    steps = max(axes[0][0], axes[1][0]) - 1
    return pl.pallas_call(
        functools.partial(allreduce_kernel, axes),
        out_shape=jax.ShapeDtypeStruct((rows, width), jnp.float32),
        in_specs=[pl.BlockSpec(memory_space=pl.ANY)],
        out_specs=pl.BlockSpec(memory_space=pl.ANY),
        scratch_shapes=[
            pltpu.VMEM((rows, width), jnp.float32),
            pltpu.VMEM((rows, width), jnp.float32),
            pltpu.VMEM((2, rows, w1), jnp.float32),
            pltpu.VMEM((2, 2, steps, rows, w1 // 2), jnp.float32),
            pltpu.VMEM((2, 2, steps, rows, w1 // 2), jnp.float32),
            pltpu.VMEM((2, steps, rows, w2), jnp.float32),
            pltpu.SemaphoreType.DMA(()),
            pltpu.SemaphoreType.DMA((2, axes[0][0], 2)),
            pltpu.SemaphoreType.DMA((4, 2, 2, steps)),
            pltpu.SemaphoreType.DMA((4, 2, 2, steps)),
        ],
        compiler_params=pltpu.CompilerParams(
            collective_id=2, has_side_effects=True, vmem_limit_bytes=60 * 1024 * 1024),
    )(owned)


eps_norm = 1e-06


def per_device(mesh, data, sensitivity, block_tiles, block_bundles):
    columns = data.shape[0]
    bundles = block_bundles.reshape(-1)
    requests = lax.all_to_all(block_tiles, "tile", split_axis=1, concat_axis=1, tiled=True).reshape(
        -1
    )
    bundle_onehot = (bundles[:, None] == jnp.arange(BUND_DEV, dtype=jnp.int32)[None, :]).astype(
        jnp.float32
    )
    owner_onehot = (requests[:, None] == jnp.arange(TILE_DEV, dtype=jnp.int32)[None, :]).astype(
        jnp.bfloat16
    )

    def fetch(field_bf):
        owned = field_bf.reshape(columns, TILE_DEV, CB)
        outgoing = jnp.take(owned, requests, axis=1, mode="clip")
        tiles = lax.all_to_all(outgoing, "tile", split_axis=1, concat_axis=1, tiled=True)
        return tiles

    def forward(field_bf):
        tiles = fetch(field_bf)
        partial_value = jnp.einsum(
            "cnk,nrk->ncr", tiles, sensitivity, preferred_element_type=jnp.float32
        )
        hi_f = lax.reduce_precision(partial_value, exponent_bits=8, mantissa_bits=7)
        rest = partial_value - hi_f
        mid_f = lax.reduce_precision(rest, exponent_bits=8, mantissa_bits=7)
        hi, mid = hi_f.astype(jnp.bfloat16), mid_f.astype(jnp.bfloat16)
        lo = (rest - mid_f).astype(jnp.bfloat16)
        onehot_bf = bundle_onehot.astype(jnp.bfloat16)
        summed = sum(
            jnp.einsum("ncr,nb->cbr", part, onehot_bf, preferred_element_type=jnp.float32)
            for part in (hi, mid, lo)
        )
        return summed.reshape(columns, BUND_DEV * RB)

    def adjoint(rays_bf):
        picked = jnp.take(rays_bf.reshape(columns, BUND_DEV, RB), bundles, axis=1, mode="clip")
        terms = jnp.einsum(
            "cnr,nrk->cnk", picked, sensitivity, preferred_element_type=jnp.float32
        ).astype(jnp.bfloat16)
        arrived = lax.all_to_all(terms, "tile", split_axis=1, concat_axis=1, tiled=True)
        owned = jnp.einsum(
            "cnk,nt->ctk", arrived, owner_onehot, preferred_element_type=jnp.float32
        ).reshape(columns, TILE_DEV * CB)
        total = ray_allreduce(mesh, owned)
        return total

    def cell_norm(field):
        local = jnp.sum(field * field, axis=1)
        total = group_sum(mesh, ("tile",), 1, local)
        return jnp.sqrt(total + eps_norm)

    def ray_norm(rays):
        total = group_sum(mesh, ("ray", "tile"), 0, jnp.sum(rays * rays, axis=1))
        return jnp.sqrt(total + eps_norm)

    beta_now = ray_norm(data)
    rays_dir = data / beta_now[:, None]
    model_dir = adjoint(rays_dir.astype(jnp.bfloat16))
    alpha_now = cell_norm(model_dir)
    model_dir = model_dir / alpha_now[:, None]
    search = model_dir
    solution = jnp.zeros_like(model_dir)
    phi_bar = beta_now
    rho_bar = alpha_now
    for step in range(ITERS):
        rounded = model_dir.astype(jnp.bfloat16)
        rays_dir = forward(rounded) - alpha_now[:, None] * rays_dir
        beta_now = ray_norm(rays_dir)
        rays_dir = rays_dir / beta_now[:, None]
        rho_now = jnp.sqrt(rho_bar * rho_bar + beta_now * beta_now)
        cosine = rho_bar / rho_now
        sine_part = beta_now / rho_now
        phi_now = cosine * phi_bar
        phi_bar = sine_part * phi_bar
        solution = solution + (phi_now / rho_now)[:, None] * search
        if step + 1 < ITERS:
            model_dir = adjoint(rays_dir.astype(jnp.bfloat16)) - beta_now[:, None] * model_dir
            alpha_now = cell_norm(model_dir)
            model_dir = model_dir / alpha_now[:, None]
            theta_now = sine_part * alpha_now
            rho_bar = -cosine * alpha_now
            search = model_dir - (theta_now / rho_now)[:, None] * search
    residual = data - forward(solution.astype(jnp.bfloat16))
    return (solution, residual)


def solution(mesh):
    return jax.shard_map(
        functools.partial(per_device, mesh),
        mesh=mesh,
        in_specs=(
            P(None, ("ray", "tile")),
            P(("ray", "tile"), None, None),
            P(("ray", "tile"), None, None),
            P(("ray", "tile"), None, None),
        ),
        out_specs=(P(None, "tile"), P(None, ("ray", "tile"))),
        check_vma=False,
    )
```

```python
import jax
import jax.numpy as jnp
from jax import lax
from jax.sharding import PartitionSpec as P

RB = 256
CB = 512
ITERS = 2
BUND_DEV = 8
TILE_DEV = 48


import functools
from jax.experimental import pallas as pl
from jax.experimental.pallas import tpu as pltpu

MESH = pl.DeviceIdType.MESH


def stage_plan(mesh, axes):
    plan = [(axis, mesh.shape[axis], 1) for axis in ("tile", "ray") if axis in axes]
    return tuple(stage for stage in plan if stage[1] > 1)


def reduce_kernel(plan, x_ref, o_ref, vals, send_sems, recv_sems):
    here = {"ray": lax.axis_index("ray"), "tile": lax.axis_index("tile")}

    def peer(axis, size, stride, k):
        idx = here[axis]
        pos = (idx // stride) % size
        other = idx + (((pos + k) % size) - pos) * stride
        coords = dict(here)
        coords[axis] = other
        return (coords["ray"], coords["tile"])

    barrier = pltpu.get_barrier_semaphore()
    count = 0
    for axis, size, stride in plan:
        def greet(k, carry, axis=axis, size=size, stride=stride):
            pl.semaphore_signal(barrier, inc=1, device_id=peer(axis, size, stride, k), device_id_type=MESH)
            return carry
        lax.fori_loop(1, size, greet, 0)
        count += size - 1
    pl.semaphore_wait(barrier, count)

    def copy_of(s, axis, size, stride, k):
        src = x_ref if s == 0 else vals.at[s, 0]
        return pltpu.make_async_remote_copy(
            src_ref=src,
            dst_ref=vals.at[s, k],
            send_sem=send_sems.at[s, k],
            recv_sem=recv_sems.at[s, k],
            device_id=peer(axis, size, stride, (size - k) % size),
            device_id_type=MESH,
        )

    for s, (axis, size, stride) in enumerate(plan):
        def start(k, carry, s=s, axis=axis, size=size, stride=stride):
            copy_of(s, axis, size, stride, k).start()
            return carry

        def arrive(k, carry, s=s, axis=axis, size=size, stride=stride):
            copy_of(s, axis, size, stride, k).wait_recv()
            return carry
        lax.fori_loop(1, size, start, 0)
        lax.fori_loop(1, size, arrive, 0)
        pos = (here[axis] // stride) % size
        own = x_ref[...] if s == 0 else vals[s, 0]
        total = jnp.where(pos == 0, own, vals[s, (size - pos) % size])
        for q in range(1, size):
            total = total + jnp.where(pos == q, own, vals[s, (q - pos + size) % size])
        if s + 1 < len(plan):
            vals[s + 1, 0] = total
        else:
            o_ref[...] = total
    for s, (axis, size, stride) in enumerate(plan):
        def sent(k, carry, s=s, axis=axis, size=size, stride=stride):
            copy_of(s, axis, size, stride, k).wait_send()
            return carry
        lax.fori_loop(1, size, sent, 0)


def group_sum(mesh, axes, collective_id, partial):
    plan = stage_plan(mesh, axes)
    width = partial.shape[0]
    block = jnp.zeros((8, 128), jnp.float32).at[0, :width].set(partial)
    depth = max(size for _, size, _ in plan)
    out = pl.pallas_call(
        functools.partial(reduce_kernel, plan),
        out_shape=jax.ShapeDtypeStruct((8, 128), jnp.float32),
        in_specs=[pl.BlockSpec(memory_space=pltpu.VMEM)],
        out_specs=pl.BlockSpec(memory_space=pltpu.VMEM),
        scratch_shapes=[
            pltpu.VMEM((len(plan), depth, 8, 128), jnp.float32),
            pltpu.SemaphoreType.DMA((len(plan), depth)),
            pltpu.SemaphoreType.DMA((len(plan), depth)),
        ],
        compiler_params=pltpu.CompilerParams(collective_id=collective_id, has_side_effects=True),
    )(block)
    return out[0, :width]


def ray_axes(mesh):
    rays = mesh.shape["ray"]
    inner = 4 if rays % 4 == 0 else rays
    return ((inner, 1), (rays // inner, inner))


def allreduce_kernel(axes, x_hbm, o_hbm, x_ref, o_ref, part, rbuf1, acc1, rbuf2, load_sem, store_sems, send_sems, recv_sems):
    me = lax.axis_index("ray")
    tile = lax.axis_index("tile")
    rows = x_hbm.shape[0]
    half = x_hbm.shape[1] // 2
    w1 = half // axes[0][0]
    w2 = w1 // axes[1][0]

    def pos(axis):
        size, stride = axis
        return (me // stride) % size

    def peer(axis, k):
        size, stride = axis
        p = pos(axis)
        return (me + (((p - k + size) % size) - p) * stride, tile)

    def cols(start, width):
        return pl.ds(pl.multiple_of(start, 128), width)

    def add_rows(dst, a, b):
        def body(r, carry):
            block = pl.ds(pl.multiple_of(r * 8, 8), 8)
            dst[block, :] = a[block, :] + b[block, :]
            return carry
        lax.fori_loop(0, rows // 8, body, 0)

    load = pltpu.make_async_copy(x_hbm, x_ref, load_sem)
    load.start()
    barrier = pltpu.get_barrier_semaphore()
    greeted = 0
    for axis in axes:
        for k in range(1, axis[0]):
            pl.semaphore_signal(barrier, inc=1, device_id=peer(axis, k), device_id_type=MESH)
            greeted += 1
    pl.semaphore_wait(barrier, greeted)

    plans = [(axes[0], axes[1]), (axes[1], axes[0])]
    sends = []

    def send(stage, h, d, s, axis, src, dst, landing):
        size = axis[0]
        k = size - 1 if d == 0 else 1
        sems = dict(send_sem=send_sems.at[stage, h, d, s], recv_sem=recv_sems.at[stage, h, d, s],
                    device_id=peer(axis, k), device_id_type=MESH)
        copy = pltpu.make_async_remote_copy(src_ref=src, dst_ref=dst, **sems)
        copy.start()
        sends.append(copy)
        return pltpu.make_async_remote_copy(src_ref=src, dst_ref=landing, **sems)

    def reduce_scatter(stage, segs, rbuf, acc, first):
        steps = segs[0][0][0] - 1
        for s in range(steps):
            waits = []
            for h, (axis, own, final) in enumerate(segs):
                size, p = axis[0], pos(axis)
                for d in range(2):
                    sign = 1 if d == 0 else -1
                    src = first[h]((p - sign * (s + 1) + 2 * size) % size, d) if s == 0 else acc.at[h, d, s - 1]
                    waits.append((h, d, send(stage, h, d, s, axis, src, rbuf.at[h, d, s], rbuf.at[h, d, s])))
            for h, d, copy in waits:
                copy.wait_recv()
            if s == 0:
                load.wait()
            for h, (axis, own, final) in enumerate(segs):
                size, p = axis[0], pos(axis)
                for d in range(2):
                    sign = 1 if d == 0 else -1
                    mine = own((p - sign * (s + 2) + 2 * size) % size, d)
                    dst = final(d) if s == steps - 1 else acc.at[h, d, s]
                    add_rows(dst, rbuf.at[h, d, s], mine)

    def all_gather(stage, segs):
        steps = segs[0][0][0] - 1
        for s in range(steps):
            waits = []
            for h, (axis, region) in enumerate(segs):
                size, p = axis[0], pos(axis)
                for d in range(2):
                    sign = 1 if d == 0 else -1
                    src = region((p - sign * s + 2 * size) % size, d)
                    landing = region((p - sign * (s + 1) + 2 * size) % size, d)
                    waits.append(send(stage, h, d, s, axis, src, src, landing))
            for copy in waits:
                copy.wait_recv()
            for h, (axis, region) in enumerate(segs):
                size, p = axis[0], pos(axis)
                for d in range(2):
                    sign = 1 if d == 0 else -1
                    store(h, (p - sign * (s + 1) + 2 * size) % size, d)

    def direct_reduce_scatter(stage, segs, rbuf, width):
        waits = []
        for h, (axis, own, final) in enumerate(segs):
            size, p = axis[0], pos(axis)
            for k in range(1, size):
                slot = rbuf.at[h, k - 1]
                copy = pltpu.make_async_remote_copy(
                    src_ref=own((p - k + size) % size), dst_ref=slot,
                    send_sem=send_sems.at[stage, h, 0, k - 1], recv_sem=recv_sems.at[stage, h, 0, k - 1],
                    device_id=peer(axis, k), device_id_type=MESH)
                copy.start()
                sends.append(copy)
                waits.append(copy)
        for copy in waits:
            copy.wait_recv()
        for h, (axis, own, final) in enumerate(segs):
            size, p = axis[0], pos(axis)
            def body(r, carry, h=h, size=size, p=p, own=own, final=final):
                block = pl.ds(pl.multiple_of(r * 8, 8), 8)
                total = None
                for q in range(size):
                    k = (q - p + size) % size
                    mine = own(p)[block, :]
                    other = rbuf[h, jnp.maximum(k - 1, 0), block, :]
                    val = jnp.where(k == 0, mine, other)
                    total = val if total is None else total + val
                final[block, :] = total
                return carry
            lax.fori_loop(0, rows // 8, body, 0)

    def direct_all_gather(stage, segs):
        waits = []
        for h, (axis, region) in enumerate(segs):
            size, p = axis[0], pos(axis)
            for k in range(1, size):
                copy = pltpu.make_async_remote_copy(
                    src_ref=region(p), dst_ref=region(p),
                    send_sem=send_sems.at[stage, h, 0, k - 1], recv_sem=recv_sems.at[stage, h, 0, k - 1],
                    device_id=peer(axis, k), device_id_type=MESH)
                copy.start()
                sends.append(copy)
                waits.append(pltpu.make_async_remote_copy(
                    src_ref=region(p), dst_ref=region((p + k) % size),
                    send_sem=send_sems.at[stage, h, 0, k - 1], recv_sem=recv_sems.at[stage, h, 0, k - 1],
                    device_id=peer(axis, k), device_id_type=MESH))
        for copy in waits:
            copy.wait_recv()

    q1, q2 = w1 // 2, w2 // 2
    stores = []

    def store(h, j, d):
        region = cols(h * half + j * w1 + d * q1, q1)
        copy = pltpu.make_async_copy(o_ref.at[:, region], o_hbm.at[:, region], store_sems.at[h, j, d])
        copy.start()
        stores.append(copy)
    seg1, seg2, seg3, seg4 = [], [], [], []
    for h, (a1, a2) in enumerate(plans):
        p1, p2 = pos(a1), pos(a2)
        base = h * half + p1 * w1
        seg1.append((a1,
                     lambda j, d, h=h: x_ref.at[:, cols(h * half + j * w1 + d * q1, q1)],
                     lambda d, h=h: part.at[h, :, cols(d * q1, q1)]))
        seg2.append((a2,
                     lambda j, h=h: part.at[h, :, cols(j * w2, w2)],
                     o_ref.at[:, cols(base + p2 * w2, w2)]))
        seg3.append((a2, lambda j, base=base: o_ref.at[:, cols(base + j * w2, w2)]))
        seg4.append((a1, lambda j, d, h=h: o_ref.at[:, cols(h * half + j * w1 + d * q1, q1)]))
    firsts = [lambda j, d, h=h: x_hbm.at[:, cols(h * half + j * w1 + d * q1, q1)] for h in range(2)]
    reduce_scatter(0, seg1, rbuf1, acc1, firsts)
    direct_reduce_scatter(1, seg2, rbuf2, w2)
    direct_all_gather(2, seg3)
    for h, (a1, a2) in enumerate(plans):
        for d in range(2):
            store(h, pos(a1), d)
    all_gather(3, seg4)
    for copy in sends:
        copy.wait_send()
    for copy in stores:
        copy.wait()


def ray_allreduce(mesh, owned):
    axes = ray_axes(mesh)
    rows, width = owned.shape
    half = width // 2
    w1 = half // axes[0][0]
    w2 = w1 // axes[1][0]
    steps = max(axes[0][0], axes[1][0]) - 1
    return pl.pallas_call(
        functools.partial(allreduce_kernel, axes),
        out_shape=jax.ShapeDtypeStruct((rows, width), jnp.float32),
        in_specs=[pl.BlockSpec(memory_space=pl.ANY)],
        out_specs=pl.BlockSpec(memory_space=pl.ANY),
        scratch_shapes=[
            pltpu.VMEM((rows, width), jnp.float32),
            pltpu.VMEM((rows, width), jnp.float32),
            pltpu.VMEM((2, rows, w1), jnp.float32),
            pltpu.VMEM((2, 2, steps, rows, w1 // 2), jnp.float32),
            pltpu.VMEM((2, 2, steps, rows, w1 // 2), jnp.float32),
            pltpu.VMEM((2, steps, rows, w2), jnp.float32),
            pltpu.SemaphoreType.DMA(()),
            pltpu.SemaphoreType.DMA((2, axes[0][0], 2)),
            pltpu.SemaphoreType.DMA((4, 2, 2, steps)),
            pltpu.SemaphoreType.DMA((4, 2, 2, steps)),
        ],
        compiler_params=pltpu.CompilerParams(
            collective_id=2, has_side_effects=True, vmem_limit_bytes=32 * 1024 * 1024),
    )(owned)


eps_norm = 1e-06


def per_device(mesh, data, sensitivity, block_tiles, block_bundles):
    columns = data.shape[0]
    bundles = block_bundles.reshape(-1)
    requests = lax.all_to_all(block_tiles, "tile", split_axis=1, concat_axis=1, tiled=True).reshape(
        -1
    )
    bundle_onehot = (bundles[:, None] == jnp.arange(BUND_DEV, dtype=jnp.int32)[None, :]).astype(
        jnp.float32
    )
    owner_onehot = (requests[:, None] == jnp.arange(TILE_DEV, dtype=jnp.int32)[None, :]).astype(
        jnp.bfloat16
    )

    def fetch(field_bf):
        owned = field_bf.reshape(columns, TILE_DEV, CB)
        outgoing = jnp.take(owned, requests, axis=1, mode="clip")
        tiles = lax.all_to_all(outgoing, "tile", split_axis=1, concat_axis=1, tiled=True)
        return tiles

    def forward(field_bf):
        tiles = fetch(field_bf)
        partial_value = jnp.einsum(
            "cnk,nrk->ncr", tiles, sensitivity, preferred_element_type=jnp.float32
        )
        summed = jnp.einsum(
            "ncr,nb->cbr", partial_value, bundle_onehot, precision=lax.Precision.HIGHEST
        )
        return summed.reshape(columns, BUND_DEV * RB)

    def adjoint(rays_bf):
        picked = jnp.take(rays_bf.reshape(columns, BUND_DEV, RB), bundles, axis=1, mode="clip")
        terms = jnp.einsum(
            "cnr,nrk->cnk", picked, sensitivity, preferred_element_type=jnp.float32
        ).astype(jnp.bfloat16)
        arrived = lax.all_to_all(terms, "tile", split_axis=1, concat_axis=1, tiled=True)
        owned = jnp.einsum(
            "cnk,nt->ctk", arrived, owner_onehot, preferred_element_type=jnp.float32
        ).reshape(columns, TILE_DEV * CB)
        total = ray_allreduce(mesh, owned)
        return total

    def cell_norm(field):
        local = jnp.sum(field * field, axis=1)
        total = group_sum(mesh, ("tile",), 1, local)
        return jnp.sqrt(total + eps_norm)

    def ray_norm(rays):
        total = group_sum(mesh, ("ray", "tile"), 0, jnp.sum(rays * rays, axis=1))
        return jnp.sqrt(total + eps_norm)

    beta_now = ray_norm(data)
    rays_dir = data / beta_now[:, None]
    model_dir = adjoint(rays_dir.astype(jnp.bfloat16))
    alpha_now = cell_norm(model_dir)
    model_dir = model_dir / alpha_now[:, None]
    search = model_dir
    solution = jnp.zeros_like(model_dir)
    phi_bar = beta_now
    rho_bar = alpha_now
    for step in range(ITERS):
        rounded = model_dir.astype(jnp.bfloat16)
        rays_dir = forward(rounded) - alpha_now[:, None] * rays_dir
        beta_now = ray_norm(rays_dir)
        rays_dir = rays_dir / beta_now[:, None]
        rho_now = jnp.sqrt(rho_bar * rho_bar + beta_now * beta_now)
        cosine = rho_bar / rho_now
        sine_part = beta_now / rho_now
        phi_now = cosine * phi_bar
        phi_bar = sine_part * phi_bar
        solution = solution + (phi_now / rho_now)[:, None] * search
        if step + 1 < ITERS:
            model_dir = adjoint(rays_dir.astype(jnp.bfloat16)) - beta_now[:, None] * model_dir
            alpha_now = cell_norm(model_dir)
            model_dir = model_dir / alpha_now[:, None]
            theta_now = sine_part * alpha_now
            rho_bar = -cosine * alpha_now
            search = model_dir - (theta_now / rho_now)[:, None] * search
    residual = data - forward(solution.astype(jnp.bfloat16))
    return (solution, residual)


def solution(mesh):
    return jax.shard_map(
        functools.partial(per_device, mesh),
        mesh=mesh,
        in_specs=(
            P(None, ("ray", "tile")),
            P(("ray", "tile"), None, None),
            P(("ray", "tile"), None, None),
            P(("ray", "tile"), None, None),
        ),
        out_specs=(P(None, "tile"), P(None, ("ray", "tile"))),
        check_vma=False,
    )
```

```python
import jax
import jax.numpy as jnp
from jax import lax
from jax.sharding import PartitionSpec as P

RB = 256
CB = 512
ITERS = 2
BUND_DEV = 8
TILE_DEV = 48


import functools
from jax.experimental import pallas as pl
from jax.experimental.pallas import tpu as pltpu

MESH = pl.DeviceIdType.MESH


def stage_plan(mesh, axes):
    plan = [(axis, mesh.shape[axis], 1) for axis in ("tile", "ray") if axis in axes]
    return tuple(stage for stage in plan if stage[1] > 1)


def reduce_kernel(plan, x_ref, o_ref, vals, send_sems, recv_sems):
    here = {"ray": lax.axis_index("ray"), "tile": lax.axis_index("tile")}

    def peer(axis, size, stride, k):
        idx = here[axis]
        pos = (idx // stride) % size
        other = idx + (((pos + k) % size) - pos) * stride
        coords = dict(here)
        coords[axis] = other
        return (coords["ray"], coords["tile"])

    barrier = pltpu.get_barrier_semaphore()
    count = 0
    for axis, size, stride in plan:
        def greet(k, carry, axis=axis, size=size, stride=stride):
            pl.semaphore_signal(barrier, inc=1, device_id=peer(axis, size, stride, k), device_id_type=MESH)
            return carry
        lax.fori_loop(1, size, greet, 0)
        count += size - 1
    pl.semaphore_wait(barrier, count)

    def copy_of(s, axis, size, stride, k):
        src = x_ref if s == 0 else vals.at[s, 0]
        return pltpu.make_async_remote_copy(
            src_ref=src,
            dst_ref=vals.at[s, k],
            send_sem=send_sems.at[s, k],
            recv_sem=recv_sems.at[s, k],
            device_id=peer(axis, size, stride, (size - k) % size),
            device_id_type=MESH,
        )

    for s, (axis, size, stride) in enumerate(plan):
        def start(k, carry, s=s, axis=axis, size=size, stride=stride):
            copy_of(s, axis, size, stride, k).start()
            return carry

        def arrive(k, carry, s=s, axis=axis, size=size, stride=stride):
            copy_of(s, axis, size, stride, k).wait_recv()
            return carry
        lax.fori_loop(1, size, start, 0)
        lax.fori_loop(1, size, arrive, 0)
        pos = (here[axis] // stride) % size
        own = x_ref[...] if s == 0 else vals[s, 0]
        total = jnp.where(pos == 0, own, vals[s, (size - pos) % size])
        for q in range(1, size):
            total = total + jnp.where(pos == q, own, vals[s, (q - pos + size) % size])
        if s + 1 < len(plan):
            vals[s + 1, 0] = total
        else:
            o_ref[...] = total
    for s, (axis, size, stride) in enumerate(plan):
        def sent(k, carry, s=s, axis=axis, size=size, stride=stride):
            copy_of(s, axis, size, stride, k).wait_send()
            return carry
        lax.fori_loop(1, size, sent, 0)


def group_sum(mesh, axes, collective_id, partial):
    plan = stage_plan(mesh, axes)
    width = partial.shape[0]
    block = jnp.zeros((8, 128), jnp.float32).at[0, :width].set(partial)
    depth = max(size for _, size, _ in plan)
    out = pl.pallas_call(
        functools.partial(reduce_kernel, plan),
        out_shape=jax.ShapeDtypeStruct((8, 128), jnp.float32),
        in_specs=[pl.BlockSpec(memory_space=pltpu.VMEM)],
        out_specs=pl.BlockSpec(memory_space=pltpu.VMEM),
        scratch_shapes=[
            pltpu.VMEM((len(plan), depth, 8, 128), jnp.float32),
            pltpu.SemaphoreType.DMA((len(plan), depth)),
            pltpu.SemaphoreType.DMA((len(plan), depth)),
        ],
        compiler_params=pltpu.CompilerParams(collective_id=collective_id, has_side_effects=True, vmem_limit_bytes=1024 * 1024),
    )(block)
    return out[0, :width]


def ray_axes(mesh):
    rays = mesh.shape["ray"]
    inner = 4 if rays % 4 == 0 else rays
    return ((inner, 1), (rays // inner, inner))


def allreduce_kernel(axes, x_hbm, o_hbm, x_ref, o_ref, part, rbuf1, acc1, rbuf2, load_sem, store_sems, send_sems, recv_sems):
    me = lax.axis_index("ray")
    tile = lax.axis_index("tile")
    rows = x_hbm.shape[0]
    half = x_hbm.shape[1] // 2
    w1 = half // axes[0][0]
    w2 = w1 // axes[1][0]

    def pos(axis):
        size, stride = axis
        return (me // stride) % size

    def peer(axis, k):
        size, stride = axis
        p = pos(axis)
        return (me + (((p - k + size) % size) - p) * stride, tile)

    def cols(start, width):
        return pl.ds(pl.multiple_of(start, 128), width)

    def add_rows(dst, a, b):
        def body(r, carry):
            block = pl.ds(pl.multiple_of(r * 8, 8), 8)
            dst[block, :] = a[block, :] + b[block, :]
            return carry
        lax.fori_loop(0, rows // 8, body, 0)

    load = pltpu.make_async_copy(x_hbm, x_ref, load_sem)
    load.start()
    barrier = pltpu.get_barrier_semaphore()
    greeted = 0
    for axis in axes:
        for k in range(1, axis[0]):
            pl.semaphore_signal(barrier, inc=1, device_id=peer(axis, k), device_id_type=MESH)
            greeted += 1
    pl.semaphore_wait(barrier, greeted)

    plans = [(axes[0], axes[1]), (axes[1], axes[0])]
    sends = []

    def send(stage, h, d, s, axis, src, dst, landing):
        size = axis[0]
        k = size - 1 if d == 0 else 1
        sems = dict(send_sem=send_sems.at[stage, h, d, s], recv_sem=recv_sems.at[stage, h, d, s],
                    device_id=peer(axis, k), device_id_type=MESH)
        copy = pltpu.make_async_remote_copy(src_ref=src, dst_ref=dst, **sems)
        copy.start()
        sends.append(copy)
        return pltpu.make_async_remote_copy(src_ref=src, dst_ref=landing, **sems)

    def reduce_scatter(stage, segs, rbuf, acc, first):
        steps = segs[0][0][0] - 1
        for s in range(steps):
            waits = []
            for h, (axis, own, final) in enumerate(segs):
                size, p = axis[0], pos(axis)
                for d in range(2):
                    sign = 1 if d == 0 else -1
                    src = first[h]((p - sign * (s + 1) + 2 * size) % size, d) if s == 0 else acc.at[h, d, s - 1]
                    waits.append((h, d, send(stage, h, d, s, axis, src, rbuf.at[h, d, s], rbuf.at[h, d, s])))
            for h, d, copy in waits:
                copy.wait_recv()
            if s == 0:
                load.wait()
            for h, (axis, own, final) in enumerate(segs):
                size, p = axis[0], pos(axis)
                for d in range(2):
                    sign = 1 if d == 0 else -1
                    mine = own((p - sign * (s + 2) + 2 * size) % size, d)
                    dst = final(d) if s == steps - 1 else acc.at[h, d, s]
                    add_rows(dst, rbuf.at[h, d, s], mine)

    def all_gather(stage, segs):
        steps = segs[0][0][0] - 1
        for s in range(steps):
            waits = []
            for h, (axis, region) in enumerate(segs):
                size, p = axis[0], pos(axis)
                for d in range(2):
                    sign = 1 if d == 0 else -1
                    src = region((p - sign * s + 2 * size) % size, d)
                    landing = region((p - sign * (s + 1) + 2 * size) % size, d)
                    waits.append(send(stage, h, d, s, axis, src, src, landing))
            for copy in waits:
                copy.wait_recv()
            for h, (axis, region) in enumerate(segs):
                size, p = axis[0], pos(axis)
                for d in range(2):
                    sign = 1 if d == 0 else -1
                    store(h, (p - sign * (s + 1) + 2 * size) % size, d)

    def direct_reduce_scatter(stage, segs, rbuf, width):
        waits = []
        for h, (axis, own, final) in enumerate(segs):
            size, p = axis[0], pos(axis)
            for k in range(1, size):
                slot = rbuf.at[h, k - 1]
                copy = pltpu.make_async_remote_copy(
                    src_ref=own((p - k + size) % size), dst_ref=slot,
                    send_sem=send_sems.at[stage, h, 0, k - 1], recv_sem=recv_sems.at[stage, h, 0, k - 1],
                    device_id=peer(axis, k), device_id_type=MESH)
                copy.start()
                sends.append(copy)
                waits.append(copy)
        for copy in waits:
            copy.wait_recv()
        for h, (axis, own, final) in enumerate(segs):
            size, p = axis[0], pos(axis)
            def body(r, carry, h=h, size=size, p=p, own=own, final=final):
                block = pl.ds(pl.multiple_of(r * 8, 8), 8)
                total = None
                for q in range(size):
                    k = (q - p + size) % size
                    mine = own(p)[block, :]
                    other = rbuf[h, jnp.maximum(k - 1, 0), block, :]
                    val = jnp.where(k == 0, mine, other)
                    total = val if total is None else total + val
                final[block, :] = total
                return carry
            lax.fori_loop(0, rows // 8, body, 0)

    def direct_all_gather(stage, segs):
        waits = []
        for h, (axis, region) in enumerate(segs):
            size, p = axis[0], pos(axis)
            for k in range(1, size):
                copy = pltpu.make_async_remote_copy(
                    src_ref=region(p), dst_ref=region(p),
                    send_sem=send_sems.at[stage, h, 0, k - 1], recv_sem=recv_sems.at[stage, h, 0, k - 1],
                    device_id=peer(axis, k), device_id_type=MESH)
                copy.start()
                sends.append(copy)
                waits.append(pltpu.make_async_remote_copy(
                    src_ref=region(p), dst_ref=region((p + k) % size),
                    send_sem=send_sems.at[stage, h, 0, k - 1], recv_sem=recv_sems.at[stage, h, 0, k - 1],
                    device_id=peer(axis, k), device_id_type=MESH))
        for copy in waits:
            copy.wait_recv()

    q1, q2 = w1 // 2, w2 // 2
    stores = []

    def store(h, j, d):
        region = cols(h * half + j * w1 + d * q1, q1)
        copy = pltpu.make_async_copy(o_ref.at[:, region], o_hbm.at[:, region], store_sems.at[h, j, d])
        copy.start()
        stores.append(copy)
    seg1, seg2, seg3, seg4 = [], [], [], []
    for h, (a1, a2) in enumerate(plans):
        p1, p2 = pos(a1), pos(a2)
        base = h * half + p1 * w1
        seg1.append((a1,
                     lambda j, d, h=h: x_ref.at[:, cols(h * half + j * w1 + d * q1, q1)],
                     lambda d, h=h: part.at[h, :, cols(d * q1, q1)]))
        seg2.append((a2,
                     lambda j, h=h: part.at[h, :, cols(j * w2, w2)],
                     o_ref.at[:, cols(base + p2 * w2, w2)]))
        seg3.append((a2, lambda j, base=base: o_ref.at[:, cols(base + j * w2, w2)]))
        seg4.append((a1, lambda j, d, h=h: o_ref.at[:, cols(h * half + j * w1 + d * q1, q1)]))
    firsts = [lambda j, d, h=h: x_hbm.at[:, cols(h * half + j * w1 + d * q1, q1)] for h in range(2)]
    reduce_scatter(0, seg1, rbuf1, acc1, firsts)
    direct_reduce_scatter(1, seg2, rbuf2, w2)
    direct_all_gather(2, seg3)
    for h, (a1, a2) in enumerate(plans):
        for d in range(2):
            store(h, pos(a1), d)
    all_gather(3, seg4)
    for copy in sends:
        copy.wait_send()
    for copy in stores:
        copy.wait()


def ray_allreduce(mesh, owned):
    axes = ray_axes(mesh)
    rows, width = owned.shape
    half = width // 2
    w1 = half // axes[0][0]
    w2 = w1 // axes[1][0]
    steps = max(axes[0][0], axes[1][0]) - 1
    return pl.pallas_call(
        functools.partial(allreduce_kernel, axes),
        out_shape=jax.ShapeDtypeStruct((rows, width), jnp.float32),
        in_specs=[pl.BlockSpec(memory_space=pl.ANY)],
        out_specs=pl.BlockSpec(memory_space=pl.ANY),
        scratch_shapes=[
            pltpu.VMEM((rows, width), jnp.float32),
            pltpu.VMEM((rows, width), jnp.float32),
            pltpu.VMEM((2, rows, w1), jnp.float32),
            pltpu.VMEM((2, 2, steps, rows, w1 // 2), jnp.float32),
            pltpu.VMEM((2, 2, steps, rows, w1 // 2), jnp.float32),
            pltpu.VMEM((2, steps, rows, w2), jnp.float32),
            pltpu.SemaphoreType.DMA(()),
            pltpu.SemaphoreType.DMA((2, axes[0][0], 2)),
            pltpu.SemaphoreType.DMA((4, 2, 2, steps)),
            pltpu.SemaphoreType.DMA((4, 2, 2, steps)),
        ],
        compiler_params=pltpu.CompilerParams(
            collective_id=2, has_side_effects=True, vmem_limit_bytes=32 * 1024 * 1024),
    )(owned)


eps_norm = 1e-06


def per_device(mesh, data, sensitivity, block_tiles, block_bundles):
    columns = data.shape[0]
    bundles = block_bundles.reshape(-1)
    requests = lax.all_to_all(block_tiles, "tile", split_axis=1, concat_axis=1, tiled=True).reshape(
        -1
    )
    bundle_onehot = (bundles[:, None] == jnp.arange(BUND_DEV, dtype=jnp.int32)[None, :]).astype(
        jnp.float32
    )
    owner_onehot = (requests[:, None] == jnp.arange(TILE_DEV, dtype=jnp.int32)[None, :]).astype(
        jnp.bfloat16
    )

    def fetch(field_bf):
        owned = field_bf.reshape(columns, TILE_DEV, CB)
        outgoing = jnp.take(owned, requests, axis=1, mode="clip")
        tiles = lax.all_to_all(outgoing, "tile", split_axis=1, concat_axis=1, tiled=True)
        return tiles

    def forward(field_bf):
        tiles = fetch(field_bf)
        partial_value = jnp.einsum(
            "cnk,nrk->ncr", tiles, sensitivity, preferred_element_type=jnp.float32
        )
        summed = jnp.einsum(
            "ncr,nb->cbr", partial_value, bundle_onehot, precision=lax.Precision.HIGHEST
        )
        return summed.reshape(columns, BUND_DEV * RB)

    def adjoint(rays_bf):
        picked = jnp.take(rays_bf.reshape(columns, BUND_DEV, RB), bundles, axis=1, mode="clip")
        terms = jnp.einsum(
            "cnr,nrk->cnk", picked, sensitivity, preferred_element_type=jnp.float32
        ).astype(jnp.bfloat16)
        arrived = lax.all_to_all(terms, "tile", split_axis=1, concat_axis=1, tiled=True)
        owned = jnp.einsum(
            "cnk,nt->ctk", arrived, owner_onehot, preferred_element_type=jnp.float32
        ).reshape(columns, TILE_DEV * CB)
        total = ray_allreduce(mesh, owned)
        return total

    def cell_norm(field):
        local = jnp.sum(field * field, axis=1)
        total = group_sum(mesh, ("tile",), 1, local)
        return jnp.sqrt(total + eps_norm)

    def ray_norm(rays):
        total = group_sum(mesh, ("ray", "tile"), 0, jnp.sum(rays * rays, axis=1))
        return jnp.sqrt(total + eps_norm)

    beta_now = ray_norm(data)
    rays_dir = data / beta_now[:, None]
    model_dir = adjoint(rays_dir.astype(jnp.bfloat16))
    alpha_now = cell_norm(model_dir)
    model_dir = model_dir / alpha_now[:, None]
    search = model_dir
    solution = jnp.zeros_like(model_dir)
    phi_bar = beta_now
    rho_bar = alpha_now
    for step in range(ITERS):
        rounded = model_dir.astype(jnp.bfloat16)
        rays_dir = forward(rounded) - alpha_now[:, None] * rays_dir
        beta_now = ray_norm(rays_dir)
        rays_dir = rays_dir / beta_now[:, None]
        rho_now = jnp.sqrt(rho_bar * rho_bar + beta_now * beta_now)
        cosine = rho_bar / rho_now
        sine_part = beta_now / rho_now
        phi_now = cosine * phi_bar
        phi_bar = sine_part * phi_bar
        solution = solution + (phi_now / rho_now)[:, None] * search
        if step + 1 < ITERS:
            model_dir = adjoint(rays_dir.astype(jnp.bfloat16)) - beta_now[:, None] * model_dir
            alpha_now = cell_norm(model_dir)
            model_dir = model_dir / alpha_now[:, None]
            theta_now = sine_part * alpha_now
            rho_bar = -cosine * alpha_now
            search = model_dir - (theta_now / rho_now)[:, None] * search
    residual = data - forward(solution.astype(jnp.bfloat16))
    return (solution, residual)


def solution(mesh):
    return jax.shard_map(
        functools.partial(per_device, mesh),
        mesh=mesh,
        in_specs=(
            P(None, ("ray", "tile")),
            P(("ray", "tile"), None, None),
            P(("ray", "tile"), None, None),
            P(("ray", "tile"), None, None),
        ),
        out_specs=(P(None, "tile"), P(None, ("ray", "tile"))),
        check_vma=False,
    )
```
